32 devices in a mesh: batch: 2 (over y), row: 4 (over x, core), col: 4 (over z).
Axes of the slice: x: 2, y: 2, z: 4, core: 2. Of those that a mesh axis runs over, the one named last changes fastest.
Arguments:
- patches: bfloat16 [2, 4096, 1280], P('batch', 'col', 'row'), may hold values from -6 to 6
- qkv_weight: bfloat16 [1280, 3, 1280], P('row', None, 'col'), may hold values from -0.15625 to 0.15625
- qv_bias: float32 [2, 1280], P(None, 'col'), may hold values from -0.6 to 0.6
- proj_weight: bfloat16 [1280, 1280], P('col', 'row'), may hold values from -2.5 to 2.5
- proj_bias: float32 [1280], P('row'), may hold values from -1.2 to 1.2
- norm1_gain: float32 [1280], P('row'), may hold values from 0.5 to 1.5
- norm1_shift: float32 [1280], P('row'), may hold values from -1.2 to 1.2
- norm2_gain: float32 [1280], P('row'), may hold values from 0.5 to 1.5
- norm2_shift: float32 [1280], P('row'), may hold values from -1.2 to 1.2
- fc1_weight: bfloat16 [1280, 5120], P('row', 'col'), may hold values from -0.15625 to 0.15625
- fc1_bias: float32 [5120], P('col'), may hold values from -1.2 to 1.2
- fc2_weight: bfloat16 [5120, 1280], P('col', 'row'), may hold values from -0.078125 to 0.078125
- fc2_bias: float32 [1280], P('row'), may hold values from -1.2 to 1.2
- height_table: bfloat16 [127, 80], replicated, may hold values from -0.625 to 0.625
- width_table: bfloat16 [127, 80], replicated, may hold values from -0.625 to 0.625
- out_grad: bfloat16 [2, 4096, 1280], P('batch', 'col', 'row'), may hold values from -6 to 6
Outputs:
- block_out: bfloat16 [2, 4096, 1280], P('batch', 'col', 'row')
- patches_grad: float32 [2, 4096, 1280], P('batch', 'col', 'row')
- qkv_weight_grad: float32 [1280, 3, 1280], P('row', None, 'col')
- qv_bias_grad: float32 [2, 1280], P(None, 'col')
- proj_weight_grad: float32 [1280, 1280], P('col', 'row')
- proj_bias_grad: float32 [1280], P('row')
- norm1_gain_grad: float32 [1280], P('row')
- norm1_shift_grad: float32 [1280], P('row')
- norm2_gain_grad: float32 [1280], P('row')
- norm2_shift_grad: float32 [1280], P('row')
- fc1_weight_grad: float32 [1280, 5120], P('row', 'col')
- fc1_bias_grad: float32 [5120], P('col')
- fc2_weight_grad: float32 [5120, 1280], P('col', 'row')
- fc2_bias_grad: float32 [1280], P('row')
- height_table_grad: float32 [127, 80], replicated
- width_table_grad: float32 [127, 80], replicated
The draws below stay inside these ranges and needn't reach their ends.
All inputs are finite; a program needn't handle non-finite values.
Results may differ from the reference program's by a relative error of at most 0.012.
Values may be sent and summed in bfloat16 or wider, within the bound.
A program may use at most 256 MiB of HBM per device.

```python
import jax
import jax.numpy as jnp
from jax import lax

D = 1280
HEADS = 16
HEAD_DIM = 80
FF = 5120
GRID = 64
TOKENS = 4096
IMAGES = 2


def block_levels(own_key, shape, cuts, low, largest):
    gain, own = 1.0, jax.random.fold_in(own_key, 6)
    for dim, shards_of in cuts:
        heights = jnp.exp(jax.random.uniform(jax.random.fold_in(own, dim), (shards_of,), jnp.float32, low / len(cuts), largest / len(cuts)))
        gain = gain * jnp.repeat(heights, shape[dim] // shards_of).reshape([-1 if axis == dim else 1 for axis in range(len(shape))])
    return gain


def bell_draw(stream_key, extent, width, reach, cuts=(), held_as=jnp.bfloat16):
    values = width * jax.random.normal(stream_key, extent, jnp.float32)
    if cuts:
        values = values * block_levels(stream_key, extent, cuts, -0.22, 0.18)
    return jnp.clip(values, -reach, reach).astype(held_as)


def setup_inputs(seed: int = 0) -> dict:
    key_of = jax.random.split(jax.random.key(seed), 17)
    patches = bell_draw(key_of[0], (IMAGES, TOKENS, D), 1.0, 6.0, ((0, 2), (1, 4), (2, 4)))
    qkv_weight = bell_draw(key_of[1], (D, 3, D), D ** -0.5, 0.15625, ((0, 4), (2, 4)))
    qv_bias = bell_draw(key_of[2], (2, D), 0.1, 0.6, ((1, 4),), jnp.float32)
    proj_weight = bell_draw(key_of[3], (D, D), (max(D // 256, 1)) ** -0.5, 2.5, ((0, 4), (1, 4)))
    proj_bias = bell_draw(key_of[4], (D,), 0.2, 1.2, ((0, 4),), jnp.float32)
    norm1_gain = jnp.clip(1.0 + 0.1 * jax.random.normal(key_of[5], (D,), jnp.float32), 0.5, 1.5)
    norm1_shift = bell_draw(key_of[6], (D,), 0.2, 1.2, ((0, 4),), jnp.float32)
    norm2_gain = jnp.clip(1.0 + 0.1 * jax.random.normal(key_of[7], (D,), jnp.float32), 0.5, 1.5)
    norm2_shift = bell_draw(key_of[8], (D,), 0.2, 1.2, ((0, 4),), jnp.float32)
    fc1_weight = bell_draw(key_of[9], (D, FF), D ** -0.5, 0.15625, ((0, 4), (1, 4)))
    fc1_bias = bell_draw(key_of[10], (FF,), 0.2, 1.2, ((0, 4),), jnp.float32)
    fc2_weight = bell_draw(key_of[11], (FF, D), FF ** -0.5, 0.078125, ((0, 4), (1, 4)))
    fc2_bias = bell_draw(key_of[12], (D,), 0.2, 1.2, ((0, 4),), jnp.float32)
    height_table = bell_draw(key_of[13], (2 * GRID - 1, HEAD_DIM), HEAD_DIM ** -0.5, 0.625)
    width_table = bell_draw(key_of[14], (2 * GRID - 1, HEAD_DIM), HEAD_DIM ** -0.5, 0.625)
    out_grad = bell_draw(key_of[15], (IMAGES, TOKENS, D), 1.0, 6.0, ((0, 2), (1, 4), (2, 4)))
    return {"patches": patches, "qkv_weight": qkv_weight, "qv_bias": qv_bias, "proj_weight": proj_weight, "proj_bias": proj_bias, "norm1_gain": norm1_gain, "norm1_shift": norm1_shift, "norm2_gain": norm2_gain, "norm2_shift": norm2_shift, "fc1_weight": fc1_weight, "fc1_bias": fc1_bias, "fc2_weight": fc2_weight, "fc2_bias": fc2_bias, "height_table": height_table, "width_table": width_table, "out_grad": out_grad}


EPSILON = 1e-06
HIGHEST = lax.Precision.HIGHEST

@jax.custom_vjp
def low(v):
    return lax.optimization_barrier(v.astype(jnp.bfloat16)).astype(jnp.float32)

@jax.custom_vjp
def low_back(v):
    return v

def low_keep(v):
    return (low(v), None)

def low_pass(kept, grad):
    return (grad,)

def back_keep(v):
    return (v, None)

def back_low(kept, grad):
    return (low(grad),)
low.defvjp(low_keep, low_pass)
low_back.defvjp(back_keep, back_low)

def normalize(values, norm_gain, norm_shift):
    center = lax.optimization_barrier(jnp.mean(values, -1, keepdims=True))
    spread = lax.optimization_barrier(jnp.mean(values * values, -1, keepdims=True)) - center * center
    return (values - center) * lax.rsqrt(spread + EPSILON) * norm_gain + norm_shift

def forward(residual, qkv_weight, qv_bias, proj_weight, proj_bias, norm1_gain, norm1_shift, norm2_gain, norm2_shift, fc1_weight, fc1_bias, fc2_weight, fc2_bias, height_table, width_table):
    image_tokens = GRID * GRID
    normed1 = low(normalize(residual, norm1_gain, norm1_shift))
    projected = jnp.einsum('lf,fkh->lkh', normed1, qkv_weight, precision=HIGHEST)
    queries = low(low_back(projected[:, 0] + qv_bias[0]))
    key_rows = low(low_back(projected[:, 1]))
    value_rows = low(low_back(projected[:, 2] + qv_bias[1]))
    offsets = (jnp.arange(GRID)[:, None] - jnp.arange(GRID)[None, :] + GRID - 1).astype(jnp.int32)
    rows_table = height_table[offsets]
    cols_table = width_table[offsets]

    def split_heads(values):
        return values.reshape(image_tokens, HEADS, HEAD_DIM).transpose(1, 0, 2)

    def one_head(operands):
        query_one, key_one, value_one = operands
        query_grid = query_one.reshape(GRID, GRID, HEAD_DIM)
        rel_rows = jnp.einsum('hwc,hkc->hwk', query_grid, rows_table, precision=HIGHEST)
        rel_cols = jnp.einsum('hwc,wkc->hwk', query_grid, cols_table, precision=HIGHEST)
        position = (rel_rows[:, :, :, None] + rel_cols[:, :, None, :]).reshape(image_tokens, image_tokens)
        scores = low_back(jnp.dot(query_one * HEAD_DIM ** (-0.5), key_one.T, precision=HIGHEST) + position)
        weights = jax.nn.softmax(scores, -1)
        return jnp.dot(low(weights), value_one, precision=HIGHEST)
    attended = lax.map(jax.checkpoint(one_head), (split_heads(queries), split_heads(key_rows), split_heads(value_rows)))
    merged = low(low_back(attended.transpose(1, 0, 2).reshape(image_tokens, D)))
    middle = residual + low_back(jnp.dot(merged, proj_weight, precision=HIGHEST) + proj_bias)
    normed2 = low(normalize(middle, norm2_gain, norm2_shift))
    preact = low_back(jnp.dot(normed2, fc1_weight, precision=HIGHEST) + fc1_bias)
    activated = low(jax.nn.gelu(preact, approximate=False))
    return middle + (jnp.dot(activated, fc2_weight, precision=HIGHEST) + fc2_bias)

def reference(patches, qkv_weight, qv_bias, proj_weight, proj_bias, norm1_gain, norm1_shift, norm2_gain, norm2_shift, fc1_weight, fc1_bias, fc2_weight, fc2_bias, height_table, width_table, out_grad):
    params = tuple((item.astype(jnp.float32) for item in (qkv_weight, qv_bias, proj_weight, proj_bias, norm1_gain, norm1_shift, norm2_gain, norm2_shift, fc1_weight, fc1_bias, fc2_weight, fc2_bias, height_table, width_table)))
    start_sums = tuple((jnp.zeros(item.shape, jnp.float32) for item in params))

    def one_image(running, operands):
        image_in, image_cot = operands
        result, backward = jax.vjp(forward, image_in.astype(jnp.float32), *params)
        grads = backward(image_cot.astype(jnp.float32))
        running = tuple((left + right for left, right in zip(running, grads[1:])))
        return (running, (result.astype(jnp.bfloat16), grads[0]))
    totals, (results, input_grads) = lax.scan(one_image, start_sums, (patches, out_grad))
    return (results, input_grads, totals[0], totals[1], totals[2], totals[3], totals[4], totals[5], totals[6], totals[7], totals[8], totals[9], totals[10], totals[11], totals[12], totals[13])
```

```python
import math
from functools import partial

import jax
import jax.numpy as jnp
from jax import lax
from jax.experimental import pallas as pl
from jax.experimental.pallas import tpu as pltpu
from jax.sharding import PartitionSpec as P

D = 1280
HEAD_DIM = 80
GRID = 64
EPSILON = 1e-06

LINES = 4
QUERIES = LINES * GRID
KEYS = 512
LOG2E = math.log2(math.e)
SCALE = HEAD_DIM**-0.5
BF16 = jnp.bfloat16
F32 = jnp.float32


def mm(left, right):
    return jnp.dot(left, right, preferred_element_type=F32)


def mm_nt(left, right):
    return lax.dot_general(left, right, (((1,), (1,)), ((), ())), preferred_element_type=F32)


def split(values, parts):
    terms = []
    for _ in range(parts):
        term = values.astype(BF16)
        terms.append(term)
        values = values - term.astype(F32)
    return terms


def skew(values, shift):
    n = values.shape[1]
    for bit, rows in ((32, 96), (16, 80), (8, 72)):
        take = jnp.broadcast_to(shift, (rows, n)) & bit
        values = jnp.where(take != 0, values[bit : bit + rows], values[:rows])
    for bit in (4, 2, 1):
        take = jnp.broadcast_to(shift, values.shape) & bit
        values = jnp.where(take != 0, pltpu.roll(values, values.shape[0] - bit, 0), values)
    return values[:GRID]


def unskew(values, shift):
    n = values.shape[1]
    values = jnp.concatenate([values, jnp.zeros((8, n), F32)], 0)
    for bit in (1, 2, 4):
        take = jnp.broadcast_to(shift, values.shape) & bit
        values = jnp.where(take != 0, pltpu.roll(values, bit, 0), values)
    for bit in (8, 16, 32):
        zeros = jnp.zeros((bit, n), F32)
        take = jnp.broadcast_to(shift, (values.shape[0] + bit, n)) & bit
        values = jnp.where(
            take != 0,
            jnp.concatenate([zeros, values], 0),
            jnp.concatenate([values, zeros], 0),
        )
    return values


def token_shifts(step):
    lane = lax.broadcasted_iota(jnp.int32, (1, QUERIES), 1)
    return (GRID - 1) - (step * LINES + lane // GRID), (GRID - 1) - lane % GRID


def fill_keys(k_ref, kaug):
    count, _, width = k_ref.shape
    token = lax.broadcasted_iota(jnp.int32, (width, 2 * GRID), 0)
    lane = lax.broadcasted_iota(jnp.int32, (width, 2 * GRID), 1)
    pad_row = lax.broadcasted_iota(jnp.int32, (128 - HEAD_DIM, width), 0)
    pad = jnp.where(pad_row < 3, 1.0, 0.0)
    for part in range(count):
        at = token + part * width
        place = jnp.where(lane < GRID, at // GRID, at % GRID + GRID)
        hot = jnp.where(place == lane, 1.0, 0.0)
        kaug[part * width : (part + 1) * width, 0:128] = hot.astype(BF16)
        key = jnp.concatenate([k_ref[part].astype(F32), pad], 0)
        kaug[part * width : (part + 1) * width, 128:256] = key.T.astype(BF16)


def query_columns(q, tab, step, tail):
    shift_rows, shift_cols = token_shifts(step)
    both = mm(tab, q)
    rel_rows = skew(both[: 2 * GRID], shift_rows)
    rel_cols = skew(both[2 * GRID :], shift_cols)
    rel = jnp.concatenate([rel_rows, rel_cols], 0) * (1.0 / SCALE)
    return jnp.concatenate([rel.astype(BF16), q, tail], 0)


def attend_kernel(q_ref, k_ref, v_ref, tab_ref, merged_ref, exact_ref, stat_ref, kaug):
    step = pl.program_id(0)

    @pl.when(step == 0)
    def _():
        fill_keys(k_ref, kaug)

    width = k_ref.shape[2]
    q = q_ref[0]
    columns = query_columns(q, tab_ref[...], step, jnp.zeros((128 - HEAD_DIM, QUERIES), BF16))
    top = total = acc = None
    for chunk in range(kaug.shape[0] // KEYS):
        start = chunk * KEYS
        scores = mm(kaug[start : start + KEYS, :], columns)
        chunk_top = jnp.max(scores, 0, keepdims=True)
        new_top = chunk_top if top is None else jnp.maximum(top, chunk_top)
        weights = jnp.exp2((scores - new_top) * (SCALE * LOG2E))
        chunk_total = jnp.sum(weights, 0, keepdims=True)
        v = v_ref[start // width, :, start % width : start % width + KEYS]
        result = mm(v, weights.astype(BF16))
        if top is None:
            total, acc = chunk_total, result
        else:
            keep = jnp.exp2((top - new_top) * (SCALE * LOG2E))
            total, acc = total * keep + chunk_total, acc * keep + result
        top = new_top
    exact = acc * (1.0 / total)
    exact_ref[0] = exact
    merged_ref[0] = exact.astype(BF16)
    stat_ref[0] = jnp.broadcast_to(top + jnp.log2(total) * (1.0 / (SCALE * LOG2E)), (8, QUERIES))


def attend_back_kernel(
    q_ref, k_ref, v_ref, tab_ref, tab_t_ref, grad_ref, exact_ref, stat_ref,
    out_ref, tab_grad_ref, kaug, kaug_t, vaug, key_sum, value_sum,
):
    step = pl.program_id(0)
    count, _, width = k_ref.shape
    tail_row = lax.broadcasted_iota(jnp.int32, (128 - HEAD_DIM, width), 0)

    @pl.when(step == 0)
    def _():
        fill_keys(k_ref, kaug)
        pad = jnp.where(tail_row < 3, 1.0, 0.0)
        for part in range(count):
            rows = slice(part * width, (part + 1) * width)
            value = jnp.concatenate([v_ref[part].astype(F32), pad], 0)
            vaug[rows, :] = value.T.astype(BF16)
            kaug_t[0:128, rows] = kaug[rows, 0:128].astype(F32).T.astype(BF16)
            kaug_t[128:208, rows] = k_ref[part]
            kaug_t[208:256, rows] = jnp.zeros((48, width), BF16)
        key_sum[...] = jnp.zeros_like(key_sum)
        value_sum[...] = jnp.zeros_like(value_sum)
        tab_grad_ref[...] = jnp.zeros_like(tab_grad_ref)

    q = q_ref[0]
    grad = grad_ref[0]
    tail_row = lax.broadcasted_iota(jnp.int32, (128 - HEAD_DIM, QUERIES), 0)

    def tail(row):
        out = jnp.zeros((128 - HEAD_DIM, QUERIES), F32)
        for place, term in enumerate(split(row, 3)):
            out = jnp.where(tail_row == place, term.astype(F32), out)
        return out.astype(BF16)

    inner = jnp.sum(grad.astype(F32) * exact_ref[0], 0, keepdims=True)
    columns = query_columns(q, tab_ref[...], step, tail(-stat_ref[0, 0:1]))
    grad_columns = jnp.concatenate([grad, tail(-inner)], 0)
    zero_tail = jnp.zeros((128 - HEAD_DIM, QUERIES), F32)
    grad_rows = jnp.concatenate([grad.astype(F32), zero_tail], 0).T.astype(BF16)
    q_rows = jnp.concatenate([q.astype(F32), zero_tail], 0).T.astype(BF16)
    spread = None
    for chunk in range(kaug.shape[0] // KEYS):
        keys = slice(chunk * KEYS, (chunk + 1) * KEYS)
        weights = jnp.exp2(mm(kaug[keys, :], columns) * (SCALE * LOG2E))
        score_grad = (weights * mm(vaug[keys, :], grad_columns)).astype(BF16)
        value_sum[keys, :] += mm(weights.astype(BF16), grad_rows)
        key_sum[keys, :] += mm(score_grad, q_rows)
        result = mm(kaug_t[:, keys], score_grad)
        spread = result if spread is None else spread + result

    shift_rows, shift_cols = token_shifts(step)
    lifted = jnp.concatenate(
        [unskew(spread[:GRID], shift_rows), unskew(spread[GRID : 2 * GRID], shift_cols)], 0
    )
    high, low = split(lifted, 2)
    query_grad = spread[128 : 128 + HEAD_DIM] * SCALE
    query_grad = query_grad + (mm(tab_t_ref[...], high) + mm(tab_t_ref[...], low))
    tab_grad_ref[...] += mm_nt(high, q) + mm_nt(low, q)
    per_part = width // QUERIES
    lanes = pl.ds(pl.multiple_of((step % per_part) * QUERIES, QUERIES), QUERIES)
    out_ref[step // per_part, 0:HEAD_DIM, lanes] = query_grad.astype(BF16)

    @pl.when(step == pl.num_programs(0) - 1)
    def _():
        for part in range(count):
            rows = slice(part * width, (part + 1) * width)
            key_grad = (key_sum[rows, :] * SCALE).T[:HEAD_DIM]
            out_ref[part, HEAD_DIM : 2 * HEAD_DIM, :] = key_grad.astype(BF16)
            value_grad = value_sum[rows, :].T[:HEAD_DIM]
            out_ref[part, 2 * HEAD_DIM : 3 * HEAD_DIM, :] = value_grad.astype(BF16)


def part_spec(rows, width, row_block):
    per_part = width // QUERIES
    return pl.BlockSpec((1, rows, QUERIES), lambda i: (i // per_part, row_block, i % per_part))


def whole_spec(shape, at=None):
    place = at or (0,) * len(shape)
    return pl.BlockSpec(shape, lambda i: place, pipeline_mode=pl.Buffered(1))


def attention(qkv, table):
    count, _, width = qkv.shape
    tokens = count * width
    heads = (count, HEAD_DIM, width)
    return pl.pallas_call(
        attend_kernel,
        grid=(tokens // QUERIES,),
        in_specs=[
            part_spec(HEAD_DIM, width, 0),
            whole_spec(heads, (0, 1, 0)),
            whole_spec(heads, (0, 2, 0)),
            whole_spec(table.shape),
        ],
        out_specs=[part_spec(HEAD_DIM, width, 0), part_spec(HEAD_DIM, width, 0), part_spec(8, width, 0)],
        out_shape=[
            jax.ShapeDtypeStruct(heads, BF16),
            jax.ShapeDtypeStruct(heads, F32),
            jax.ShapeDtypeStruct((count, 8, width), F32),
        ],
        scratch_shapes=[pltpu.VMEM((tokens, 256), BF16)],
        compiler_params=pltpu.CompilerParams(vmem_limit_bytes=48 << 20),
        cost_estimate=pl.CostEstimate(
            flops=2 * tokens * tokens * 512,
            bytes_accessed=6 * tokens * HEAD_DIM * 2,
            transcendentals=tokens * tokens,
        ),
        name="attend",
    )(qkv, qkv, qkv, table)


def attention_back(qkv, table, grad, exact, stat):
    count, _, width = qkv.shape
    tokens = count * width
    heads = (count, HEAD_DIM, width)
    return pl.pallas_call(
        attend_back_kernel,
        grid=(tokens // QUERIES,),
        in_specs=[
            part_spec(HEAD_DIM, width, 0),
            whole_spec(heads, (0, 1, 0)),
            whole_spec(heads, (0, 2, 0)),
            whole_spec(table.shape),
            whole_spec(table.shape[::-1]),
            part_spec(HEAD_DIM, width, 0),
            part_spec(HEAD_DIM, width, 0),
            part_spec(8, width, 0),
        ],
        out_specs=[whole_spec((count, 3 * HEAD_DIM, width)), whole_spec(table.shape)],
        out_shape=[
            jax.ShapeDtypeStruct((count, 3 * HEAD_DIM, width), BF16),
            jax.ShapeDtypeStruct(table.shape, F32),
        ],
        scratch_shapes=[
            pltpu.VMEM((tokens, 256), BF16),
            pltpu.VMEM((256, tokens), BF16),
            pltpu.VMEM((tokens, 128), BF16),
            pltpu.VMEM((tokens, 128), F32),
            pltpu.VMEM((tokens, 128), F32),
        ],
        compiler_params=pltpu.CompilerParams(vmem_limit_bytes=48 << 20),
        cost_estimate=pl.CostEstimate(
            flops=2 * tokens * tokens * 1280,
            bytes_accessed=12 * tokens * HEAD_DIM * 2,
            transcendentals=tokens * tokens,
        ),
        name="attend_back",
    )(qkv, qkv, qkv, table, table.T, grad, exact, stat)


def moments(values):
    center = jnp.mean(values, -1, keepdims=True)
    spread = jnp.mean(values * values, -1, keepdims=True)
    return center, lax.rsqrt(spread - center * center + EPSILON)


def shards(
    patches,
    qkv_weight,
    qv_bias,
    proj_weight,
    proj_bias,
    norm1_gain,
    norm1_shift,
    norm2_gain,
    norm2_shift,
    fc1_weight,
    fc1_bias,
    fc2_weight,
    fc2_bias,
    height_table,
    width_table,
    out_grad,
):
    rows, cols = lax.axis_size("row"), lax.axis_size("col")
    row, col = lax.axis_index("row"), lax.axis_index("col")
    width = patches.shape[1]
    part = patches.shape[2]
    model = part * rows
    own = width // rows
    hidden = fc1_bias.shape[0] // rows
    head = HEAD_DIM

    def over_row(values):
        return lax.all_gather(values, "row", axis=1, tiled=True)

    def spread_rows(values):
        moved = lax.all_to_all(values, "row", 0, 0, tiled=True)
        return moved.transpose(1, 0, 2).reshape(values.shape[1], model)

    def whole_weight(values):
        return lax.all_gather(spread_rows(values), "col", axis=0, tiled=False)

    residual = over_row(patches[0])
    cotangent = over_row(out_grad[0])
    vectors = lax.all_gather(
        jnp.stack([norm1_gain, norm1_shift, norm2_gain, norm2_shift, proj_bias, fc2_bias]),
        "row", axis=1, tiled=True,
    )
    gain1, shift1, gain2, shift2, bias_proj, bias_fc2 = [vectors[i] for i in range(6)]
    by_col = lax.all_gather(
        jnp.concatenate([qv_bias.reshape(-1), fc1_bias]), "col", axis=0, tiled=False
    )
    bias_qv = by_col[:, : 2 * rows * head].reshape(cols, 2, rows, head)
    bias_qv = lax.dynamic_index_in_dim(bias_qv, row, 2, keepdims=False)
    bias_fc1 = by_col[:, 2 * rows * head :].reshape(cols, rows, hidden)
    bias_fc1 = lax.dynamic_index_in_dim(bias_fc1, row, 1, keepdims=False)
    bias_fc1 = bias_fc1.reshape(cols * hidden)

    local_qkv = qkv_weight.reshape(part, 3, rows, head).transpose(2, 1, 3, 0)
    weight_qkv = whole_weight(local_qkv.reshape(rows, 3 * head, part))
    weight_proj = whole_weight(proj_weight.reshape(rows, head, part)).reshape(cols * head, model)
    weight_fc1 = whole_weight(fc1_weight.T.reshape(rows, hidden, part)).reshape(cols * hidden, model)
    weight_fc2 = whole_weight(fc2_weight.reshape(rows, hidden, part)).reshape(cols * hidden, model)

    zero_row = jnp.zeros((1, head), BF16)
    table = jnp.concatenate([height_table[::-1], zero_row, width_table[::-1], zero_row], 0)

    first = residual.astype(F32)
    center1, inv1 = moments(first)
    scaled1 = (first - center1) * inv1
    normed1 = (scaled1 * gain1 + shift1).astype(BF16)
    bias = jnp.stack([bias_qv[:, 0], jnp.zeros_like(bias_qv[:, 0]), bias_qv[:, 1]], 1)
    qkv = mm_nt(weight_qkv.reshape(cols * 3 * head, model), normed1)
    qkv = (qkv.reshape(cols, 3 * head, width) + bias.reshape(cols, 3 * head, 1)).astype(BF16)
    qkv = lax.all_to_all(qkv, "col", 0, 0, tiled=True)
    merged, exact, stat = attention(qkv, table)
    merged = lax.all_to_all(merged, "col", 0, 0, tiled=True).reshape(cols * head, width)

    def contract_rows(left, right):
        return lax.dot_general(left, right, (((0,), (0,)), ((), ())), preferred_element_type=F32)

    def tokens_of_row(values):
        return lax.dynamic_slice_in_dim(values, row * own, own, 0)

    def sum_tokens(values):
        return lax.psum_scatter(values.astype(BF16), "row", scatter_dimension=0, tiled=True)

    projected = sum_tokens(contract_rows(merged, weight_proj)).astype(F32)
    middle = tokens_of_row(residual).astype(F32) + (projected + bias_proj)
    center2, inv2 = moments(middle)
    scaled2 = (middle - center2) * inv2
    normed2 = (scaled2 * gain2 + shift2).astype(BF16)
    normed2 = lax.all_gather(normed2, "row", axis=0, tiled=True)
    preact = mm_nt(normed2, weight_fc1) + bias_fc1
    activated, gelu_back = jax.vjp(partial(jax.nn.gelu, approximate=False), preact)
    activated = activated.astype(BF16)
    lowered = sum_tokens(mm(activated, weight_fc2)).astype(F32)
    final = (middle + (lowered + bias_fc2)).astype(BF16)
    final = final.reshape(own, rows, part).transpose(1, 0, 2)
    final = lax.all_to_all(final, "row", 0, 0, tiled=True).reshape(width, part)

    act_grad = mm_nt(cotangent, weight_fc2)
    preact_grad = gelu_back(act_grad)[0].astype(BF16)
    normed2_grad = sum_tokens(mm(preact_grad, weight_fc1)).astype(F32)
    scaled_grad = normed2_grad * gain2
    middle_grad = tokens_of_row(cotangent).astype(F32) + inv2 * (
        scaled_grad
        - jnp.mean(scaled_grad, -1, keepdims=True)
        - scaled2 * jnp.mean(scaled_grad * scaled2, -1, keepdims=True)
    )
    branch_grad = lax.all_gather(middle_grad.astype(BF16), "row", axis=0, tiled=True)
    middle_own = middle_grad.reshape(own, rows, part).transpose(1, 0, 2)
    middle_own = lax.all_to_all(middle_own, "row", 0, 0, tiled=True).reshape(width, part)

    merged_grad = mm_nt(weight_proj, branch_grad).astype(BF16).reshape(cols, head, width)
    merged_grad = lax.all_to_all(merged_grad, "col", 0, 0, tiled=True)
    qkv_grad, table_grad = attention_back(qkv, table, merged_grad, exact, stat)
    bias_grad = jnp.sum(qkv_grad, (0, 2), dtype=F32).reshape(3, head)
    qkv_grad = lax.all_to_all(qkv_grad, "col", 0, 0, tiled=True).reshape(cols * 3 * head, width)

    normed1_grad = contract_rows(qkv_grad, weight_qkv.reshape(cols * 3 * head, model))
    gain1_part = jnp.sum(normed1_grad * scaled1, 0)
    shift1_part = jnp.sum(normed1_grad, 0)
    scaled_grad = normed1_grad * gain1
    means = lax.psum(
        jnp.stack([jnp.sum(scaled_grad, -1), jnp.sum(scaled_grad * scaled1, -1)]), "row"
    ) / model
    by_row = normed1_grad.astype(BF16).reshape(width, rows, part).transpose(1, 0, 2)
    normed1_own = lax.psum_scatter(by_row, "row", scatter_dimension=0, tiled=False).astype(F32)
    scaled1_own = (patches[0].astype(F32) - center1) * inv1
    input_grad = middle_own + inv1 * (
        normed1_own * norm1_gain - means[0][:, None] - scaled1_own * means[1][:, None]
    )

    def weight_back(values):
        values = lax.psum_scatter(values.astype(BF16), "col", scatter_dimension=0, tiled=False)
        values = lax.psum(values, "batch")
        values = values.reshape(-1, rows, part).transpose(1, 0, 2)
        return lax.all_to_all(values, "row", 0, 0, tiled=True).astype(F32)

    fc2_grad = contract_rows(activated, cotangent).reshape(cols, hidden, model)
    fc2_grad = weight_back(fc2_grad).reshape(rows * hidden, part)
    fc1_grad = contract_rows(preact_grad, normed2).reshape(cols, hidden, model)
    fc1_grad = weight_back(fc1_grad).reshape(rows * hidden, part).T
    proj_grad = mm(merged, branch_grad).reshape(cols, head, model)
    proj_grad = weight_back(proj_grad).reshape(rows * head, part)
    qkv_weight_grad = mm(qkv_grad, normed1).reshape(cols, 3 * head, model)
    qkv_weight_grad = weight_back(qkv_weight_grad).reshape(rows, 3, head, part)
    qkv_weight_grad = qkv_weight_grad.transpose(3, 1, 0, 2).reshape(part, 3, rows * head)

    everywhere = ("batch", "row", "col")
    fc1_bias_part = jnp.sum(preact_grad, 0, dtype=F32).reshape(cols, 1, hidden)
    fc1_bias_part = lax.dynamic_update_slice(
        jnp.zeros((cols, rows, hidden), F32), fc1_bias_part, (0, row, 0)
    )
    fc2_bias_part = jnp.sum(out_grad[0], 0, dtype=F32)
    fc2_bias_grad = lax.psum(fc2_bias_part, ("batch", "col"))
    gain2_grad, shift2_grad, proj_bias_grad, fc1_bias_grad = lax.psum(
        (
            jnp.sum(normed2_grad * scaled2, 0),
            jnp.sum(normed2_grad, 0),
            jnp.sum(tokens_of_row(branch_grad), 0, dtype=F32),
            fc1_bias_part,
        ),
        everywhere,
    )
    bias_part = lax.dynamic_update_slice(
        jnp.zeros((cols, 2, rows, head), F32),
        jnp.stack([bias_grad[0], bias_grad[2]])[None, :, None],
        (col, 0, row, 0),
    )
    table_grad, bias_total = lax.psum((table_grad, bias_part), everywhere)
    gain1_grad, shift1_grad = lax.psum((gain1_part, shift1_part), everywhere)

    def features_of_row(values):
        return lax.dynamic_slice_in_dim(values, row * part, part, 0)

    side = 2 * GRID - 1
    return (
        final[None],
        input_grad[None],
        qkv_weight_grad,
        lax.dynamic_index_in_dim(bias_total, col, 0, keepdims=False).reshape(2, rows * head),
        proj_grad,
        features_of_row(proj_bias_grad),
        features_of_row(gain1_grad),
        features_of_row(shift1_grad),
        features_of_row(gain2_grad),
        features_of_row(shift2_grad),
        fc1_grad,
        lax.dynamic_index_in_dim(fc1_bias_grad, col, 0, keepdims=False).reshape(rows * hidden),
        fc2_grad,
        fc2_bias_grad,
        table_grad[:side][::-1],
        table_grad[2 * GRID : 2 * GRID + side][::-1],
    )


def solution(mesh):
    in_specs = (
        P("batch", "col", "row"),
        P("row", None, "col"),
        P(None, "col"),
        P("col", "row"),
        P("row"),
        P("row"),
        P("row"),
        P("row"),
        P("row"),
        P("row", "col"),
        P("col"),
        P("col", "row"),
        P("row"),
        P(),
        P(),
        P("batch", "col", "row"),
    )
    out_specs = (
        P("batch", "col", "row"),
        P("batch", "col", "row"),
        P("row", None, "col"),
        P(None, "col"),
        P("col", "row"),
        P("row"),
        P("row"),
        P("row"),
        P("row"),
        P("row"),
        P("row", "col"),
        P("col"),
        P("col", "row"),
        P("row"),
        P(),
        P(),
    )
    return jax.shard_map(shards, mesh=mesh, in_specs=in_specs, out_specs=out_specs, check_vma=False)
```

```python
import math
from functools import partial

import jax
import jax.numpy as jnp
from jax import lax
from jax.experimental import pallas as pl
from jax.experimental.pallas import tpu as pltpu
from jax.sharding import PartitionSpec as P

D = 1280
HEAD_DIM = 80
GRID = 64
EPSILON = 1e-06

LINES = 4
QUERIES = LINES * GRID
KEYS = 512
LOG2E = math.log2(math.e)
SCALE = HEAD_DIM**-0.5
BF16 = jnp.bfloat16
F32 = jnp.float32
MESH = pl.DeviceIdType.MESH


def mm(left, right):
    return jnp.dot(left, right, preferred_element_type=F32)


def mm_nt(left, right):
    return lax.dot_general(left, right, (((1,), (1,)), ((), ())), preferred_element_type=F32)


def split(values, parts):
    terms = []
    for _ in range(parts):
        term = values.astype(BF16)
        terms.append(term)
        values = values - term.astype(F32)
    return terms


def skew(values, shift):
    n = values.shape[1]
    for bit, rows in ((32, 96), (16, 80), (8, 72)):
        take = jnp.broadcast_to(shift, (rows, n)) & bit
        values = jnp.where(take != 0, values[bit : bit + rows], values[:rows])
    for bit in (4, 2, 1):
        take = jnp.broadcast_to(shift, values.shape) & bit
        values = jnp.where(take != 0, pltpu.roll(values, values.shape[0] - bit, 0), values)
    return values[:GRID]


def unskew(values, shift):
    n = values.shape[1]
    values = jnp.concatenate([values, jnp.zeros((8, n), F32)], 0)
    for bit in (1, 2, 4):
        take = jnp.broadcast_to(shift, values.shape) & bit
        values = jnp.where(take != 0, pltpu.roll(values, bit, 0), values)
    for bit in (8, 16, 32):
        zeros = jnp.zeros((bit, n), F32)
        take = jnp.broadcast_to(shift, (values.shape[0] + bit, n)) & bit
        values = jnp.where(
            take != 0,
            jnp.concatenate([zeros, values], 0),
            jnp.concatenate([values, zeros], 0),
        )
    return values


def token_shifts(step):
    lane = lax.broadcasted_iota(jnp.int32, (1, QUERIES), 1)
    return (GRID - 1) - (step * LINES + lane // GRID), (GRID - 1) - lane % GRID


def fill_keys(k_ref, kaug):
    count, _, width = k_ref.shape
    token = lax.broadcasted_iota(jnp.int32, (width, 2 * GRID), 0)
    lane = lax.broadcasted_iota(jnp.int32, (width, 2 * GRID), 1)
    pad_row = lax.broadcasted_iota(jnp.int32, (128 - HEAD_DIM, width), 0)
    pad = jnp.where(pad_row < 3, 1.0, 0.0)
    for part in range(count):
        at = token + part * width
        place = jnp.where(lane < GRID, at // GRID, at % GRID + GRID)
        hot = jnp.where(place == lane, 1.0, 0.0)
        kaug[part * width : (part + 1) * width, 0:128] = hot.astype(BF16)
        key = jnp.concatenate([k_ref[part].astype(F32), pad], 0)
        kaug[part * width : (part + 1) * width, 128:256] = key.T.astype(BF16)


def query_columns(q, tab, step, tail):
    shift_rows, shift_cols = token_shifts(step)
    both = mm(tab, q)
    rel_rows = skew(both[: 2 * GRID], shift_rows)
    rel_cols = skew(both[2 * GRID :], shift_cols)
    rel = jnp.concatenate([rel_rows, rel_cols], 0) * (1.0 / SCALE)
    return jnp.concatenate([rel.astype(BF16), q, tail], 0)


def attend_kernel(q_ref, k_ref, v_ref, tab_ref, merged_ref, exact_ref, stat_ref, kaug):
    step = pl.program_id(0)

    @pl.when(step == 0)
    def _():
        fill_keys(k_ref, kaug)

    width = k_ref.shape[2]
    q = q_ref[0]
    columns = query_columns(q, tab_ref[...], step, jnp.zeros((128 - HEAD_DIM, QUERIES), BF16))
    top = total = acc = None
    for chunk in range(kaug.shape[0] // KEYS):
        start = chunk * KEYS
        scores = mm(kaug[start : start + KEYS, :], columns)
        chunk_top = jnp.max(scores, 0, keepdims=True)
        new_top = chunk_top if top is None else jnp.maximum(top, chunk_top)
        weights = jnp.exp2((scores - new_top) * (SCALE * LOG2E))
        chunk_total = jnp.sum(weights, 0, keepdims=True)
        v = v_ref[start // width, :, start % width : start % width + KEYS]
        result = mm(v, weights.astype(BF16))
        if top is None:
            total, acc = chunk_total, result
        else:
            keep = jnp.exp2((top - new_top) * (SCALE * LOG2E))
            total, acc = total * keep + chunk_total, acc * keep + result
        top = new_top
    exact = acc * (1.0 / total)
    exact_ref[0] = exact
    merged_ref[0] = exact.astype(BF16)
    stat_ref[0] = jnp.broadcast_to(top + jnp.log2(total) * (1.0 / (SCALE * LOG2E)), (8, QUERIES))


def attend_back_kernel(
    q_ref, k_ref, v_ref, tab_ref, tab_t_ref, grad_ref, exact_ref, stat_ref,
    out_ref, tab_grad_ref, kaug, kaug_t, vaug, key_sum, value_sum,
):
    step = pl.program_id(0)
    count, _, width = k_ref.shape
    tail_row = lax.broadcasted_iota(jnp.int32, (128 - HEAD_DIM, width), 0)

    @pl.when(step == 0)
    def _():
        fill_keys(k_ref, kaug)
        pad = jnp.where(tail_row < 3, 1.0, 0.0)
        for part in range(count):
            rows = slice(part * width, (part + 1) * width)
            value = jnp.concatenate([v_ref[part].astype(F32), pad], 0)
            vaug[rows, :] = value.T.astype(BF16)
            kaug_t[0:128, rows] = kaug[rows, 0:128].astype(F32).T.astype(BF16)
            kaug_t[128:208, rows] = k_ref[part]
            kaug_t[208:256, rows] = jnp.zeros((48, width), BF16)
        key_sum[...] = jnp.zeros_like(key_sum)
        value_sum[...] = jnp.zeros_like(value_sum)
        tab_grad_ref[...] = jnp.zeros_like(tab_grad_ref)

    q = q_ref[0]
    grad = grad_ref[0]
    tail_row = lax.broadcasted_iota(jnp.int32, (128 - HEAD_DIM, QUERIES), 0)

    def tail(row):
        out = jnp.zeros((128 - HEAD_DIM, QUERIES), F32)
        for place, term in enumerate(split(row, 3)):
            out = jnp.where(tail_row == place, term.astype(F32), out)
        return out.astype(BF16)

    inner = jnp.sum(grad.astype(F32) * exact_ref[0], 0, keepdims=True)
    columns = query_columns(q, tab_ref[...], step, tail(-stat_ref[0, 0:1]))
    grad_columns = jnp.concatenate([grad, tail(-inner)], 0)
    zero_tail = jnp.zeros((128 - HEAD_DIM, QUERIES), F32)
    grad_rows = jnp.concatenate([grad.astype(F32), zero_tail], 0).T.astype(BF16)
    q_rows = jnp.concatenate([q.astype(F32), zero_tail], 0).T.astype(BF16)
    spread = None
    for chunk in range(kaug.shape[0] // KEYS):
        keys = slice(chunk * KEYS, (chunk + 1) * KEYS)
        weights = jnp.exp2(mm(kaug[keys, :], columns) * (SCALE * LOG2E))
        score_grad = (weights * mm(vaug[keys, :], grad_columns)).astype(BF16)
        value_sum[keys, :] += mm(weights.astype(BF16), grad_rows)
        key_sum[keys, :] += mm(score_grad, q_rows)
        result = mm(kaug_t[:, keys], score_grad)
        spread = result if spread is None else spread + result

    shift_rows, shift_cols = token_shifts(step)
    lifted = jnp.concatenate(
        [unskew(spread[:GRID], shift_rows), unskew(spread[GRID : 2 * GRID], shift_cols)], 0
    )
    high, low = split(lifted, 2)
    query_grad = spread[128 : 128 + HEAD_DIM] * SCALE
    query_grad = query_grad + (mm(tab_t_ref[...], high) + mm(tab_t_ref[...], low))
    tab_grad_ref[...] += mm_nt(high, q) + mm_nt(low, q)
    per_part = width // QUERIES
    lanes = pl.ds(pl.multiple_of((step % per_part) * QUERIES, QUERIES), QUERIES)
    out_ref[step // per_part, 0:HEAD_DIM, lanes] = query_grad.astype(BF16)

    @pl.when(step == pl.num_programs(0) - 1)
    def _():
        for part in range(count):
            rows = slice(part * width, (part + 1) * width)
            key_grad = (key_sum[rows, :] * SCALE).T[:HEAD_DIM]
            out_ref[part, HEAD_DIM : 2 * HEAD_DIM, :] = key_grad.astype(BF16)
            value_grad = value_sum[rows, :].T[:HEAD_DIM]
            out_ref[part, 2 * HEAD_DIM : 3 * HEAD_DIM, :] = value_grad.astype(BF16)


def part_spec(rows, width, row_block):
    per_part = width // QUERIES
    return pl.BlockSpec((1, rows, QUERIES), lambda i: (i // per_part, row_block, i % per_part))


def whole_spec(shape, at=None):
    place = at or (0,) * len(shape)
    return pl.BlockSpec(shape, lambda i: place, pipeline_mode=pl.Buffered(1))


MIX_SUBS = 2
TO_NEAR, PASS_ON, TO_FAR, OUT_NEAR, OUT_FAR, OUT_ON = range(6)


def normal(values):
    center, inv = moments(values)
    return (values - center) * inv, inv


def normal_back(grad, scaled, inv, gain):
    grad = grad * gain
    return inv * (
        grad
        - jnp.mean(grad, -1, keepdims=True)
        - scaled * jnp.mean(grad * scaled, -1, keepdims=True)
    )


def add_sums(sums_ref, piece, terms):
    for place, term in enumerate(terms):
        total = jnp.sum(term, 0, keepdims=True)
        if piece:
            total = total + sums_ref[place : place + 1]
        sums_ref[place : place + 1] = total


def forward_finish(total, piece, rows, vec_ref, first_ref, out_refs):
    middle = first_ref[rows].astype(F32) + (total + vec_ref[2:3])
    out_refs[0][rows] = middle
    scaled, _ = normal(middle)
    return (scaled * vec_ref[0:1] + vec_ref[1:2]).astype(BF16)


def backward_finish(total, piece, rows, vec_ref, first_ref, add_ref, out_refs):
    scaled, inv = normal(first_ref[rows].astype(F32))
    result = add_ref[rows].astype(F32) + normal_back(total, scaled, inv, vec_ref[0:1])
    branch = result.astype(BF16)
    out_refs[0][rows] = result
    add_sums(out_refs[1], piece, (total * scaled, total, branch.astype(F32)))
    return branch


def last_finish(total, piece, rows, vec_ref, first_ref, add_ref, out_refs):
    scaled, inv = normal(first_ref[rows].astype(F32))
    add_sums(out_refs[1], piece, (total * scaled, total))
    return add_ref[rows] + normal_back(total, scaled, inv, vec_ref[0:1])


def row_mix_kernel(finish, extra, outs, left_t, to_features, left_ref, weight_ref, *refs):
    extra_refs, refs = refs[:extra], refs[extra:]
    out_refs, refs = refs[:outs], refs[outs:]
    gathered, out_refs = out_refs[0], out_refs[1:]
    far_keep, own_keep, out_box, in_box, send_sems, recv_sems = refs[:6]
    own = far_keep.shape[0]
    sub = own // MIX_SUBS
    me = lax.axis_index("row")
    near = me + 1 - 2 * lax.rem(me, 2)
    far = lax.rem(me + 2, 4)
    diag = lax.rem(near + 2, 4)
    peers = (near, far, diag) if to_features else (near, far)
    barrier = pltpu.get_barrier_semaphore()
    for peer in peers:
        pl.semaphore_signal(barrier, device_id={"row": peer}, device_id_type=MESH)
    pl.semaphore_wait(barrier, len(peers))

    started = []

    def send(source, target, kind, piece, peer):
        copy = pltpu.make_async_remote_copy(
            src_ref=source,
            dst_ref=target,
            send_sem=send_sems.at[kind, piece],
            recv_sem=recv_sems.at[kind, piece],
            device_id={"row": peer},
            device_id_type=MESH,
        )
        copy.start()
        started.append(copy)
        return copy

    def product(owner, piece):
        at = pl.ds(pl.multiple_of(owner * own + piece * sub, sub), sub)
        if left_t:
            left = left_ref[:, at].astype(F32).T.astype(BF16)
        else:
            left = left_ref[at, :]
        return mm(left, weight_ref[...])

    pieces = [slice(piece * sub, (piece + 1) * sub) for piece in range(MIX_SUBS)]
    passed, direct, summed = [], [], []
    for piece, rows in enumerate(pieces):
        out_box[0, rows] = product(diag, piece).astype(BF16)
        passed.append(send(out_box.at[0, rows], in_box.at[0, rows], PASS_ON, piece, near))
        far_keep[rows] = product(far, piece)
    for piece, rows in enumerate(pieces):
        out_box[1, rows] = product(near, piece).astype(BF16)
        direct.append(send(out_box.at[1, rows], in_box.at[1, rows], TO_NEAR, piece, near))
        passed[piece].wait_recv()
        out_box[2, rows] = (far_keep[rows] + in_box[0, rows].astype(F32)).astype(BF16)
        summed.append(send(out_box.at[2, rows], in_box.at[2, rows], TO_FAR, piece, far))
    for piece, rows in enumerate(pieces):
        own_keep[rows] = product(me, piece)
    near_out, far_out, on_out = [], [], []
    for piece, rows in enumerate(pieces):
        direct[piece].wait_recv()
        summed[piece].wait_recv()
        total = own_keep[rows] + in_box[1, rows].astype(F32) + in_box[2, rows].astype(F32)
        result = finish(total, piece, rows, *extra_refs, out_refs)
        if to_features:
            boxes, arrived = refs[6:]
            part = gathered.shape[1]
            for place in range(4):
                boxes[place, rows] = result[:, place * part : (place + 1) * part].astype(BF16)
            arrived[me, rows] = boxes[me, rows]
            for kind, peer, copies in ((OUT_NEAR, near, near_out), (OUT_FAR, far, far_out), (OUT_ON, diag, on_out)):
                copies.append(send(boxes.at[peer, rows], arrived.at[me, rows], kind, piece, peer))
        else:
            gathered[me, rows] = result
            near_out.append(send(gathered.at[me, rows], gathered.at[me, rows], OUT_NEAR, piece, near))
            far_out.append(send(gathered.at[me, rows], gathered.at[me, rows], OUT_FAR, piece, far))
    for piece, rows in enumerate(pieces):
        far_out[piece].wait_recv()
        if not to_features:
            on_out.append(send(gathered.at[far, rows], gathered.at[far, rows], OUT_ON, piece, near))
    for copy in near_out + on_out:
        copy.wait_recv()
    if to_features:
        boxes, arrived = refs[6:]
        for source in range(4):
            gathered[source * own : (source + 1) * own, :] = arrived[source].astype(F32)
    for copy in started:
        copy.wait_send()


def row_mix(finish, name, number, left, weight, extra, out_shapes, left_t, to_features=False):
    tokens = left.shape[1] if left_t else left.shape[0]
    model = weight.shape[1]
    own = tokens // 4
    if to_features:
        first = jax.ShapeDtypeStruct((tokens, model // 4), F32)
        more = [pltpu.VMEM((4, own, model // 4), BF16), pltpu.VMEM((4, own, model // 4), BF16)]
    else:
        first = jax.ShapeDtypeStruct((4, own, model), BF16)
        more = []
    vmem = pl.BlockSpec(memory_space=pltpu.VMEM)
    return pl.pallas_call(
        partial(row_mix_kernel, finish, len(extra), 1 + len(out_shapes), left_t, to_features),
        out_shape=[first, *out_shapes],
        in_specs=[vmem] * (2 + len(extra)),
        out_specs=[vmem] * (1 + len(out_shapes)),
        scratch_shapes=[
            pltpu.VMEM((own, model), F32),
            pltpu.VMEM((own, model), F32),
            pltpu.VMEM((3, own, model), BF16),
            pltpu.VMEM((3, own, model), BF16),
            pltpu.SemaphoreType.DMA((6, MIX_SUBS)),
            pltpu.SemaphoreType.DMA((6, MIX_SUBS)),
            *more,
        ],
        compiler_params=pltpu.CompilerParams(
            collective_id=number, has_side_effects=True, vmem_limit_bytes=48 << 20
        ),
        cost_estimate=pl.CostEstimate(
            flops=2 * tokens * weight.size, bytes_accessed=16 * own * model, transcendentals=0
        ),
        name=name,
    )(left, weight, *extra)


def attention(qkv, table):
    count, _, width = qkv.shape
    tokens = count * width
    heads = (count, HEAD_DIM, width)
    return pl.pallas_call(
        attend_kernel,
        grid=(tokens // QUERIES,),
        in_specs=[
            part_spec(HEAD_DIM, width, 0),
            whole_spec(heads, (0, 1, 0)),
            whole_spec(heads, (0, 2, 0)),
            whole_spec(table.shape),
        ],
        out_specs=[part_spec(HEAD_DIM, width, 0), part_spec(HEAD_DIM, width, 0), part_spec(8, width, 0)],
        out_shape=[
            jax.ShapeDtypeStruct(heads, BF16),
            jax.ShapeDtypeStruct(heads, F32),
            jax.ShapeDtypeStruct((count, 8, width), F32),
        ],
        scratch_shapes=[pltpu.VMEM((tokens, 256), BF16)],
        compiler_params=pltpu.CompilerParams(vmem_limit_bytes=48 << 20),
        cost_estimate=pl.CostEstimate(
            flops=2 * tokens * tokens * 512,
            bytes_accessed=6 * tokens * HEAD_DIM * 2,
            transcendentals=tokens * tokens,
        ),
        name="attend",
    )(qkv, qkv, qkv, table)


def attention_back(qkv, table, grad, exact, stat):
    count, _, width = qkv.shape
    tokens = count * width
    heads = (count, HEAD_DIM, width)
    return pl.pallas_call(
        attend_back_kernel,
        grid=(tokens // QUERIES,),
        in_specs=[
            part_spec(HEAD_DIM, width, 0),
            whole_spec(heads, (0, 1, 0)),
            whole_spec(heads, (0, 2, 0)),
            whole_spec(table.shape),
            whole_spec(table.shape[::-1]),
            part_spec(HEAD_DIM, width, 0),
            part_spec(HEAD_DIM, width, 0),
            part_spec(8, width, 0),
        ],
        out_specs=[whole_spec((count, 3 * HEAD_DIM, width)), whole_spec(table.shape)],
        out_shape=[
            jax.ShapeDtypeStruct((count, 3 * HEAD_DIM, width), BF16),
            jax.ShapeDtypeStruct(table.shape, F32),
        ],
        scratch_shapes=[
            pltpu.VMEM((tokens, 256), BF16),
            pltpu.VMEM((256, tokens), BF16),
            pltpu.VMEM((tokens, 128), BF16),
            pltpu.VMEM((tokens, 128), F32),
            pltpu.VMEM((tokens, 128), F32),
        ],
        compiler_params=pltpu.CompilerParams(vmem_limit_bytes=48 << 20),
        cost_estimate=pl.CostEstimate(
            flops=2 * tokens * tokens * 1280,
            bytes_accessed=12 * tokens * HEAD_DIM * 2,
            transcendentals=tokens * tokens,
        ),
        name="attend_back",
    )(qkv, qkv, qkv, table, table.T, grad, exact, stat)


def sum_kernel(axes, value_ref, out_ref, *scratch):
    slots, sends, recvs = scratch[: len(axes)], scratch[len(axes) : -1], scratch[-1]
    me = {name: lax.axis_index(name) for name, _ in axes}
    barrier = pltpu.get_barrier_semaphore()
    for name, size in axes:
        for step in range(1, size):
            pl.semaphore_signal(
                barrier, device_id={name: lax.rem(me[name] + step, size)}, device_id_type=MESH
            )
    pl.semaphore_wait(barrier, sum(size - 1 for _, size in axes))
    out_ref[...] = value_ref[...]
    for order, (name, size) in enumerate(axes):
        slot, send = slots[order], sends[order]
        slot[me[name]] = out_ref[...]
        copies = []
        for step in range(1, size):
            copy = pltpu.make_async_remote_copy(
                src_ref=out_ref,
                dst_ref=slot.at[me[name]],
                send_sem=send.at[step],
                recv_sem=recvs.at[order, step],
                device_id={name: lax.rem(me[name] + step, size)},
                device_id_type=MESH,
            )
            copy.start()
            copies.append(copy)
        for copy in copies:
            copy.wait()
        total = slot[0]
        for source in range(1, size):
            total = total + slot[source]
        out_ref[...] = total


def sum_everywhere(values):
    axes = tuple((name, lax.axis_size(name)) for name in ("row", "batch", "col"))
    return pl.pallas_call(
        partial(sum_kernel, axes),
        out_shape=jax.ShapeDtypeStruct(values.shape, F32),
        in_specs=[pl.BlockSpec(memory_space=pltpu.VMEM)],
        out_specs=pl.BlockSpec(memory_space=pltpu.VMEM),
        scratch_shapes=[
            *[pltpu.VMEM((size, *values.shape), F32) for _, size in axes],
            *[pltpu.SemaphoreType.DMA((size,)) for _, size in axes],
            pltpu.SemaphoreType.DMA((len(axes), max(size for _, size in axes))),
        ],
        compiler_params=pltpu.CompilerParams(collective_id=0, has_side_effects=True, vmem_limit_bytes=32 << 20),
        name="sum_everywhere",
    )(values)


def moments(values):
    center = jnp.mean(values, -1, keepdims=True)
    spread = jnp.mean(values * values, -1, keepdims=True)
    return center, lax.rsqrt(spread - center * center + EPSILON)


def shards(
    patches,
    qkv_weight,
    qv_bias,
    proj_weight,
    proj_bias,
    norm1_gain,
    norm1_shift,
    norm2_gain,
    norm2_shift,
    fc1_weight,
    fc1_bias,
    fc2_weight,
    fc2_bias,
    height_table,
    width_table,
    out_grad,
):
    rows, cols = lax.axis_size("row"), lax.axis_size("col")
    row, col = lax.axis_index("row"), lax.axis_index("col")
    width = patches.shape[1]
    part = patches.shape[2]
    model = part * rows
    own = width // rows
    hidden = fc1_bias.shape[0] // rows
    head = HEAD_DIM

    def over_row(values):
        return lax.all_gather(values, "row", axis=1, tiled=True)

    def spread_rows(values):
        moved = lax.all_to_all(values, "row", 0, 0, tiled=True)
        return moved.transpose(1, 0, 2).reshape(values.shape[1], model)

    residual = over_row(patches[0])
    cotangent = over_row(out_grad[0])
    vectors = lax.all_gather(
        jnp.stack([norm1_gain, norm1_shift, norm2_gain, norm2_shift, proj_bias, fc2_bias]),
        "row", axis=1, tiled=True,
    )
    gain1, shift1, gain2, shift2, bias_proj, bias_fc2 = [vectors[i] for i in range(6)]
    by_col = lax.all_gather(
        jnp.concatenate([qv_bias.reshape(-1), fc1_bias]), "col", axis=0, tiled=False
    )
    bias_qv = by_col[:, : 2 * rows * head].reshape(cols, 2, rows, head)
    bias_qv = lax.dynamic_index_in_dim(bias_qv, row, 2, keepdims=False)
    bias_fc1 = by_col[:, 2 * rows * head :].reshape(cols, rows, hidden)
    bias_fc1 = lax.dynamic_index_in_dim(bias_fc1, row, 1, keepdims=False)
    bias_fc1 = bias_fc1.reshape(cols * hidden)

    local_qkv = qkv_weight.reshape(part, 3, rows, head).transpose(2, 1, 3, 0)
    local_rest = jnp.concatenate(
        [
            proj_weight.reshape(rows, head, part),
            fc1_weight.T.reshape(rows, hidden, part),
            fc2_weight.reshape(rows, hidden, part),
        ],
        1,
    )
    spread_qkv = spread_rows(local_qkv.reshape(rows, 3 * head, part))
    local_rest, spread_qkv = lax.optimization_barrier((local_rest, spread_qkv))
    spread_rest = spread_rows(local_rest)
    weight_qkv = lax.all_gather(spread_qkv, "col", axis=0, tiled=True)

    zero_row = jnp.zeros((1, head), BF16)
    table = jnp.concatenate([height_table[::-1], zero_row, width_table[::-1], zero_row], 0)

    first = residual.astype(F32)
    center1, inv1 = moments(first)
    scaled1 = (first - center1) * inv1
    normed1 = (scaled1 * gain1 + shift1).astype(BF16)
    normed1, spread_rest = lax.optimization_barrier((normed1, spread_rest))
    weight_proj = lax.all_gather(spread_rest[:head], "col", axis=0, tiled=True)
    weight_fc1 = lax.all_gather(spread_rest[head : head + hidden], "col", axis=0, tiled=True)
    weight_fc2 = lax.all_gather(spread_rest[head + hidden :], "col", axis=0, tiled=True)
    bias = jnp.stack([bias_qv[:, 0], jnp.zeros_like(bias_qv[:, 0]), bias_qv[:, 1]], 1)
    qkv = mm_nt(weight_qkv, normed1)
    qkv = (qkv.reshape(cols, 3 * head, width) + bias.reshape(cols, 3 * head, 1)).astype(BF16)
    qkv = lax.all_to_all(qkv, "col", 0, 0, tiled=True)
    qkv, weight_fc1 = lax.optimization_barrier((qkv, weight_fc1))
    merged, exact, stat = attention(qkv, table)
    merged, weight_proj, weight_fc2 = lax.optimization_barrier((merged, weight_proj, weight_fc2))
    merged = lax.all_to_all(merged, "col", 0, 0, tiled=True).reshape(cols * head, width)

    def contract_rows(left, right):
        return lax.dot_general(left, right, (((0,), (0,)), ((), ())), preferred_element_type=F32)

    def tokens_of_row(values):
        return lax.dynamic_slice_in_dim(values, row * own, own, 0)

    def sum_tokens(values):
        return lax.psum_scatter(values.astype(BF16), "row", scatter_dimension=0, tiled=True)

    own_shape = (own, model)
    vec2 = jnp.stack([gain2, shift2, bias_proj])
    normed2, middle = row_mix(
        forward_finish, "middle_and_norm2", 1, merged, weight_proj,
        (vec2, tokens_of_row(residual)), [jax.ShapeDtypeStruct(own_shape, F32)], True,
    )
    normed2 = normed2.reshape(width, model)
    preact = mm_nt(normed2, weight_fc1) + bias_fc1
    activated, gelu_back = jax.vjp(partial(jax.nn.gelu, approximate=False), preact)
    activated = activated.astype(BF16)
    lowered = sum_tokens(mm(activated, weight_fc2)).astype(F32)
    final = (middle + (lowered + bias_fc2)).astype(BF16)
    final = final.reshape(own, rows, part).transpose(1, 0, 2)
    final = lax.all_to_all(final, "row", 0, 0, tiled=True).reshape(width, part)

    act_grad = mm_nt(cotangent, weight_fc2)
    preact_grad = gelu_back(act_grad)[0].astype(BF16)
    own_and_sums = [jax.ShapeDtypeStruct(own_shape, F32), jax.ShapeDtypeStruct((3, model), F32)]
    branch_grad, middle_grad, sums2 = row_mix(
        backward_finish, "middle_grad", 2, preact_grad, weight_fc1,
        (vec2, middle, tokens_of_row(cotangent)), own_and_sums, False,
    )
    branch_grad = branch_grad.reshape(width, model)

    merged_grad = mm_nt(weight_proj, branch_grad).astype(BF16).reshape(cols, head, width)
    merged_grad = lax.all_to_all(merged_grad, "col", 0, 0, tiled=True)
    qkv_grad, table_grad = attention_back(qkv, table, merged_grad, exact, stat)
    bias_grad = jnp.sum(qkv_grad, (0, 2), dtype=F32).reshape(3, head)
    qkv_grad = lax.all_to_all(qkv_grad, "col", 0, 0, tiled=True).reshape(cols * 3 * head, width)

    input_grad, _, sums1 = row_mix(
        last_finish, "patches_grad", 3, qkv_grad, weight_qkv,
        (gain1[None], tokens_of_row(residual), middle_grad), own_and_sums, True, True,
    )

    def weight_back(values):
        values = lax.psum_scatter(values.astype(BF16), "col", scatter_dimension=0, tiled=False)
        values = values.reshape(-1, rows, part).transpose(1, 0, 2)
        values = lax.all_to_all(values, "row", 0, 0, tiled=True)
        if lax.axis_size("batch") != 2:
            return lax.psum(values, "batch").astype(F32)
        other = lax.ppermute(values, "batch", [(0, 1), (1, 0)])
        return values.astype(F32) + other.astype(F32)

    fc2_grad = contract_rows(activated, cotangent).reshape(cols, hidden, model)
    fc2_grad = weight_back(fc2_grad).reshape(rows * hidden, part)
    fc1_grad = contract_rows(preact_grad, normed2).reshape(cols, hidden, model)
    fc1_grad = weight_back(fc1_grad).reshape(rows * hidden, part).T
    proj_grad = mm(merged, branch_grad).reshape(cols, head, model)
    proj_grad = weight_back(proj_grad).reshape(rows * head, part)
    qkv_weight_grad = mm(qkv_grad, normed1).reshape(cols, 3 * head, model)
    qkv_weight_grad = weight_back(qkv_weight_grad).reshape(rows, 3, head, part)
    qkv_weight_grad = qkv_weight_grad.transpose(3, 1, 0, 2).reshape(part, 3, rows * head)

    fc1_bias_part = jnp.sum(preact_grad, 0, dtype=F32).reshape(cols, 1, hidden)
    fc1_bias_part = lax.dynamic_update_slice(
        jnp.zeros((cols, rows, hidden), F32), fc1_bias_part, (0, row, 0)
    )
    fc2_bias_part = lax.dynamic_update_slice(
        jnp.zeros((rows, part), F32), jnp.sum(out_grad[0], 0, dtype=F32)[None], (row, 0)
    )
    bias_part = lax.dynamic_update_slice(
        jnp.zeros((cols, 2, rows, head), F32),
        jnp.stack([bias_grad[0], bias_grad[2]])[None, :, None],
        (col, 0, row, 0),
    )
    pieces = [
        table_grad,
        bias_part,
        fc1_bias_part,
        fc2_bias_part,
        sums2,
        sums1[:2],
    ]
    flat = jnp.concatenate([piece.reshape(-1) for piece in pieces]).reshape(-1, 128)
    flat = sum_everywhere(flat).reshape(-1)
    sums = []
    for piece in pieces:
        sums.append(flat[: piece.size].reshape(piece.shape))
        flat = flat[piece.size :]
    (
        table_grad, bias_total, fc1_bias_grad, fc2_bias_grad,
        (gain2_grad, shift2_grad, proj_bias_grad), (gain1_grad, shift1_grad),
    ) = sums

    def features_of_row(values):
        return lax.dynamic_slice_in_dim(values, row * part, part, 0)

    side = 2 * GRID - 1
    return (
        final[None],
        input_grad[None],
        qkv_weight_grad,
        lax.dynamic_index_in_dim(bias_total, col, 0, keepdims=False).reshape(2, rows * head),
        proj_grad,
        features_of_row(proj_bias_grad),
        features_of_row(gain1_grad),
        features_of_row(shift1_grad),
        features_of_row(gain2_grad),
        features_of_row(shift2_grad),
        fc1_grad,
        lax.dynamic_index_in_dim(fc1_bias_grad, col, 0, keepdims=False).reshape(rows * hidden),
        fc2_grad,
        lax.dynamic_index_in_dim(fc2_bias_grad, row, 0, keepdims=False),
        table_grad[:side][::-1],
        table_grad[2 * GRID : 2 * GRID + side][::-1],
    )


def solution(mesh):
    in_specs = (
        P("batch", "col", "row"),
        P("row", None, "col"),
        P(None, "col"),
        P("col", "row"),
        P("row"),
        P("row"),
        P("row"),
        P("row"),
        P("row"),
        P("row", "col"),
        P("col"),
        P("col", "row"),
        P("row"),
        P(),
        P(),
        P("batch", "col", "row"),
    )
    out_specs = (
        P("batch", "col", "row"),
        P("batch", "col", "row"),
        P("row", None, "col"),
        P(None, "col"),
        P("col", "row"),
        P("row"),
        P("row"),
        P("row"),
        P("row"),
        P("row"),
        P("row", "col"),
        P("col"),
        P("col", "row"),
        P("row"),
        P(),
        P(),
    )
    return jax.shard_map(shards, mesh=mesh, in_specs=in_specs, out_specs=out_specs, check_vma=False)
```

```python
import math
from functools import partial

import jax
import jax.numpy as jnp
from jax import lax
from jax.experimental import pallas as pl
from jax.experimental.pallas import tpu as pltpu
from jax.sharding import PartitionSpec as P

D = 1280
HEAD_DIM = 80
GRID = 64
EPSILON = 1e-06

LINES = 4
QUERIES = LINES * GRID
KEYS = 512
LOG2E = math.log2(math.e)
SCALE = HEAD_DIM**-0.5
BF16 = jnp.bfloat16
F32 = jnp.float32
MESH = pl.DeviceIdType.MESH


def mm(left, right):
    return jnp.dot(left, right, preferred_element_type=F32)


def mm_nt(left, right):
    return lax.dot_general(left, right, (((1,), (1,)), ((), ())), preferred_element_type=F32)


def split(values, parts):
    terms = []
    for _ in range(parts):
        term = values.astype(BF16)
        terms.append(term)
        values = values - term.astype(F32)
    return terms


def skew(values, shift):
    n = values.shape[1]
    for bit, rows in ((32, 96), (16, 80), (8, 72)):
        take = jnp.broadcast_to(shift, (rows, n)) & bit
        values = jnp.where(take != 0, values[bit : bit + rows], values[:rows])
    for bit in (4, 2, 1):
        take = jnp.broadcast_to(shift, values.shape) & bit
        values = jnp.where(take != 0, pltpu.roll(values, values.shape[0] - bit, 0), values)
    return values[:GRID]


def unskew(values, shift):
    n = values.shape[1]
    values = jnp.concatenate([values, jnp.zeros((8, n), F32)], 0)
    for bit in (1, 2, 4):
        take = jnp.broadcast_to(shift, values.shape) & bit
        values = jnp.where(take != 0, pltpu.roll(values, bit, 0), values)
    for bit in (8, 16, 32):
        zeros = jnp.zeros((bit, n), F32)
        take = jnp.broadcast_to(shift, (values.shape[0] + bit, n)) & bit
        values = jnp.where(
            take != 0,
            jnp.concatenate([zeros, values], 0),
            jnp.concatenate([values, zeros], 0),
        )
    return values


def token_shifts(step):
    lane = lax.broadcasted_iota(jnp.int32, (1, QUERIES), 1)
    return (GRID - 1) - (step * LINES + lane // GRID), (GRID - 1) - lane % GRID


def query_columns(q, tab, step, tail):
    shift_rows, shift_cols = token_shifts(step)
    both = mm(tab, q)
    rel_rows = skew(both[: 2 * GRID], shift_rows)
    rel_cols = skew(both[2 * GRID :], shift_cols)
    rel = jnp.concatenate([rel_rows, rel_cols], 0) * (1.0 / SCALE)
    return jnp.concatenate([rel.astype(BF16), q, tail], 0)


def col_peer(step):
    me = lax.axis_index("col")
    odd, high = step % 2, step // 2
    return lax.rem(me + odd - 2 * odd * lax.rem(me, 2) + 2 * high, 4)


def col_barrier():
    barrier = pltpu.get_barrier_semaphore()
    for step in range(1, 4):
        pl.semaphore_signal(barrier, device_id={"col": col_peer(step)}, device_id_type=MESH)
    pl.semaphore_wait(barrier, 3)


def col_copy(source, target, sems, kind, step):
    return pltpu.make_async_remote_copy(
        src_ref=source,
        dst_ref=target,
        send_sem=sems.at[0, kind, step],
        recv_sem=sems.at[1, kind, step],
        device_id={"col": col_peer(step)},
        device_id_type=MESH,
    )


def attend_kernel(
    given_ref, tab_ref, proj_ref, merged_ref, qkv_ref, exact_ref, stat_ref, proj_all_ref,
    kaug, columns, acc, top, total, box, sems,
):
    me = lax.axis_index("col")
    width = given_ref.shape[2]
    blocks = width // QUERIES
    col_barrier()

    def part_copy(step):
        return col_copy(given_ref.at[col_peer(step)], qkv_ref.at[me], sems, 0, step)

    def merged_copy(step):
        return col_copy(box.at[col_peer(step)], merged_ref.at[me], sems, 1, step)

    def proj_copy(step):
        return col_copy(proj_ref, proj_all_ref.at[me], sems, 2, step)

    for step in range(1, 4):
        part_copy(step).start()
    for step in range(1, 4):
        proj_copy(step).start()
    qkv_ref[me] = given_ref[me]
    proj_all_ref[me] = proj_ref[...]

    pad = jnp.zeros((128 - HEAD_DIM, width), F32)
    token = lax.broadcasted_iota(jnp.int32, (width, 2 * GRID), 0)
    lane = lax.broadcasted_iota(jnp.int32, (width, 2 * GRID), 1)
    tail = jnp.zeros((128 - HEAD_DIM, QUERIES), BF16)
    factor = SCALE * LOG2E

    def prepare(part):
        at = token + part * width
        hot = jnp.where(jnp.where(lane < GRID, at // GRID, at % GRID + GRID) == lane, 1.0, 0.0)
        key = qkv_ref[part, HEAD_DIM : 2 * HEAD_DIM]
        kaug[part, :, 0:128] = hot.astype(BF16)
        kaug[part, :, 128:256] = jnp.concatenate([key.astype(F32), pad], 0).T.astype(BF16)
        for block in range(blocks):
            at = slice(block * QUERIES, (block + 1) * QUERIES)
            columns[part, :, at] = query_columns(
                qkv_ref[part, 0:HEAD_DIM, at], tab_ref[...], part * blocks + block, tail
            )
        acc[part] = jnp.zeros((HEAD_DIM, width), F32)
        top[part] = jnp.full((8, width), -1e30, F32)
        total[part] = jnp.zeros((8, width), F32)

    def finish(part):
        whole, best = total[part, 0:1], top[part, 0:1]
        result = acc[part] * (1.0 / whole)
        exact_ref[part] = result
        box[part] = result.astype(BF16)
        stat_ref[part] = jnp.broadcast_to(best + jnp.log2(whole) * (1.0 / factor), (8, width))

    def pair(turn, carry):
        newest = (turn + 15) // 16 + (turn + 12) // 16 + (turn + 7) // 16
        place = turn - newest * newest
        q_step = jnp.where(place < newest, place, newest)
        k_step = jnp.where(place < newest, newest, place - newest)
        q_part, k_part = col_peer(q_step), col_peer(k_step)

        @pl.when(jnp.logical_and(place == 0, newest > 0))
        def _():
            part_copy(newest).wait_recv()

        @pl.when(place == 0)
        def _():
            prepare(col_peer(newest))

        for block in range(blocks):
            at = slice(block * QUERIES, (block + 1) * QUERIES)
            best, whole, result = top[q_part, 0:1, at], total[q_part, 0:1, at], acc[q_part, :, at]
            for start in range(0, width, KEYS):
                keys = slice(start, start + KEYS)
                scores = mm(kaug[k_part, keys], columns[q_part, :, at])
                new_best = jnp.maximum(best, jnp.max(scores, 0, keepdims=True))
                weights = jnp.exp2((scores - new_best) * factor)
                keep = jnp.exp2((best - new_best) * factor)
                whole = whole * keep + jnp.sum(weights, 0, keepdims=True)
                value = qkv_ref[k_part, 2 * HEAD_DIM : 3 * HEAD_DIM, keys]
                result = result * keep + mm(value, weights.astype(BF16))
                best = new_best
            top[q_part, :, at] = jnp.broadcast_to(best, (8, QUERIES))
            total[q_part, :, at] = jnp.broadcast_to(whole, (8, QUERIES))
            acc[q_part, :, at] = result

        @pl.when(jnp.logical_and(turn >= 9, jnp.logical_or(place < 3, turn == 15)))
        def _():
            finish(q_part)

        @pl.when(jnp.logical_and(turn >= 9, jnp.logical_or(jnp.logical_and(turn > 9, place < 3), turn == 15)))
        def _():
            merged_copy(q_step).start()

        return carry

    lax.fori_loop(0, 16, pair, 0)
    merged_ref[me] = box[me]
    for step in range(1, 4):
        part_copy(step).wait_send()
        proj_copy(step).wait()
        merged_copy(step).wait()


GRADS, QUERY_OUT, KEY_OUT, PROJ_OUT = range(4)
KEY_ROWS = slice(HEAD_DIM, 3 * HEAD_DIM)


def attend_back_kernel(
    images, qkv_ref, tab_ref, tab_t_ref, given_ref, exact_ref, stat_ref, proj_ref, fc2_ref,
    out_ref, tab_grad_ref, bias_out, proj_out, fc2_out,
    bias_ref, proj_rows, proj_box, grads, kaug, kaug_t, vaug, key_sum, value_sum, spread, columns,
    grad_columns, grad_rows, q_rows, box, sems, *weight_parts,
):
    me = lax.axis_index("col")
    width = qkv_ref.shape[2]
    blocks = width // QUERIES
    meet(
        ("row", row_peers()),
        ("col", [col_peer(step) for step in range(1, 4)]),
        ("batch", image_peers(images) if images == 2 else ()),
    )

    def write_proj(place, values):
        proj_out[place] = values

    def write_fc2(place, values):
        fc2_out[place] = values

    fc2 = weight_steps(fc2_ref, images, weight_parts[:4], write_fc2)
    proj = weight_steps(proj_rows, images, weight_parts[4:], write_proj)

    def grad_copy(step):
        return col_copy(given_ref.at[col_peer(step)], grads.at[me], sems, GRADS, step)

    def query_copy(step):
        at = col_peer(step)
        return col_copy(box.at[at, 0:HEAD_DIM], out_ref.at[me, 0:HEAD_DIM], sems, QUERY_OUT, step)

    def key_copy(step):
        at = col_peer(step)
        return col_copy(box.at[at, KEY_ROWS], out_ref.at[me, KEY_ROWS], sems, KEY_OUT, step)

    def proj_copy(step):
        return col_copy(proj_ref.at[col_peer(step)], proj_box.at[me], sems, PROJ_OUT, step)

    for step in range(1, 4):
        grad_copy(step).start()
    for step in range(1, 4):
        proj_copy(step).start()
    next(fc2)
    grads[me] = given_ref[me]
    proj_box[me] = proj_ref[me]

    tail_row = lax.broadcasted_iota(jnp.int32, (128 - HEAD_DIM, width), 0)
    pad = jnp.where(tail_row < 3, 1.0, 0.0)
    token = lax.broadcasted_iota(jnp.int32, (width, 2 * GRID), 0)
    lane = lax.broadcasted_iota(jnp.int32, (width, 2 * GRID), 1)

    def fill(part, carry):
        at = token + part * width
        hot = jnp.where(jnp.where(lane < GRID, at // GRID, at % GRID + GRID) == lane, 1.0, 0.0)
        key, value = qkv_ref[part, HEAD_DIM : 2 * HEAD_DIM], qkv_ref[part, 2 * HEAD_DIM : 3 * HEAD_DIM]
        kaug[part, :, 0:128] = hot.astype(BF16)
        kaug[part, :, 128:256] = jnp.concatenate([key.astype(F32), pad], 0).T.astype(BF16)
        vaug[part] = jnp.concatenate([value.astype(F32), pad], 0).T.astype(BF16)
        kaug_t[part, 0:128] = hot.T.astype(BF16)
        kaug_t[part, 128:208] = key
        kaug_t[part, 208:256] = jnp.zeros((48, width), BF16)
        return carry

    lax.fori_loop(0, 4, fill, 0)
    key_sum[...] = jnp.zeros_like(key_sum)
    value_sum[...] = jnp.zeros_like(value_sum)
    spread[...] = jnp.zeros_like(spread)
    tab_grad_ref[...] = jnp.zeros_like(tab_grad_ref)
    bias_ref[...] = jnp.zeros_like(bias_ref)

    block_row = lax.broadcasted_iota(jnp.int32, (128 - HEAD_DIM, QUERIES), 0)

    def tail(row):
        out = jnp.zeros((128 - HEAD_DIM, QUERIES), F32)
        for place, term in enumerate(split(row, 3)):
            out = jnp.where(block_row == place, term.astype(F32), out)
        return out.astype(BF16)

    zero_tail = jnp.zeros((128 - HEAD_DIM, QUERIES), F32)

    def prepare(part):
        for block in range(blocks):
            at = slice(block * QUERIES, (block + 1) * QUERIES)
            q, grad = qkv_ref[part, 0:HEAD_DIM, at], grads[part, :, at]
            inner = jnp.sum(grad.astype(F32) * exact_ref[part, :, at], 0, keepdims=True)
            columns[part, :, at] = query_columns(
                q, tab_ref[...], part * blocks + block, tail(-stat_ref[part, 0:1, at])
            )
            grad_columns[part, :, at] = jnp.concatenate([grad, tail(-inner)], 0)
            grad_rows[part, at] = jnp.concatenate([grad.astype(F32), zero_tail], 0).T.astype(BF16)
            q_rows[part, at] = jnp.concatenate([q.astype(F32), zero_tail], 0).T.astype(BF16)

    def add_bias(first, values):
        total = jnp.sum(values.astype(F32), 1, keepdims=True)
        bias_ref[first : first + values.shape[0]] += jnp.broadcast_to(total, (values.shape[0], 128))

    def finish_queries(part):
        for block in range(blocks):
            at = slice(block * QUERIES, (block + 1) * QUERIES)
            rows, cols = token_shifts(part * blocks + block)
            lifted = jnp.concatenate(
                [unskew(spread[part, 0:GRID, at], rows), unskew(spread[part, GRID : 2 * GRID, at], cols)], 0
            )
            high, low = split(lifted, 2)
            query_grad = spread[part, 128 : 128 + HEAD_DIM, at] * SCALE
            query_grad = query_grad + (mm(tab_t_ref[...], high) + mm(tab_t_ref[...], low))
            q = qkv_ref[part, 0:HEAD_DIM, at]
            tab_grad_ref[...] += mm_nt(q, high) + mm_nt(q, low)
            box[part, 0:HEAD_DIM, at] = query_grad.astype(BF16)
        add_bias(0, box[part, 0:HEAD_DIM])

    def finish_keys(part):
        key_grad = (key_sum[part] * SCALE).T[:HEAD_DIM].astype(BF16)
        value_grad = value_sum[part].T[:HEAD_DIM].astype(BF16)
        box[part, HEAD_DIM : 2 * HEAD_DIM] = key_grad
        box[part, 2 * HEAD_DIM : 3 * HEAD_DIM] = value_grad
        add_bias(HEAD_DIM, key_grad)
        add_bias(2 * HEAD_DIM, value_grad)

    def pair(turn, carry):
        outer, inner = turn // 4, turn % 4
        q_step = inner + (outer // 3) * (3 - 2 * inner)
        k_step = 3 - outer
        q_part, k_part = col_peer(q_step), col_peer(k_step)

        @pl.when(jnp.logical_and(turn > 0, turn < 4))
        def _():
            grad_copy(q_step).wait_recv()

        @pl.when(turn < 4)
        def _():
            prepare(q_part)

        for block in range(blocks):
            at = slice(block * QUERIES, (block + 1) * QUERIES)
            total = None
            for start in range(0, width, KEYS):
                keys = slice(start, start + KEYS)
                weights = jnp.exp2(mm(kaug[k_part, keys], columns[q_part, :, at]) * (SCALE * LOG2E))
                score_grad = (weights * mm(vaug[k_part, keys], grad_columns[q_part, :, at])).astype(BF16)
                value_sum[k_part, keys] += mm(weights.astype(BF16), grad_rows[q_part, at])
                key_sum[k_part, keys] += mm(score_grad, q_rows[q_part, at])
                result = mm(kaug_t[k_part, :, keys], score_grad)
                total = result if total is None else total + result
            spread[q_part, :, at] += total

        @pl.when(inner == 3)
        def _():
            finish_keys(k_part)

        @pl.when(jnp.logical_and(inner == 3, outer < 3))
        def _():
            key_copy(k_step).start()

        @pl.when(outer == 3)
        def _():
            finish_queries(q_part)

        @pl.when(jnp.logical_and(outer == 3, inner < 3))
        def _():
            query_copy(q_step).start()

        return carry

    lax.fori_loop(0, 4, pair, 0)
    for step in range(1, 4):
        proj_copy(step).wait()
    total = proj_box[0].astype(F32)
    for source in range(1, 4):
        total = total + proj_box[source].astype(F32)
    proj_rows[...] = total.astype(BF16)
    next(fc2)
    next(proj)
    lax.fori_loop(4, 8, pair, 0)
    next(proj)
    next(fc2, None)
    lax.fori_loop(8, 16, pair, 0)
    next(proj, None)
    out_ref[me] = box[me]
    for step in range(1, 4):
        grad_copy(step).wait_send()
        query_copy(step).wait()
        key_copy(step).wait()
    bias_out[0:1] = bias_ref[0:128].T[0:1]
    bias_out[1:2] = bias_ref[2 * HEAD_DIM : 2 * HEAD_DIM + 128].T[0:1]


MIX_SUBS = 2
TO_NEAR, PASS_ON, TO_FAR, OUT_NEAR, OUT_FAR, OUT_ON = range(6)


def normal(values):
    center, inv = moments(values)
    return (values - center) * inv, inv


def normal_back(grad, scaled, inv, gain):
    grad = grad * gain
    return inv * (
        grad
        - jnp.mean(grad, -1, keepdims=True)
        - scaled * jnp.mean(grad * scaled, -1, keepdims=True)
    )


def add_sums(sums_ref, piece, terms):
    for place, term in enumerate(terms):
        total = jnp.sum(term, 0, keepdims=True)
        if piece:
            total = total + sums_ref[place : place + 1]
        sums_ref[place : place + 1] = total


def forward_finish(total, piece, rows, vec_ref, first_ref, out_refs):
    middle = first_ref[rows].astype(F32) + (total + vec_ref[2:3])
    out_refs[0][rows] = middle
    scaled, _ = normal(middle)
    return (scaled * vec_ref[0:1] + vec_ref[1:2]).astype(BF16)


def backward_finish(total, piece, rows, vec_ref, first_ref, add_ref, out_refs):
    scaled, inv = normal(first_ref[rows].astype(F32))
    result = add_ref[rows].astype(F32) + normal_back(total, scaled, inv, vec_ref[0:1])
    branch = result.astype(BF16)
    out_refs[0][rows] = result
    add_sums(out_refs[1], piece, (total * scaled, total, branch.astype(F32)))
    return branch


def last_finish(total, piece, rows, vec_ref, first_ref, add_ref, out_refs):
    scaled, inv = normal(first_ref[rows].astype(F32))
    add_sums(out_refs[1], piece, (total * scaled, total))
    return add_ref[rows] + normal_back(total, scaled, inv, vec_ref[0:1])


def row_peers():
    me = lax.axis_index("row")
    near = me + 1 - 2 * lax.rem(me, 2)
    return near, lax.rem(me + 2, 4), lax.rem(near + 2, 4)


def meet(*groups):
    barrier = pltpu.get_barrier_semaphore()
    for axis, peers in groups:
        for peer in peers:
            pl.semaphore_signal(barrier, device_id={axis: peer}, device_id_type=MESH)
    pl.semaphore_wait(barrier, sum(len(peers) for _, peers in groups))


def row_mix_steps(left_ref, weight_ref, gathered, finish, left_t, to_features, scratch):
    far_keep, own_keep, out_box, in_box, sems, *more = scratch
    own = far_keep.shape[0]
    sub = own // MIX_SUBS
    me = lax.axis_index("row")
    near, far, diag = row_peers()
    started = []

    def send(source, target, kind, piece, peer):
        copy = pltpu.make_async_remote_copy(
            src_ref=source,
            dst_ref=target,
            send_sem=sems.at[0, kind, piece],
            recv_sem=sems.at[1, kind, piece],
            device_id={"row": peer},
            device_id_type=MESH,
        )
        copy.start()
        started.append(copy)
        return copy

    def product(owner, piece):
        at = pl.ds(pl.multiple_of(owner * own + piece * sub, sub), sub)
        if left_t:
            left = left_ref[:, at].astype(F32).T.astype(BF16)
        else:
            left = left_ref[at, :]
        return mm(left, weight_ref[...])

    pieces = [slice(piece * sub, (piece + 1) * sub) for piece in range(MIX_SUBS)]
    passed, direct, summed = [], [], []
    for piece, rows in enumerate(pieces):
        out_box[0, rows] = product(diag, piece).astype(BF16)
        passed.append(send(out_box.at[0, rows], in_box.at[0, rows], PASS_ON, piece, near))
        far_keep[rows] = product(far, piece)
    yield
    for piece, rows in enumerate(pieces):
        out_box[1, rows] = product(near, piece).astype(BF16)
        direct.append(send(out_box.at[1, rows], in_box.at[1, rows], TO_NEAR, piece, near))
        passed[piece].wait_recv()
        out_box[2, rows] = (far_keep[rows] + in_box[0, rows].astype(F32)).astype(BF16)
        summed.append(send(out_box.at[2, rows], in_box.at[2, rows], TO_FAR, piece, far))
    yield
    for piece, rows in enumerate(pieces):
        own_keep[rows] = product(me, piece)
    yield
    near_out, far_out, on_out = [], [], []
    for piece, rows in enumerate(pieces):
        direct[piece].wait_recv()
        summed[piece].wait_recv()
        total = own_keep[rows] + in_box[1, rows].astype(F32) + in_box[2, rows].astype(F32)
        result = finish(total, piece, rows)
        if to_features:
            boxes, arrived = more
            part = gathered.shape[1]
            for place in range(4):
                boxes[place, rows] = result[:, place * part : (place + 1) * part].astype(BF16)
            arrived[me, rows] = boxes[me, rows]
            for kind, peer, copies in (
                (OUT_NEAR, near, near_out), (OUT_FAR, far, far_out), (OUT_ON, diag, on_out)
            ):
                copies.append(send(boxes.at[peer, rows], arrived.at[me, rows], kind, piece, peer))
        else:
            gathered[me, rows] = result
            near_out.append(send(gathered.at[me, rows], gathered.at[me, rows], OUT_NEAR, piece, near))
            far_out.append(send(gathered.at[me, rows], gathered.at[me, rows], OUT_FAR, piece, far))
    yield
    for piece, rows in enumerate(pieces):
        far_out[piece].wait_recv()
        if not to_features:
            on_out.append(send(gathered.at[far, rows], gathered.at[far, rows], OUT_ON, piece, near))
    for copy in near_out + on_out:
        copy.wait_recv()
    if to_features:
        boxes, arrived = more
        for source in range(4):
            gathered[source * own : (source + 1) * own, :] = arrived[source].astype(gathered.dtype)
    for copy in started:
        copy.wait_send()


def mix_scratch(own, model, to_features):
    boxes = [pltpu.VMEM((4, own, model // 4), BF16)] * 2 if to_features else []
    return [
        pltpu.VMEM((own, model), F32),
        pltpu.VMEM((own, model), F32),
        pltpu.VMEM((3, own, model), BF16),
        pltpu.VMEM((3, own, model), BF16),
        pltpu.SemaphoreType.DMA((2, 6, MIX_SUBS)),
        *boxes,
    ]


def row_mix_kernel(finish, extra, outs, left_t, left_ref, weight_ref, *refs):
    extra_refs, refs = refs[:extra], refs[extra:]
    (gathered, *out_refs), scratch = refs[:outs], refs[outs:]
    near, far, _ = row_peers()
    meet(("row", (near, far)))

    def last(total, piece, rows):
        return finish(total, piece, rows, *extra_refs, out_refs)

    for _ in row_mix_steps(left_ref, weight_ref, gathered, last, left_t, False, scratch):
        pass


def row_mix(finish, name, number, left, weight, extra, out_shapes, left_t):
    tokens = left.shape[1] if left_t else left.shape[0]
    model = weight.shape[1]
    own = tokens // 4
    vmem = pl.BlockSpec(memory_space=pltpu.VMEM)
    return pl.pallas_call(
        partial(row_mix_kernel, finish, len(extra), 1 + len(out_shapes), left_t),
        out_shape=[jax.ShapeDtypeStruct((4, own, model), BF16), *out_shapes],
        in_specs=[vmem] * (2 + len(extra)),
        out_specs=[vmem] * (1 + len(out_shapes)),
        scratch_shapes=mix_scratch(own, model, False),
        compiler_params=pltpu.CompilerParams(
            collective_id=number, has_side_effects=True, vmem_limit_bytes=48 << 20
        ),
        cost_estimate=pl.CostEstimate(
            flops=2 * tokens * weight.size, bytes_accessed=16 * own * model, transcendentals=0
        ),
        name=name,
    )(left, weight, *extra)


def weight_steps(values_ref, images, scratch, write):
    boxes, arrived, other, sems = scratch
    me, part = lax.axis_index("row"), boxes.shape[2]
    for place in range(4):
        boxes[place] = values_ref[:, place * part : (place + 1) * part]
    arrived[me] = boxes[me]
    copies = []
    for order, peer in enumerate(row_peers()):
        copy = pltpu.make_async_remote_copy(
            src_ref=boxes.at[peer],
            dst_ref=arrived.at[me],
            send_sem=sems.at[0, order],
            recv_sem=sems.at[1, order],
            device_id={"row": peer},
            device_id_type=MESH,
        )
        copy.start()
        copies.append(copy)
    yield
    for copy in copies:
        copy.wait()
    if images == 2:
        swap = pltpu.make_async_remote_copy(
            src_ref=arrived,
            dst_ref=other,
            send_sem=sems.at[0, 3],
            recv_sem=sems.at[1, 3],
            device_id={"batch": 1 - lax.axis_index("batch")},
            device_id_type=MESH,
        )
        swap.start()
        yield
        swap.wait()
        for place in range(4):
            write(place, arrived[place].astype(F32) + other[place].astype(F32))
    else:
        yield
        for place in range(4):
            write(place, arrived[place].astype(F32))


def weight_scratch(n, part):
    return [*[pltpu.VMEM((4, n, part), BF16)] * 3, pltpu.SemaphoreType.DMA((2, 4))]


def image_peers(images):
    me = lax.axis_index("batch")
    return [lax.rem(me + step, images) for step in range(1, images)]


def sum_steps(total, axes, scratch):
    *slots, sends, recvs = scratch
    for order, (name, size) in enumerate(axes):
        me, slot = lax.axis_index(name), slots[order]
        slot[me] = total[...]
        copies = []
        for step in range(1, size):
            copy = pltpu.make_async_remote_copy(
                src_ref=total,
                dst_ref=slot.at[me],
                send_sem=sends.at[order, step],
                recv_sem=recvs.at[order, step],
                device_id={name: lax.rem(me + step, size)},
                device_id_type=MESH,
            )
            copy.start()
            copies.append(copy)
        yield
        for copy in copies:
            copy.wait()
        whole = slot[0]
        for source in range(1, size):
            whole = whole + slot[source]
        total[...] = whole


def sum_scratch(rows, axes):
    most = max(size for _, size in axes)
    return [
        *[pltpu.VMEM((size, rows, 128), F32) for _, size in axes],
        *[pltpu.SemaphoreType.DMA((len(axes), most))] * 2,
    ]


def column_steps(grad_ref, normed_ref, box, arrived, own_keep, out, sems):
    me = lax.axis_index("col")
    copies = []
    for step in range(1, 4):
        box[step - 1] = mm(grad_ref[col_peer(step)], normed_ref[...]).astype(BF16)
        copy = col_copy(box.at[step - 1], arrived.at[step - 1], sems, 0, step)
        copy.start()
        copies.append(copy)
    yield
    own_keep[...] = mm(grad_ref[me], normed_ref[...])
    yield
    for copy in copies:
        copy.wait()
    total = own_keep[...]
    for step in range(3):
        total = total + arrived[step].astype(F32)
    out[...] = total.astype(BF16)


EARLY_ROWS, TABLE_ROWS, BIAS_ROWS, LAST_ROWS = 80, 160, 32, 24


def tail_kernel(
    axes,
    qkv_grad_ref, grads_ref, weight_qkv_ref, normed1_ref, first_ref, middle_grad_ref, gain_ref,
    activated_ref, weight_fc2_ref, middle_ref, bias_fc2_ref, fc1_ref, early_ref, table_ref, bias_ref,
    patches_out, block_out, qkv_out, fc1_out, small,
    *scratch,
):
    sums1, qkv_rows, box, arrived, own_keep, col_sems, *scratch = scratch
    mix1, mix2 = scratch[:7], scratch[7:14]
    qkv_scratch, fc1_scratch, sum_parts = scratch[14:18], scratch[18:22], scratch[22:]
    row, col = lax.axis_index("row"), lax.axis_index("col")
    images = dict(axes)["batch"]
    meet(
        ("row", row_peers()),
        ("col", [col_peer(step) for step in range(1, 4)]),
        ("batch", image_peers(images)),
    )

    def finish1(total, piece, rows):
        return last_finish(total, piece, rows, gain_ref, first_ref, middle_grad_ref, (None, sums1))

    def finish2(total, piece, rows):
        return middle_ref[rows] + (total + bias_fc2_ref[0:1])

    def write_fc1(place, values):
        n = values.shape[0]
        fc1_out[place * n : (place + 1) * n] = values

    head_grads = []

    def write_qkv(place, values):
        head_grads.append(values)

    qkv_sum = column_steps(grads_ref, normed1_ref, box, arrived, own_keep, qkv_rows, col_sems)
    patches = row_mix_steps(qkv_grad_ref, weight_qkv_ref, patches_out, finish1, True, True, mix1)
    block = row_mix_steps(activated_ref, weight_fc2_ref, block_out, finish2, False, True, mix2)
    fc1 = weight_steps(fc1_ref, images, fc1_scratch, write_fc1)
    qkv = weight_steps(qkv_rows, images, qkv_scratch, write_qkv)
    sums = sum_steps(small, axes, sum_parts)

    def go(*steps):
        for step in steps:
            next(step, None)

    go(qkv_sum, patches, block, fc1)
    go(patches, block, patches, block, qkv_sum)
    go(patches)

    small[0:EARLY_ROWS] = early_ref[...]
    at = EARLY_ROWS
    for half in range(2):
        small[at : at + TABLE_ROWS // 2] = table_ref[:, half * 128 : (half + 1) * 128]
        at += TABLE_ROWS // 2
    place = lax.broadcasted_iota(jnp.int32, (BIAS_ROWS, 128), 0) - 2 * (col * 4 + row)
    small[at : at + BIAS_ROWS] = jnp.where(
        place == 0, bias_ref[0:1], jnp.where(place == 1, bias_ref[1:2], 0.0)
    )
    at += BIAS_ROWS
    lines = sums1.shape[1] // 128
    last = [sums1[i : i + 1, j * 128 : (j + 1) * 128] for i in range(2) for j in range(lines)]
    spare = jnp.zeros((LAST_ROWS - len(last), 128), F32)
    small[at : at + LAST_ROWS] = jnp.concatenate([*last, spare], 0)

    go(sums, block, fc1, qkv_sum, qkv)
    go(sums, patches, block, qkv, sums, fc1, sums, qkv)
    count = len(head_grads)
    for kind in range(3):
        rows = slice(kind * HEAD_DIM, (kind + 1) * HEAD_DIM)
        qkv_out[kind] = jnp.concatenate([values[rows] for values in head_grads], 0).T


def tail(
    qkv_grad, weight_qkv, normed1, first, middle_grad, gain, activated, weight_fc2, middle, bias_fc2, fc1, early, table, bias
):
    cols, n, tokens = qkv_grad.shape
    model = weight_qkv.shape[1]
    own, part = tokens // 4, model // 4
    axes = tuple((name, lax.axis_size(name)) for name in ("row", "batch", "col"))
    small_rows = EARLY_ROWS + TABLE_ROWS + BIAS_ROWS + LAST_ROWS
    vmem = pl.BlockSpec(memory_space=pltpu.VMEM)
    return pl.pallas_call(
        partial(tail_kernel, axes),
        in_specs=[vmem] * 15,
        out_specs=[vmem] * 5,
        out_shape=[
            jax.ShapeDtypeStruct((tokens, part), F32),
            jax.ShapeDtypeStruct((tokens, part), BF16),
            jax.ShapeDtypeStruct((3, part, 4 * HEAD_DIM), F32),
            jax.ShapeDtypeStruct((4 * fc1.shape[0], part), F32),
            jax.ShapeDtypeStruct((small_rows, 128), F32),
        ],
        scratch_shapes=[
            pltpu.VMEM((3, model), F32),
            pltpu.VMEM((n, model), BF16),
            pltpu.VMEM((3, n, model), BF16),
            pltpu.VMEM((3, n, model), BF16),
            pltpu.VMEM((n, model), F32),
            pltpu.SemaphoreType.DMA((2, 1, 4)),
            *mix_scratch(own, model, True),
            *mix_scratch(own, model, True),
            *weight_scratch(n, part),
            *weight_scratch(fc1.shape[0], part),
            *sum_scratch(small_rows, axes),
        ],
        compiler_params=pltpu.CompilerParams(
            collective_id=3, has_side_effects=True, vmem_limit_bytes=60 << 20
        ),
        name="tail",
    )(
        qkv_grad.reshape(cols * n, tokens), qkv_grad, weight_qkv, normed1, first, middle_grad, gain,
        activated, weight_fc2, middle, bias_fc2, fc1, early, table, bias,
    )


HIDDEN = 256
ROWS = 256


def hidden_kernel(x_ref, w1_ref, bias_ref, cot_ref, w2_ref, act_ref, grad_ref, bias_grad_ref):
    total = None
    for start in range(0, x_ref.shape[0], ROWS):
        rows = slice(start, start + ROWS)
        preact = mm_nt(x_ref[rows], w1_ref[...]) + bias_ref[...]
        act_grad = mm_nt(cot_ref[rows], w2_ref[...])
        below = 0.5 + 0.5 * lax.erf(preact * (0.5**0.5))
        density = jnp.exp(preact * preact * -0.5) * ((2 * math.pi) ** -0.5)
        act_ref[rows] = (preact * below).astype(BF16)
        grad = (act_grad * (below + preact * density)).astype(BF16)
        grad_ref[rows] = grad
        part = jnp.sum(grad.astype(F32), 0, keepdims=True)
        total = part if total is None else total + part
    bias_grad_ref[...] = total


def feed_forward(x, w1, bias, cotangent, w2):
    tokens, model = x.shape
    hidden = w1.shape[0]
    step = HIDDEN if hidden % HIDDEN == 0 else hidden
    whole = pl.BlockSpec((tokens, model), lambda i: (0, 0), pipeline_mode=pl.Buffered(1))
    weight = pl.BlockSpec((step, model), lambda i: (i, 0))
    vector = pl.BlockSpec((1, step), lambda i: (0, i))
    columns = pl.BlockSpec((tokens, step), lambda i: (0, i))
    return pl.pallas_call(
        hidden_kernel,
        grid=(hidden // step,),
        in_specs=[whole, weight, vector, whole, weight],
        out_specs=[columns, columns, vector],
        out_shape=[
            jax.ShapeDtypeStruct((tokens, hidden), BF16),
            jax.ShapeDtypeStruct((tokens, hidden), BF16),
            jax.ShapeDtypeStruct((1, hidden), F32),
        ],
        compiler_params=pltpu.CompilerParams(vmem_limit_bytes=40 << 20),
        cost_estimate=pl.CostEstimate(
            flops=4 * tokens * hidden * model,
            bytes_accessed=4 * (tokens + hidden) * model + 4 * tokens * hidden,
            transcendentals=2 * tokens * hidden,
        ),
        name="feed_forward",
    )(x, w1, bias, cotangent, w2)


def attention(qkv, table, proj):
    count, _, width = qkv.shape
    tokens = count * width
    vmem = pl.BlockSpec(memory_space=pltpu.VMEM)
    return pl.pallas_call(
        attend_kernel,
        in_specs=[vmem] * 3,
        out_specs=[vmem] * 5,
        out_shape=[
            jax.ShapeDtypeStruct((count, HEAD_DIM, width), BF16),
            jax.ShapeDtypeStruct(qkv.shape, BF16),
            jax.ShapeDtypeStruct((count, HEAD_DIM, width), F32),
            jax.ShapeDtypeStruct((count, 8, width), F32),
            jax.ShapeDtypeStruct((count, *proj.shape), BF16),
        ],
        scratch_shapes=[
            pltpu.VMEM((count, width, 256), BF16),
            pltpu.VMEM((count, 256, width), BF16),
            pltpu.VMEM((count, HEAD_DIM, width), F32),
            pltpu.VMEM((count, 8, width), F32),
            pltpu.VMEM((count, 8, width), F32),
            pltpu.VMEM((count, HEAD_DIM, width), BF16),
            pltpu.SemaphoreType.DMA((2, 3, 4)),
        ],
        compiler_params=pltpu.CompilerParams(
            collective_id=5, has_side_effects=True, vmem_limit_bytes=48 << 20
        ),
        cost_estimate=pl.CostEstimate(
            flops=2 * tokens * tokens * 512,
            bytes_accessed=6 * tokens * HEAD_DIM * 2,
            transcendentals=tokens * tokens,
        ),
        name="attend",
    )(qkv, table, proj)


def attention_back(qkv, table, grad, exact, stat, proj, fc2):
    count, _, width = qkv.shape
    tokens = count * width
    images, part = lax.axis_size("batch"), fc2.shape[1] // 4
    vmem = pl.BlockSpec(memory_space=pltpu.VMEM)
    return pl.pallas_call(
        partial(attend_back_kernel, images),
        in_specs=[vmem] * 8,
        out_specs=[vmem] * 5,
        out_shape=[
            jax.ShapeDtypeStruct((count, 3 * HEAD_DIM, width), BF16),
            jax.ShapeDtypeStruct(table.shape[::-1], F32),
            jax.ShapeDtypeStruct((2, 128), F32),
            jax.ShapeDtypeStruct((4, proj.shape[1], part), F32),
            jax.ShapeDtypeStruct((4, fc2.shape[0], part), F32),
        ],
        scratch_shapes=[
            pltpu.VMEM((384, 128), F32),
            pltpu.VMEM(proj.shape[1:], BF16),
            pltpu.VMEM(proj.shape, BF16),
            pltpu.VMEM((count, HEAD_DIM, width), BF16),
            pltpu.VMEM((count, width, 256), BF16),
            pltpu.VMEM((count, 256, width), BF16),
            pltpu.VMEM((count, width, 128), BF16),
            pltpu.VMEM((count, width, 128), F32),
            pltpu.VMEM((count, width, 128), F32),
            pltpu.VMEM((count, 256, width), F32),
            pltpu.VMEM((count, 256, width), BF16),
            pltpu.VMEM((count, 128, width), BF16),
            pltpu.VMEM((count, width, 128), BF16),
            pltpu.VMEM((count, width, 128), BF16),
            pltpu.VMEM((count, 3 * HEAD_DIM, width), BF16),
            pltpu.SemaphoreType.DMA((2, 4, 4)),
            *weight_scratch(fc2.shape[0], part),
            *weight_scratch(proj.shape[1], part),
        ],
        compiler_params=pltpu.CompilerParams(
            collective_id=4, has_side_effects=True, vmem_limit_bytes=60 << 20
        ),
        cost_estimate=pl.CostEstimate(
            flops=2 * tokens * tokens * 1280,
            bytes_accessed=12 * tokens * HEAD_DIM * 2,
            transcendentals=tokens * tokens,
        ),
        name="attend_back",
    )(qkv, table, table.T, grad, exact, stat, proj, fc2)


def moments(values):
    center = jnp.mean(values, -1, keepdims=True)
    spread = jnp.mean(values * values, -1, keepdims=True)
    return center, lax.rsqrt(spread - center * center + EPSILON)


def shards(
    patches,
    qkv_weight,
    qv_bias,
    proj_weight,
    proj_bias,
    norm1_gain,
    norm1_shift,
    norm2_gain,
    norm2_shift,
    fc1_weight,
    fc1_bias,
    fc2_weight,
    fc2_bias,
    height_table,
    width_table,
    out_grad,
):
    rows, cols = lax.axis_size("row"), lax.axis_size("col")
    row, col = lax.axis_index("row"), lax.axis_index("col")
    width = patches.shape[1]
    part = patches.shape[2]
    model = part * rows
    own = width // rows
    hidden = fc1_bias.shape[0] // rows
    head = HEAD_DIM

    def over_row(values):
        return lax.all_gather(values, "row", axis=1, tiled=True)

    def spread_rows(values):
        moved = lax.all_to_all(values, "row", 0, 0, tiled=True)
        return moved.transpose(1, 0, 2).reshape(values.shape[1], model)

    images = lax.axis_size("batch")

    residual = over_row(patches[0])
    cotangent = over_row(out_grad[0])
    vectors = lax.all_gather(
        jnp.stack([norm1_gain, norm1_shift, norm2_gain, norm2_shift, proj_bias, fc2_bias]),
        "row", axis=1, tiled=True,
    )
    gain1, shift1, gain2, shift2, bias_proj, bias_fc2 = [vectors[i] for i in range(6)]
    by_col = lax.all_gather(
        jnp.concatenate([qv_bias.reshape(-1), fc1_bias]), "col", axis=0, tiled=False
    )
    bias_qv = by_col[:, : 2 * rows * head].reshape(cols, 2, rows, head)
    bias_qv = lax.dynamic_index_in_dim(bias_qv, row, 2, keepdims=False)
    bias_fc1 = by_col[:, 2 * rows * head :].reshape(cols, rows, hidden)
    bias_fc1 = lax.dynamic_index_in_dim(bias_fc1, row, 1, keepdims=False)
    bias_fc1 = bias_fc1.reshape(cols * hidden)

    local_qkv = qkv_weight.reshape(part, 3, rows, head).transpose(2, 1, 3, 0)
    local_rest = jnp.concatenate(
        [
            proj_weight.reshape(rows, head, part),
            fc1_weight.T.reshape(rows, hidden, part),
            fc2_weight.reshape(rows, hidden, part),
        ],
        1,
    )
    spread_qkv = spread_rows(local_qkv.reshape(rows, 3 * head, part))
    local_rest, spread_qkv = lax.optimization_barrier((local_rest, spread_qkv))
    spread_rest = spread_rows(local_rest)
    weight_qkv = lax.all_gather(spread_qkv, "col", axis=0, tiled=True)

    zero_row = jnp.zeros((1, head), BF16)
    table = jnp.concatenate([height_table[::-1], zero_row, width_table[::-1], zero_row], 0)

    first = residual.astype(F32)
    center1, inv1 = moments(first)
    scaled1 = (first - center1) * inv1
    normed1 = (scaled1 * gain1 + shift1).astype(BF16)
    normed1, spread_rest = lax.optimization_barrier((normed1, spread_rest))
    bias = jnp.stack([bias_qv[:, 0], jnp.zeros_like(bias_qv[:, 0]), bias_qv[:, 1]], 1)
    qkv = mm_nt(weight_qkv, normed1)
    qkv = (qkv.reshape(cols, 3 * head, width) + bias.reshape(cols, 3 * head, 1)).astype(BF16)
    qkv, spread_rest = lax.optimization_barrier((qkv, spread_rest))
    weight_fc1 = lax.all_gather(spread_rest[head : head + hidden], "col", axis=0, tiled=True)
    weight_fc2 = lax.all_gather(spread_rest[head + hidden :], "col", axis=0, tiled=True)
    merged, qkv, exact, stat, weight_proj = attention(qkv, table, spread_rest[:head])
    weight_proj = weight_proj.reshape(cols * head, model)
    merged, weight_fc1 = lax.optimization_barrier((merged, weight_fc1))
    merged = merged.reshape(cols * head, width)

    def contract_rows(left, right):
        return lax.dot_general(left, right, (((0,), (0,)), ((), ())), preferred_element_type=F32)

    def sum_columns(values):
        return lax.psum_scatter(values, "col", scatter_dimension=0, tiled=False)

    def tokens_of_row(values):
        return lax.dynamic_slice_in_dim(values, row * own, own, 0)

    def sum_tokens(values):
        return lax.psum_scatter(values.astype(BF16), "row", scatter_dimension=0, tiled=True)

    own_shape = (own, model)
    vec2 = jnp.stack([gain2, shift2, bias_proj])
    normed2, middle = row_mix(
        forward_finish, "middle_and_norm2", 1, merged, weight_proj,
        (vec2, tokens_of_row(residual)), [jax.ShapeDtypeStruct(own_shape, F32)], True,
    )
    normed2 = normed2.reshape(width, model)
    activated, preact_grad, fc1_bias_part = feed_forward(
        normed2, weight_fc1, bias_fc1[None], cotangent, weight_fc2
    )
    fc2_grad = contract_rows(activated, cotangent).astype(BF16)
    fc2_grad, preact_grad = lax.optimization_barrier((fc2_grad, preact_grad))

    own_and_sums = [jax.ShapeDtypeStruct(own_shape, F32), jax.ShapeDtypeStruct((3, model), F32)]
    branch_grad, middle_grad, sums2 = row_mix(
        backward_finish, "middle_grad", 2, preact_grad, weight_fc1,
        (vec2, middle, tokens_of_row(cotangent)), own_and_sums, False,
    )
    branch_grad = branch_grad.reshape(width, model)

    merged_grad = mm_nt(weight_proj, branch_grad).astype(BF16).reshape(cols, head, width)
    merged_grad, activated, preact_grad, normed2, branch_grad = lax.optimization_barrier(
        (merged_grad, activated, preact_grad, normed2, branch_grad)
    )
    fc1_grad = contract_rows(preact_grad, normed2).astype(BF16)
    proj_grad = mm(merged, branch_grad).astype(BF16)
    fc2_grad = sum_columns(fc2_grad.reshape(cols, hidden, model))
    early = jnp.concatenate(
        [
            lax.dynamic_update_slice(jnp.zeros((rows, cols * hidden), F32), fc1_bias_part, (row, 0)).reshape(-1),
            lax.dynamic_update_slice(
                jnp.zeros((model,), F32), jnp.sum(out_grad[0], 0, dtype=F32), (row * part,)
            ),
            sums2.reshape(-1),
        ]
    ).reshape(-1, 128)
    merged_grad, fc1_grad, proj_grad, fc2_grad, early = lax.optimization_barrier(
        (merged_grad, fc1_grad, proj_grad, fc2_grad, early)
    )
    fc1_grad = sum_columns(fc1_grad.reshape(cols, hidden, model))
    qkv_grad, table_grad, bias_grad, proj_grad, fc2_grad = attention_back(
        qkv, table, merged_grad, exact, stat, proj_grad.reshape(cols, head, model), fc2_grad
    )
    input_grad, final, qkv_weight_grad, fc1_grad, small = tail(
        qkv_grad, weight_qkv, normed1, tokens_of_row(residual), middle_grad, gain1[None],
        activated, weight_fc2, middle, bias_fc2[None], fc1_grad, early, table_grad, bias_grad,
    )

    def sum_images(values):
        return values if images == 2 else lax.psum(values.astype(BF16), "batch").astype(F32)

    fc2_grad = sum_images(fc2_grad).reshape(rows * hidden, part)
    proj_grad = sum_images(proj_grad).reshape(rows * head, part)
    fc1_grad = sum_images(fc1_grad).T
    qkv_weight_grad = sum_images(qkv_weight_grad).transpose(1, 0, 2)

    lines = model // 128
    fc1_bias_grad = small[: 4 * lines].reshape(rows, cols, hidden)
    fc1_bias_grad = lax.dynamic_index_in_dim(fc1_bias_grad, col, 1, keepdims=False).reshape(rows * hidden)
    fc2_bias_grad = small[4 * lines : 5 * lines].reshape(-1)
    gain2_grad, shift2_grad, proj_bias_grad = small[5 * lines : 8 * lines].reshape(3, model)
    at = EARLY_ROWS
    table_grad = jnp.concatenate([small[at : at + TABLE_ROWS // 2], small[at + TABLE_ROWS // 2 : at + TABLE_ROWS]], 1)
    table_grad = table_grad.T
    at += TABLE_ROWS
    bias_total = small[at : at + BIAS_ROWS].reshape(cols, rows, 2, 128)
    bias_total = lax.dynamic_index_in_dim(bias_total, col, 0, keepdims=False)[:, :, :head]
    bias_total = bias_total.transpose(1, 0, 2).reshape(2, rows * head)
    at += BIAS_ROWS
    gain1_grad, shift1_grad = small[at : at + 2 * lines].reshape(2, model)

    def features_of_row(values):
        return lax.dynamic_slice_in_dim(values, row * part, part, 0)

    side = 2 * GRID - 1
    return (
        final[None],
        input_grad[None],
        qkv_weight_grad,
        bias_total,
        proj_grad,
        features_of_row(proj_bias_grad),
        features_of_row(gain1_grad),
        features_of_row(shift1_grad),
        features_of_row(gain2_grad),
        features_of_row(shift2_grad),
        fc1_grad,
        fc1_bias_grad,
        fc2_grad,
        features_of_row(fc2_bias_grad),
        table_grad[:side][::-1],
        table_grad[2 * GRID : 2 * GRID + side][::-1],
    )


def solution(mesh):
    in_specs = (
        P("batch", "col", "row"),
        P("row", None, "col"),
        P(None, "col"),
        P("col", "row"),
        P("row"),
        P("row"),
        P("row"),
        P("row"),
        P("row"),
        P("row", "col"),
        P("col"),
        P("col", "row"),
        P("row"),
        P(),
        P(),
        P("batch", "col", "row"),
    )
    out_specs = (
        P("batch", "col", "row"),
        P("batch", "col", "row"),
        P("row", None, "col"),
        P(None, "col"),
        P("col", "row"),
        P("row"),
        P("row"),
        P("row"),
        P("row"),
        P("row"),
        P("row", "col"),
        P("col"),
        P("col", "row"),
        P("row"),
        P(),
        P(),
    )
    return jax.shard_map(shards, mesh=mesh, in_specs=in_specs, out_specs=out_specs, check_vma=False)
```

```python
import math
from functools import partial

import jax
import jax.numpy as jnp
from jax import lax
from jax.experimental import pallas as pl
from jax.experimental.pallas import tpu as pltpu
from jax.sharding import PartitionSpec as P

D = 1280
HEAD_DIM = 80
GRID = 64
EPSILON = 1e-06

LINES = 4
QUERIES = LINES * GRID
KEYS = 512
LOG2E = math.log2(math.e)
SCALE = HEAD_DIM**-0.5
BF16 = jnp.bfloat16
F32 = jnp.float32
MESH = pl.DeviceIdType.MESH


def mm(left, right):
    return jnp.dot(left, right, preferred_element_type=F32)


def mm_nt(left, right):
    return lax.dot_general(left, right, (((1,), (1,)), ((), ())), preferred_element_type=F32)


def split(values, parts):
    terms = []
    for _ in range(parts):
        term = values.astype(BF16)
        terms.append(term)
        values = values - term.astype(F32)
    return terms


def skew(values, shift):
    n = values.shape[1]
    for bit, rows in ((32, 96), (16, 80), (8, 72)):
        take = jnp.broadcast_to(shift, (rows, n)) & bit
        values = jnp.where(take != 0, values[bit : bit + rows], values[:rows])
    for bit in (4, 2, 1):
        take = jnp.broadcast_to(shift, values.shape) & bit
        values = jnp.where(take != 0, pltpu.roll(values, values.shape[0] - bit, 0), values)
    return values[:GRID]


def unskew(values, shift):
    n = values.shape[1]
    values = jnp.concatenate([values, jnp.zeros((8, n), F32)], 0)
    for bit in (1, 2, 4):
        take = jnp.broadcast_to(shift, values.shape) & bit
        values = jnp.where(take != 0, pltpu.roll(values, bit, 0), values)
    for bit in (8, 16, 32):
        zeros = jnp.zeros((bit, n), F32)
        take = jnp.broadcast_to(shift, (values.shape[0] + bit, n)) & bit
        values = jnp.where(
            take != 0,
            jnp.concatenate([zeros, values], 0),
            jnp.concatenate([values, zeros], 0),
        )
    return values


def token_shifts(step):
    lane = lax.broadcasted_iota(jnp.int32, (1, QUERIES), 1)
    return (GRID - 1) - (step * LINES + lane // GRID), (GRID - 1) - lane % GRID


def query_columns(q, tab, step, tail):
    shift_rows, shift_cols = token_shifts(step)
    both = mm(tab, q)
    rel_rows = skew(both[: 2 * GRID], shift_rows)
    rel_cols = skew(both[2 * GRID :], shift_cols)
    rel = jnp.concatenate([rel_rows, rel_cols], 0) * (1.0 / SCALE)
    return jnp.concatenate([rel.astype(BF16), q, tail], 0)


def col_peer(step):
    me = lax.axis_index("col")
    odd, high = step % 2, step // 2
    return lax.rem(me + odd - 2 * odd * lax.rem(me, 2) + 2 * high, 4)


def col_barrier():
    barrier = pltpu.get_barrier_semaphore()
    for step in range(1, 4):
        pl.semaphore_signal(barrier, device_id={"col": col_peer(step)}, device_id_type=MESH)
    pl.semaphore_wait(barrier, 3)


def col_copy(source, target, sems, kind, step):
    return pltpu.make_async_remote_copy(
        src_ref=source,
        dst_ref=target,
        send_sem=sems.at[0, kind, step],
        recv_sem=sems.at[1, kind, step],
        device_id={"col": col_peer(step)},
        device_id_type=MESH,
    )


class Chain:
    def __init__(self, view, sems, on_block=None):
        self.view, self.sems, self.on_block = view, sems, on_block
        self.me = lax.axis_index("col")

    def copy(self, way, hop):
        block = self.me + (hop - 1) * (2 * way - 1)
        return pltpu.make_async_remote_copy(
            src_ref=self.view(block),
            dst_ref=self.view(block),
            send_sem=self.sems.at[0, way, hop - 1],
            recv_sem=self.sems.at[1, way, hop - 1],
            device_id={"col": lax.rem(self.me + 1 + 2 * way, 4)},
            device_id_type=MESH,
        )

    def sends(self, way, hop):
        if way:
            return jnp.logical_and(self.me > 0, self.me + hop - 1 < 4)
        return jnp.logical_and(self.me < 3, self.me - hop + 1 >= 0)

    def each(self, hop, act):
        for way in range(2):

            @pl.when(self.me + hop < 4 if way else self.me - hop >= 0)
            def _():
                act(self.me + hop * (2 * way - 1), way, hop)

    def start(self, way, hop):
        @pl.when(self.sends(way, hop))
        def _():
            self.copy(way, hop).start()

    def begin(self, hop=1):
        for way in range(2):
            self.start(way, hop)

    def hop(self, hop, last=3, tell=True):
        def arrived(block, way, hop):
            self.copy(way, hop).wait_recv()

        self.each(hop, arrived)
        if hop < last:
            for way in range(2):
                self.start(way, hop + 1)
        if self.on_block and tell:
            self.each(hop, self.on_block)

    def end(self, hops=(1, 2, 3)):
        for hop in hops:
            for way in range(2):

                @pl.when(self.sends(way, hop))
                def _():
                    self.copy(way, hop).wait_send()


def image_copy(source, target, sems, *place):
    return pltpu.make_async_remote_copy(
        src_ref=source,
        dst_ref=target,
        send_sem=sems.at[(0, *place)],
        recv_sem=sems.at[(1, *place)],
        device_id={"batch": 1 - lax.axis_index("batch")},
        device_id_type=MESH,
    )


def weight_chains(weight_all, images, chain_sems, swap_sems):
    image = lax.axis_index("batch")

    def swap_copy(block, way, hop):
        return image_copy(weight_all.at[image, block], weight_all.at[image, block], swap_sems, way, hop - 1)

    def swap(block, way, hop):
        swap_copy(block, way, hop).start()

    def swapped(block, way, hop):
        swap_copy(block, way, hop).wait()

    shared = images == 2
    chains = [
        Chain(lambda i, which=which: weight_all.at[which, i], chain_sems.at[order], swap if shared else None)
        for order, which in enumerate([image] if shared else [0, 1])
    ]
    return chains, swapped if shared else None


HALF = 128


def half_start(image):
    return pl.multiple_of(image * (3 * HEAD_DIM - HALF), 16)


def row_copy(source, target, sems, kind, order, peer):
    return pltpu.make_async_remote_copy(
        src_ref=source,
        dst_ref=target,
        send_sem=sems.at[0, kind, order],
        recv_sem=sems.at[1, kind, order],
        device_id={"row": peer},
        device_id_type=MESH,
    )


def beside(blocks):
    return jnp.concatenate([block.astype(F32) for block in blocks], 1)


def start_kernel(
    images, patches_ref, qkv_ref, rest_ref, vector_ref, column_ref,
    qkv_out, normed_out, first_out, weight_out, rest_out, vectors_out, columns_out,
    patches_all, qkv_parts, rest_parts, vector_parts, halves, sems, col_sems, chain_sems, swap_sems,
):
    row, col, image = lax.axis_index("row"), lax.axis_index("col"), lax.axis_index("batch")
    near, far, diag = row_peers()
    own = first_out.shape[0]
    shared = images == 2
    meet(
        ("row", (near, far, diag)),
        ("col", [col_peer(step) for step in range(1, 4)]),
        ("batch", image_peers(images) if shared else ()),
    )

    def to_row(source, parts, kind):
        copies = [row_copy(source(peer), parts.at[row], sems, kind, i, peer) for i, peer in enumerate((near, far, diag))]
        for copy in copies:
            copy.start()
        return copies

    qkv_copies = to_row(lambda peer: qkv_ref.at[peer], qkv_parts, 0)
    vector_copies = to_row(lambda peer: vector_ref, vector_parts, 1)
    to_near = row_copy(patches_ref, patches_all.at[row], sems, 2, 0, near)
    to_far = row_copy(patches_ref, patches_all.at[row], sems, 2, 1, far)
    to_near.start()
    column_copies = [col_copy(column_ref, columns_out.at[col], col_sems, 0, step) for step in range(1, 4)]
    for copy in column_copies:
        copy.start()
    qkv_parts[row] = qkv_ref[row]
    vector_parts[row] = vector_ref[...]
    patches_all[row] = patches_ref[...]
    columns_out[col] = column_ref[...]
    for copy in qkv_copies:
        copy.wait()
    to_far.start()
    weight = beside([qkv_parts[i] for i in range(4)]).astype(BF16)
    weight_out[col] = weight

    def swap_copy(block, way, hop):
        return image_copy(halves.at[image, block], halves.at[image, block], swap_sems, way, hop - 1)

    def swap(block, way, hop):
        swap_copy(block, way, hop).start()

    if shared:
        halves[0, col] = weight[:HALF]
        halves[1, col] = weight[3 * HEAD_DIM - HALF :]
        chain = Chain(lambda i: halves.at[image, i], chain_sems, swap)
    else:
        chain = Chain(lambda i: weight_out.at[i], chain_sems)

    def product(block, way=0, hop=0):
        if hop and shared:
            swap_copy(block, way, hop).wait()
            weight_out[block, 0 : 3 * HEAD_DIM - HALF] = halves[0, block, 0 : 3 * HEAD_DIM - HALF]
            weight_out[block, 3 * HEAD_DIM - HALF :] = halves[1, block]
        bias = jnp.concatenate([columns_out[block][:, 0:256]] * 16, 0).T[: 3 * HEAD_DIM, 0:1]
        qkv_out[block] = (mm_nt(weight_out[block], normed_out[...]) + bias).astype(BF16)

    chain.begin()
    for copy in vector_copies + column_copies:
        copy.wait()
    vectors_out[...] = beside([vector_parts[i] for i in range(4)])
    to_far.wait_recv()
    pass_on = row_copy(patches_all.at[far], patches_all.at[far], sems, 2, 2, near)
    pass_on.start()
    rest_copies = to_row(lambda peer: rest_ref.at[peer], rest_parts, 3)
    rest_parts[row] = rest_ref[row]
    chain.hop(1)
    to_near.wait_recv()
    pass_on.wait_recv()
    for start in range(0, normed_out.shape[0], own):
        rows = slice(start, start + own)
        scaled, _ = normal(beside([patches_all[i, rows] for i in range(4)]))
        normed_out[rows] = (scaled * vectors_out[0:1] + vectors_out[1:2]).astype(BF16)
    chain.hop(2)
    product(col)
    chain.each(1, product)
    chain.hop(3)
    chain.each(2, product)
    rows = pl.ds(pl.multiple_of(row * own, own), own)
    first_out[...] = beside([patches_all[i, rows] for i in range(4)]).astype(BF16)
    for copy in rest_copies:
        copy.wait()
    rest_out[...] = beside([rest_parts[i] for i in range(4)]).astype(BF16)
    chain.each(3, product)
    chain.end()
    for copy in (to_near, to_far, pass_on):
        copy.wait_send()


def start(patches, local_qkv, local_rest, vectors, columns):
    width, part = patches.shape
    n, model = local_qkv.shape[1], part * 4
    rest = local_rest.shape[1]
    vmem = pl.BlockSpec(memory_space=pltpu.VMEM)
    return pl.pallas_call(
        partial(start_kernel, lax.axis_size("batch")),
        in_specs=[vmem] * 5,
        out_specs=[vmem] * 7,
        out_shape=[
            jax.ShapeDtypeStruct((4, n, width), BF16),
            jax.ShapeDtypeStruct((width, model), BF16),
            jax.ShapeDtypeStruct((width // 4, model), BF16),
            jax.ShapeDtypeStruct((4, n, model), BF16),
            jax.ShapeDtypeStruct((rest, model), BF16),
            jax.ShapeDtypeStruct((vectors.shape[0], model), F32),
            jax.ShapeDtypeStruct((4, *columns.shape), F32),
        ],
        scratch_shapes=[
            pltpu.VMEM((4, width, part), BF16),
            pltpu.VMEM((4, n, part), BF16),
            pltpu.VMEM((4, rest, part), BF16),
            pltpu.VMEM((4, *vectors.shape), F32),
            pltpu.VMEM((2, 4, HALF, model), BF16),
            pltpu.SemaphoreType.DMA((2, 4, 3)),
            pltpu.SemaphoreType.DMA((2, 1, 4)),
            pltpu.SemaphoreType.DMA((2, 2, 3)),
            pltpu.SemaphoreType.DMA((2, 2, 3)),
        ],
        compiler_params=pltpu.CompilerParams(
            collective_id=7, has_side_effects=True, vmem_limit_bytes=48 << 20
        ),
        name="start",
    )(patches, local_qkv, local_rest, vectors, columns)


CHAIN_TURNS = (4, 9)


def attend_kernel(
    images, given_ref, tab_ref, proj_ref, cot_ref, weight_ref,
    merged_ref, qkv_ref, exact_ref, stat_ref, proj_all_ref, cot_out, weight_all,
    kaug, columns, acc, top, total, box, sems, cot_parts, cot_sems, local_sems, chain_sems, swap_sems,
):
    me = lax.axis_index("col")
    width = given_ref.shape[2]
    blocks = width // QUERIES
    row, image = lax.axis_index("row"), lax.axis_index("batch")
    near, far, diag = row_peers()
    shared = images == 2
    meet(
        ("row", (near, far)),
        ("col", [col_peer(step) for step in range(1, 4)]),
        ("batch", image_peers(images) if shared else ()),
    )

    chains, swapped = weight_chains(weight_all, images, chain_sems, swap_sems)
    keep = [pltpu.make_async_copy(weight_ref.at[i], weight_all.at[i, me], local_sems.at[i]) for i in range(2)]
    for copy in keep:
        copy.start()

    def part_copy(step):
        return col_copy(given_ref.at[col_peer(step)], qkv_ref.at[me], sems, 0, step)

    def merged_copy(step):
        return col_copy(box.at[col_peer(step)], merged_ref.at[me], sems, 1, step)

    def proj_copy(step):
        return col_copy(proj_ref, proj_all_ref.at[me], sems, 2, step)

    for step in (2, 1):
        part_copy(step).start()
    to_near = row_copy(cot_ref, cot_parts.at[row], cot_sems, 0, 0, near)
    to_far = row_copy(cot_ref, cot_parts.at[row], cot_sems, 0, 1, far)
    pass_on = row_copy(cot_parts.at[far], cot_parts.at[far], cot_sems, 0, 2, near)
    to_far.start()
    to_near.start()
    cot_parts[row] = cot_ref[...]
    qkv_ref[me] = given_ref[me]
    proj_all_ref[me] = proj_ref[...]

    pad = jnp.zeros((128 - HEAD_DIM, width), F32)
    token = lax.broadcasted_iota(jnp.int32, (width, 2 * GRID), 0)
    lane = lax.broadcasted_iota(jnp.int32, (width, 2 * GRID), 1)
    tail = jnp.zeros((128 - HEAD_DIM, QUERIES), BF16)
    factor = SCALE * LOG2E

    def prepare(part):
        at = token + part * width
        hot = jnp.where(jnp.where(lane < GRID, at // GRID, at % GRID + GRID) == lane, 1.0, 0.0)
        key = qkv_ref[part, HEAD_DIM : 2 * HEAD_DIM]
        kaug[part, :, 0:128] = hot.astype(BF16)
        kaug[part, :, 128:256] = jnp.concatenate([key.astype(F32), pad], 0).T.astype(BF16)
        for block in range(blocks):
            at = slice(block * QUERIES, (block + 1) * QUERIES)
            columns[part, :, at] = query_columns(
                qkv_ref[part, 0:HEAD_DIM, at], tab_ref[...], part * blocks + block, tail
            )
        acc[part] = jnp.zeros((HEAD_DIM, width), F32)
        top[part] = jnp.full((8, width), -1e30, F32)
        total[part] = jnp.zeros((8, width), F32)

    def finish(part):
        whole, best = total[part, 0:1], top[part, 0:1]
        result = acc[part] * (1.0 / whole)
        exact_ref[part] = result
        box[part] = result.astype(BF16)
        stat_ref[part] = jnp.broadcast_to(best + jnp.log2(whole) * (1.0 / factor), (8, width))

    def pair(turn, carry):
        newest = (turn + 15) // 16 + (turn + 12) // 16 + (turn + 7) // 16
        place = turn - newest * newest
        q_step = jnp.where(place < newest, place, newest)
        k_step = jnp.where(place < newest, newest, place - newest)
        q_part, k_part = col_peer(q_step), col_peer(k_step)

        @pl.when(jnp.logical_and(place == 0, newest > 0))
        def _():
            part_copy(newest).wait_recv()

        @pl.when(place == 0)
        def _():
            prepare(col_peer(newest))

        @pl.when(turn == CHAIN_TURNS[0])
        def _():
            part_copy(3).start()
            for chain in chains:
                chain.begin()

        @pl.when(turn == CHAIN_TURNS[1])
        def _():
            for chain in chains:
                chain.hop(1)
            for step in range(1, 4):
                proj_copy(step).start()
            to_far.wait_recv()
            pass_on.start()

        for block in range(blocks):
            at = slice(block * QUERIES, (block + 1) * QUERIES)
            best, whole, result = top[q_part, 0:1, at], total[q_part, 0:1, at], acc[q_part, :, at]
            for start in range(0, width, KEYS):
                keys = slice(start, start + KEYS)
                scores = mm(kaug[k_part, keys], columns[q_part, :, at])
                new_best = jnp.maximum(best, jnp.max(scores, 0, keepdims=True))
                weights = jnp.exp2((scores - new_best) * factor)
                keep = jnp.exp2((best - new_best) * factor)
                whole = whole * keep + jnp.sum(weights, 0, keepdims=True)
                value = qkv_ref[k_part, 2 * HEAD_DIM : 3 * HEAD_DIM, keys]
                result = result * keep + mm(value, weights.astype(BF16))
                best = new_best
            top[q_part, :, at] = jnp.broadcast_to(best, (8, QUERIES))
            total[q_part, :, at] = jnp.broadcast_to(whole, (8, QUERIES))
            acc[q_part, :, at] = result

        @pl.when(jnp.logical_and(turn >= 9, jnp.logical_or(place < 3, turn == 15)))
        def _():
            finish(q_part)

        @pl.when(jnp.logical_and(turn >= 9, jnp.logical_or(jnp.logical_and(turn > 9, place < 3), turn == 15)))
        def _():
            merged_copy(q_step).start()

        return carry

    for copy in keep:
        copy.wait()
    lax.fori_loop(0, 16, pair, 0)
    for chain in chains:
        chain.hop(2, 2, False)
    to_near.wait_recv()
    pass_on.wait_recv()
    for start in range(0, width, QUERIES):
        rows = slice(start, start + QUERIES)
        cot_out[rows] = beside([cot_parts[i, rows] for i in range(4)]).astype(BF16)
    merged_ref[me] = box[me]
    for chain in chains:
        chain.end((1, 2))
        if shared:
            chain.each(1, swapped)
    for copy in (to_near, to_far, pass_on):
        copy.wait_send()
    for step in range(1, 4):
        part_copy(step).wait_send()
        proj_copy(step).wait()
        merged_copy(step).wait()


GRADS, QUERY_OUT, KEY_OUT, PROJ_OUT = range(4)
KEY_ROWS = slice(HEAD_DIM, 3 * HEAD_DIM)


def attend_back_kernel(
    images, qkv_ref, tab_ref, tab_t_ref, given_ref, exact_ref, stat_ref, proj_ref, fc2_ref,
    activated_ref, weights_ref, middle_ref, bias_fc2_ref,
    out_ref, tab_grad_ref, bias_out, proj_out, fc2_out, block_out,
    held, held_sem, bias_ref, proj_rows, proj_box, grads, kaug, kaug_t, vaug, key_sum, value_sum, spread, columns,
    grad_columns, grad_rows, q_rows, box, sems, *weight_parts,
):
    me = lax.axis_index("col")
    width = qkv_ref.shape[2]
    blocks = width // QUERIES
    weight_copy = fetch(weights_ref, 1, (held, held_sem))
    weight_copy.start()
    meet(
        ("row", row_peers()),
        ("col", [col_peer(step) for step in range(1, 4)]),
        ("batch", image_peers(images) if images == 2 else ()),
    )

    def write_proj(place, values):
        proj_out[place] = values

    def write_fc2(place, values):
        fc2_out[place] = values

    fc2 = weight_steps(fc2_ref, images, weight_parts[:4], write_fc2)
    proj = weight_steps(proj_rows, images, weight_parts[4:8], write_proj)

    def finish_block(total, piece, rows):
        return middle_ref[rows] + (total + bias_fc2_ref[0:1])

    block = row_mix_steps(activated_ref, held, block_out, finish_block, False, True, weight_parts[8:])

    def grad_copy(step):
        return col_copy(given_ref.at[col_peer(step)], grads.at[me], sems, GRADS, step)

    def query_copy(step):
        at = col_peer(step)
        return col_copy(box.at[at, 0:HEAD_DIM], out_ref.at[me, 0:HEAD_DIM], sems, QUERY_OUT, step)

    def key_copy(step):
        at = col_peer(step)
        return col_copy(box.at[at, KEY_ROWS], out_ref.at[me, KEY_ROWS], sems, KEY_OUT, step)

    def proj_copy(step):
        return col_copy(proj_ref.at[col_peer(step)], proj_box.at[me], sems, PROJ_OUT, step)

    for step in range(1, 4):
        grad_copy(step).start()
    next(fc2)
    grads[me] = given_ref[me]
    proj_box[me] = proj_ref[me]

    tail_row = lax.broadcasted_iota(jnp.int32, (128 - HEAD_DIM, width), 0)
    pad = jnp.where(tail_row < 3, 1.0, 0.0)
    token = lax.broadcasted_iota(jnp.int32, (width, 2 * GRID), 0)
    lane = lax.broadcasted_iota(jnp.int32, (width, 2 * GRID), 1)

    def fill(part, carry):
        at = token + part * width
        hot = jnp.where(jnp.where(lane < GRID, at // GRID, at % GRID + GRID) == lane, 1.0, 0.0)
        key, value = qkv_ref[part, HEAD_DIM : 2 * HEAD_DIM], qkv_ref[part, 2 * HEAD_DIM : 3 * HEAD_DIM]
        kaug[part, :, 0:128] = hot.astype(BF16)
        kaug[part, :, 128:256] = jnp.concatenate([key.astype(F32), pad], 0).T.astype(BF16)
        vaug[part] = jnp.concatenate([value.astype(F32), pad], 0).T.astype(BF16)
        kaug_t[part, 0:128] = hot.T.astype(BF16)
        kaug_t[part, 128:208] = key
        kaug_t[part, 208:256] = jnp.zeros((48, width), BF16)
        return carry

    lax.fori_loop(0, 4, fill, 0)
    key_sum[...] = jnp.zeros_like(key_sum)
    value_sum[...] = jnp.zeros_like(value_sum)
    spread[...] = jnp.zeros_like(spread)
    tab_grad_ref[...] = jnp.zeros_like(tab_grad_ref)
    bias_ref[...] = jnp.zeros_like(bias_ref)

    block_row = lax.broadcasted_iota(jnp.int32, (128 - HEAD_DIM, QUERIES), 0)

    def tail(row):
        out = jnp.zeros((128 - HEAD_DIM, QUERIES), F32)
        for place, term in enumerate(split(row, 3)):
            out = jnp.where(block_row == place, term.astype(F32), out)
        return out.astype(BF16)

    zero_tail = jnp.zeros((128 - HEAD_DIM, QUERIES), F32)

    def prepare(part):
        for block in range(blocks):
            at = slice(block * QUERIES, (block + 1) * QUERIES)
            q, grad = qkv_ref[part, 0:HEAD_DIM, at], grads[part, :, at]
            inner = jnp.sum(grad.astype(F32) * exact_ref[part, :, at], 0, keepdims=True)
            columns[part, :, at] = query_columns(
                q, tab_ref[...], part * blocks + block, tail(-stat_ref[part, 0:1, at])
            )
            grad_columns[part, :, at] = jnp.concatenate([grad, tail(-inner)], 0)
            grad_rows[part, at] = jnp.concatenate([grad.astype(F32), zero_tail], 0).T.astype(BF16)
            q_rows[part, at] = jnp.concatenate([q.astype(F32), zero_tail], 0).T.astype(BF16)

    def add_bias(first, values):
        total = jnp.sum(values.astype(F32), 1, keepdims=True)
        bias_ref[first : first + values.shape[0]] += jnp.broadcast_to(total, (values.shape[0], 128))

    def finish_queries(part):
        for block in range(blocks):
            at = slice(block * QUERIES, (block + 1) * QUERIES)
            rows, cols = token_shifts(part * blocks + block)
            lifted = jnp.concatenate(
                [unskew(spread[part, 0:GRID, at], rows), unskew(spread[part, GRID : 2 * GRID, at], cols)], 0
            )
            high, low = split(lifted, 2)
            query_grad = spread[part, 128 : 128 + HEAD_DIM, at] * SCALE
            query_grad = query_grad + (mm(tab_t_ref[...], high) + mm(tab_t_ref[...], low))
            q = qkv_ref[part, 0:HEAD_DIM, at]
            tab_grad_ref[...] += mm_nt(q, high) + mm_nt(q, low)
            box[part, 0:HEAD_DIM, at] = query_grad.astype(BF16)
        add_bias(0, box[part, 0:HEAD_DIM])

    def finish_keys(part):
        key_grad = (key_sum[part] * SCALE).T[:HEAD_DIM].astype(BF16)
        value_grad = value_sum[part].T[:HEAD_DIM].astype(BF16)
        box[part, HEAD_DIM : 2 * HEAD_DIM] = key_grad
        box[part, 2 * HEAD_DIM : 3 * HEAD_DIM] = value_grad
        add_bias(HEAD_DIM, key_grad)
        add_bias(2 * HEAD_DIM, value_grad)

    def pair(turn, carry):
        later = jnp.maximum(turn - 4, 0)
        q_step = jnp.where(turn < 4, 0, 1 + later % 3)
        k_step = jnp.where(turn < 4, 3 - turn, 3 - later // 3)
        q_part, k_part = col_peer(q_step), col_peer(k_step)

        @pl.when(jnp.logical_and(turn >= 4, turn < 7))
        def _():
            grad_copy(q_step).wait_recv()

        @pl.when(jnp.logical_or(turn == 0, jnp.logical_and(turn >= 4, turn < 7)))
        def _():
            prepare(q_part)

        @pl.when(turn == 7)
        def _():
            for step in range(1, 4):
                proj_copy(step).start()

        for block in range(blocks):
            at = slice(block * QUERIES, (block + 1) * QUERIES)
            total = None
            for start in range(0, width, KEYS):
                keys = slice(start, start + KEYS)
                weights = jnp.exp2(mm(kaug[k_part, keys], columns[q_part, :, at]) * (SCALE * LOG2E))
                score_grad = (weights * mm(vaug[k_part, keys], grad_columns[q_part, :, at])).astype(BF16)
                value_sum[k_part, keys] += mm(weights.astype(BF16), grad_rows[q_part, at])
                key_sum[k_part, keys] += mm(score_grad, q_rows[q_part, at])
                result = mm(kaug_t[k_part, :, keys], score_grad)
                total = result if total is None else total + result
            spread[q_part, :, at] += total

        keys_done = jnp.logical_and(turn >= 4, q_step == 3)
        queries_done = jnp.logical_or(turn == 3, turn >= 13)

        @pl.when(keys_done)
        def _():
            finish_keys(k_part)

        @pl.when(jnp.logical_and(keys_done, k_step > 0))
        def _():
            key_copy(k_step).start()

        @pl.when(queries_done)
        def _():
            finish_queries(q_part)

        @pl.when(jnp.logical_and(queries_done, q_step > 0))
        def _():
            query_copy(q_step).start()

        return carry

    weight_copy.wait()
    next(block)
    next(block)
    lax.fori_loop(0, 4, pair, 0)
    next(block)
    next(block)
    lax.fori_loop(4, 8, pair, 0)
    next(fc2)
    next(block, None)
    lax.fori_loop(8, 12, pair, 0)
    for step in range(1, 4):
        proj_copy(step).wait()
    total = proj_box[0].astype(F32)
    for source in range(1, 4):
        total = total + proj_box[source].astype(F32)
    proj_rows[...] = total.astype(BF16)
    next(proj)
    next(fc2, None)
    lax.fori_loop(12, 16, pair, 0)
    next(proj)
    out_ref[me] = box[me]
    for step in range(1, 4):
        grad_copy(step).wait_send()
        query_copy(step).wait()
        key_copy(step).wait()
    next(proj, None)
    bias_out[0:1] = bias_ref[0:128].T[0:1]
    bias_out[1:2] = bias_ref[2 * HEAD_DIM : 2 * HEAD_DIM + 128].T[0:1]


MIX_SUBS = 2
TO_NEAR, PASS_ON, TO_FAR, OUT_NEAR, OUT_FAR, OUT_ON = range(6)


def normal(values):
    center, inv = moments(values)
    return (values - center) * inv, inv


def normal_back(grad, scaled, inv, gain):
    grad = grad * gain
    return inv * (
        grad
        - jnp.mean(grad, -1, keepdims=True)
        - scaled * jnp.mean(grad * scaled, -1, keepdims=True)
    )


def add_sums(sums_ref, piece, terms):
    for place, term in enumerate(terms):
        total = jnp.sum(term, 0, keepdims=True)
        if piece:
            total = total + sums_ref[place : place + 1]
        sums_ref[place : place + 1] = total


def forward_finish(total, piece, rows, vec_ref, first_ref, out_refs):
    middle = first_ref[rows].astype(F32) + (total + vec_ref[2:3])
    out_refs[0][rows] = middle
    scaled, _ = normal(middle)
    return (scaled * vec_ref[0:1] + vec_ref[1:2]).astype(BF16)


def backward_finish(total, piece, rows, vec_ref, first_ref, add_ref, out_refs):
    scaled, inv = normal(first_ref[rows].astype(F32))
    result = add_ref[rows].astype(F32) + normal_back(total, scaled, inv, vec_ref[0:1])
    branch = result.astype(BF16)
    out_refs[0][rows] = result
    add_sums(out_refs[1], piece, (total * scaled, total, branch.astype(F32)))
    return branch


def last_finish(total, piece, rows, vec_ref, first_ref, add_ref, out_refs):
    scaled, inv = normal(first_ref[rows].astype(F32))
    add_sums(out_refs[1], piece, (total * scaled, total))
    return add_ref[rows] + normal_back(total, scaled, inv, vec_ref[0:1])


def row_peers():
    me = lax.axis_index("row")
    near = me + 1 - 2 * lax.rem(me, 2)
    return near, lax.rem(me + 2, 4), lax.rem(near + 2, 4)


def meet(*groups):
    barrier = pltpu.get_barrier_semaphore()
    for axis, peers in groups:
        for peer in peers:
            pl.semaphore_signal(barrier, device_id={axis: peer}, device_id_type=MESH)
    pl.semaphore_wait(barrier, sum(len(peers) for _, peers in groups))


def row_mix_steps(left_ref, weight_ref, gathered, finish, left_t, to_features, scratch):
    far_keep, own_keep, out_box, in_box, sems, *more = scratch
    own = far_keep.shape[0]
    sub = own // MIX_SUBS
    me = lax.axis_index("row")
    near, far, diag = row_peers()
    started = []

    def send(source, target, kind, piece, peer):
        copy = pltpu.make_async_remote_copy(
            src_ref=source,
            dst_ref=target,
            send_sem=sems.at[0, kind, piece],
            recv_sem=sems.at[1, kind, piece],
            device_id={"row": peer},
            device_id_type=MESH,
        )
        copy.start()
        started.append(copy)
        return copy

    def product(owner, piece):
        at = pl.ds(pl.multiple_of(owner * own + piece * sub, sub), sub)
        if left_t:
            left = left_ref[:, at].astype(F32).T.astype(BF16)
        else:
            left = left_ref[at, :]
        return mm(left, weight_ref[...])

    pieces = [slice(piece * sub, (piece + 1) * sub) for piece in range(MIX_SUBS)]
    passed, direct, summed = [], [], []
    for piece, rows in enumerate(pieces):
        out_box[0, rows] = product(diag, piece).astype(BF16)
        passed.append(send(out_box.at[0, rows], in_box.at[0, rows], PASS_ON, piece, near))
        far_keep[rows] = product(far, piece)
    yield
    for piece, rows in enumerate(pieces):
        out_box[1, rows] = product(near, piece).astype(BF16)
        direct.append(send(out_box.at[1, rows], in_box.at[1, rows], TO_NEAR, piece, near))
        passed[piece].wait_recv()
        out_box[2, rows] = (far_keep[rows] + in_box[0, rows].astype(F32)).astype(BF16)
        summed.append(send(out_box.at[2, rows], in_box.at[2, rows], TO_FAR, piece, far))
    yield
    for piece, rows in enumerate(pieces):
        own_keep[rows] = product(me, piece)
    yield
    near_out, far_out, on_out = [], [], []
    for piece, rows in enumerate(pieces):
        direct[piece].wait_recv()
        summed[piece].wait_recv()
        total = own_keep[rows] + in_box[1, rows].astype(F32) + in_box[2, rows].astype(F32)
        result = finish(total, piece, rows)
        if to_features:
            boxes, arrived = more
            part = gathered.shape[1]
            for place in range(4):
                boxes[place, rows] = result[:, place * part : (place + 1) * part].astype(BF16)
            arrived[me, rows] = boxes[me, rows]
            for kind, peer, copies in (
                (OUT_NEAR, near, near_out), (OUT_FAR, far, far_out), (OUT_ON, diag, on_out)
            ):
                copies.append(send(boxes.at[peer, rows], arrived.at[me, rows], kind, piece, peer))
        else:
            gathered[me, rows] = result
            near_out.append(send(gathered.at[me, rows], gathered.at[me, rows], OUT_NEAR, piece, near))
            far_out.append(send(gathered.at[me, rows], gathered.at[me, rows], OUT_FAR, piece, far))
    yield
    for piece, rows in enumerate(pieces):
        far_out[piece].wait_recv()
        if not to_features:
            on_out.append(send(gathered.at[far, rows], gathered.at[far, rows], OUT_ON, piece, near))
    for copy in near_out + on_out:
        copy.wait_recv()
    if to_features:
        boxes, arrived = more
        for source in range(4):
            gathered[source * own : (source + 1) * own, :] = arrived[source].astype(gathered.dtype)
    for copy in started:
        copy.wait_send()


def mix_scratch(own, model, to_features):
    boxes = [pltpu.VMEM((4, own, model // 4), BF16)] * 2 if to_features else []
    return [
        pltpu.VMEM((own, model), F32),
        pltpu.VMEM((own, model), F32),
        pltpu.VMEM((3, own, model), BF16),
        pltpu.VMEM((3, own, model), BF16),
        pltpu.SemaphoreType.DMA((2, 6, MIX_SUBS)),
        *boxes,
    ]


def row_mix_kernel(finish, extra, outs, left_t, share, images, left_ref, weight_ref, *refs):
    extra_refs, refs = refs[:extra], refs[extra:]
    if images:
        refs = refs[1:]
    if share:
        share_ref, refs = refs[0], refs[1:]
    (gathered, *out_refs), scratch = refs[:outs], refs[outs:]
    if len(weight_ref.shape) == 3:
        *scratch, held, held_sem = scratch
        copy = fetch(weight_ref, 0, (held, held_sem))
        copy.start()
    near, far, _ = row_peers()
    meet(
        ("row", (near, far)),
        ("col", [col_peer(step) for step in range(1, 4)] if images else ()),
        ("batch", image_peers(2) if share or images == 2 else ()),
    )
    if images:
        *out_refs, weight_all = out_refs
        *scratch, chain_sems, pass_sems = scratch
        chains, swapped = weight_chains(weight_all, images, chain_sems, pass_sems)
        for chain in chains:
            chain.begin(3)
            if swapped:
                chain.each(2, chain.on_block)
    if share:
        *out_refs, share_out = out_refs
        *scratch, got, swap_sems = scratch
        image, half = lax.axis_index("batch"), got.shape[1]
        given = pl.ds(pl.multiple_of((1 - image) * half, 16), half)
        kept = pl.ds(pl.multiple_of(image * half, 16), half)
        swap = image_copy(share_ref.at[:, given], got, swap_sems, 0)
        swap.start()

    def last(total, piece, rows):
        return finish(total, piece, rows, *extra_refs, out_refs)

    if len(weight_ref.shape) == 3:
        copy.wait()
        weight_ref = held
    for _ in row_mix_steps(left_ref, weight_ref, gathered, last, left_t, False, scratch):
        pass
    if images:
        for chain in chains:
            chain.hop(3)
        for chain in chains:
            chain.end((3,))
            if swapped:
                chain.each(2, swapped)
                chain.each(3, swapped)
    if share:
        swap.wait()
        for place in range(4):
            both = share_ref[place, kept].astype(F32) + got[place].astype(F32)
            share_out[place] = both.astype(BF16)


def fetch(stack_ref, which, scratch):
    return pltpu.make_async_copy(stack_ref.at[which], scratch[0], scratch[1])


def fetch_scratch(stack):
    return [pltpu.VMEM(stack.shape[1:], stack.dtype), pltpu.SemaphoreType.DMA(())]


def row_mix(finish, name, number, left, weight, extra, out_shapes, left_t, share=None, passing=None):
    tokens = left.shape[1] if left_t else left.shape[0]
    model = weight.shape[-1]
    own = tokens // 4
    vmem = pl.BlockSpec(memory_space=pltpu.VMEM)
    shared = share is not None and lax.axis_size("batch") == 2
    specs, outs, scratch = [vmem] * (2 + len(extra)), [*out_shapes], mix_scratch(own, model, False)
    operands = (left, weight, *extra)
    if shared:
        cols, n, _ = share.shape
        specs.append(vmem)
        operands = (*operands, share)
        outs.append(jax.ShapeDtypeStruct((cols, n // 2, model), BF16))
        scratch += [pltpu.VMEM((cols, n // 2, model), BF16), pltpu.SemaphoreType.DMA((2, 1))]
    out_specs = [vmem] * (1 + len(outs))
    alias, images = {}, 0
    if passing is not None:
        images = lax.axis_size("batch")
        alias = {len(operands): len(out_specs)}
        operands = (*operands, passing)
        specs.append(pl.BlockSpec(memory_space=pl.ANY))
        out_specs.append(pl.BlockSpec(memory_space=pl.ANY))
        outs.append(jax.ShapeDtypeStruct(passing.shape, passing.dtype))
        scratch += [pltpu.SemaphoreType.DMA((2, 2, 2, 3)), pltpu.SemaphoreType.DMA((2, 2, 3))]
    if weight.ndim == 3:
        specs[1] = pl.BlockSpec(memory_space=pl.ANY)
        scratch += fetch_scratch(weight)
    results = pl.pallas_call(
        partial(row_mix_kernel, finish, len(extra), 1 + len(outs), left_t, shared, images),
        out_shape=[jax.ShapeDtypeStruct((4, own, model), BF16), *outs],
        in_specs=specs,
        out_specs=out_specs,
        input_output_aliases=alias,
        scratch_shapes=scratch,
        compiler_params=pltpu.CompilerParams(
            collective_id=number, has_side_effects=True, vmem_limit_bytes=48 << 20
        ),
        cost_estimate=pl.CostEstimate(
            flops=2 * tokens * model * model, bytes_accessed=16 * own * model, transcendentals=0
        ),
        name=name,
    )(*operands)
    return results if share is None or shared else (*results, share)


def weight_steps(values_ref, images, scratch, write, joined=False):
    boxes, arrived, other, sems = scratch
    me, part = lax.axis_index("row"), boxes.shape[2]
    for place in range(4):
        boxes[place] = values_ref[:, place * part : (place + 1) * part]
    arrived[me] = boxes[me]
    copies = []
    for order, peer in enumerate(row_peers()):
        copy = pltpu.make_async_remote_copy(
            src_ref=boxes.at[peer],
            dst_ref=arrived.at[me],
            send_sem=sems.at[0, order],
            recv_sem=sems.at[1, order],
            device_id={"row": peer},
            device_id_type=MESH,
        )
        copy.start()
        copies.append(copy)
    yield
    for copy in copies:
        copy.wait()
    if images == 2:
        swap = pltpu.make_async_remote_copy(
            src_ref=arrived,
            dst_ref=other,
            send_sem=sems.at[0, 3],
            recv_sem=sems.at[1, 3],
            device_id={"batch": 1 - lax.axis_index("batch")},
            device_id_type=MESH,
        )
        swap.start()
        yield
        swap.wait()
        for place in range(4):
            if joined:
                write(place, arrived[place].astype(F32), other[place].astype(F32))
            else:
                write(place, arrived[place].astype(F32) + other[place].astype(F32))
    else:
        yield
        for place in range(4):
            write(place, arrived[place].astype(F32))


def weight_scratch(n, part):
    return [*[pltpu.VMEM((4, n, part), BF16)] * 3, pltpu.SemaphoreType.DMA((2, 4))]


def image_peers(images):
    me = lax.axis_index("batch")
    return [lax.rem(me + step, images) for step in range(1, images)]


def sum_steps(total, axes, scratch):
    *slots, sends, recvs = scratch
    for order, (name, size) in enumerate(axes):
        me, slot = lax.axis_index(name), slots[order]
        slot[me] = total[...]
        copies = []
        for step in range(1, size):
            copy = pltpu.make_async_remote_copy(
                src_ref=total,
                dst_ref=slot.at[me],
                send_sem=sends.at[order, step],
                recv_sem=recvs.at[order, step],
                device_id={name: lax.rem(me + step, size)},
                device_id_type=MESH,
            )
            copy.start()
            copies.append(copy)
        yield
        for copy in copies:
            copy.wait()
        whole = slot[0]
        for source in range(1, size):
            whole = whole + slot[source]
        total[...] = whole


def sum_scratch(rows, axes):
    most = max(size for _, size in axes)
    return [
        *[pltpu.VMEM((size, rows, 128), F32) for _, size in axes],
        *[pltpu.SemaphoreType.DMA((len(axes), most))] * 2,
    ]


def column_steps(images, grad_ref, normed_ref, out, scratch):
    keep, give, got, box, arrived, sems, swap_sems = scratch
    image, rows = lax.axis_index("batch"), out.shape[0]
    shared = images == 2
    swaps = {}
    for step in (1, 2, 3, 0):
        keep[step] = mm(grad_ref[col_peer(step)], normed_ref[...])
        if shared:
            give[step] = keep[step, pl.ds(half_start(1 - image), rows)].astype(BF16)
            swaps[step] = image_copy(give.at[step], got.at[step], swap_sems, step)
            swaps[step].start()
    yield

    def total(step):
        if not shared:
            return keep[step]
        swaps[step].wait()
        return keep[step, pl.ds(half_start(image), rows)] + got[step].astype(F32)

    copies = []
    for step in range(1, 4):
        box[step - 1] = total(step).astype(BF16)
        copy = col_copy(box.at[step - 1], arrived.at[step - 1], sems, 0, step)
        copy.start()
        copies.append(copy)
    yield
    whole = total(0)
    for step, copy in enumerate(copies):
        copy.wait()
        whole = whole + arrived[step].astype(F32)
    out[...] = whole.astype(BF16)


def column_scratch(n, rows, model):
    return [
        pltpu.VMEM((4, n, model), F32),
        *[pltpu.VMEM((4, rows, model), BF16)] * 2,
        *[pltpu.VMEM((3, rows, model), BF16)] * 2,
        pltpu.SemaphoreType.DMA((2, 1, 4)),
        pltpu.SemaphoreType.DMA((2, 4)),
    ]


EARLY_ROWS, TABLE_ROWS, BIAS_ROWS, LAST_ROWS = 80, 160, 32, 24


def tail_kernel(
    axes,
    qkv_grad_ref, grads_ref, weight_qkv_ref, normed1_ref, first_ref, middle_grad_ref, gain_ref,
    fc1_ref, early_ref, table_ref, bias_ref, patches_out, qkv_out, fc1_out, small,
    *scratch,
):
    sums1, qkv_rows, *scratch = scratch
    col_scratch, scratch = scratch[:7], scratch[7:]
    mix, qkv_scratch, fc1_scratch, sum_parts = scratch[:7], scratch[7:11], scratch[11:15], scratch[15:]
    row, col = lax.axis_index("row"), lax.axis_index("col")
    images = dict(axes)["batch"]
    meet(
        ("row", row_peers()),
        ("col", [col_peer(step) for step in range(1, 4)]),
        ("batch", image_peers(images)),
    )

    def finish1(total, piece, rows):
        return last_finish(total, piece, rows, gain_ref, first_ref, middle_grad_ref, (None, sums1))

    image = lax.axis_index("batch")
    shared = images == 2

    def write_fc1(place, values, others=None):
        n = values.shape[0]
        if others is None:
            fc1_out[place * n : (place + 1) * n] = values
        else:
            fc1_out[pl.ds(pl.multiple_of((2 * place + image) * n, 8), n)] = values
            fc1_out[pl.ds(pl.multiple_of((2 * place + 1 - image) * n, 8), n)] = others

    head_grads = []

    def write_qkv(place, values, others=None):
        if others is not None:
            first, second = jnp.where(image == 0, values, others), jnp.where(image == 0, others, values)
            values = jnp.concatenate([first[: 3 * HEAD_DIM - HALF], second], 0)
        head_grads.append(values)

    qkv_sum = column_steps(images, grads_ref, normed1_ref, qkv_rows, col_scratch)
    patches = row_mix_steps(qkv_grad_ref, weight_qkv_ref, patches_out, finish1, True, True, mix)
    fc1 = weight_steps(fc1_ref, images, fc1_scratch, write_fc1, shared)
    qkv = weight_steps(qkv_rows, images, qkv_scratch, write_qkv, shared)
    sums = sum_steps(small, axes, sum_parts)

    def go(*steps):
        for step in steps:
            next(step, None)

    go(qkv_sum, patches, patches, patches, qkv_sum, patches)

    small[0:EARLY_ROWS] = early_ref[...]
    at = EARLY_ROWS
    for half in range(2):
        small[at : at + TABLE_ROWS // 2] = table_ref[:, half * 128 : (half + 1) * 128]
        at += TABLE_ROWS // 2
    place = lax.broadcasted_iota(jnp.int32, (BIAS_ROWS, 128), 0) - 2 * (col * 4 + row)
    small[at : at + BIAS_ROWS] = jnp.where(
        place == 0, bias_ref[0:1], jnp.where(place == 1, bias_ref[1:2], 0.0)
    )
    at += BIAS_ROWS
    lines = sums1.shape[1] // 128
    last = [sums1[i : i + 1, j * 128 : (j + 1) * 128] for i in range(2) for j in range(lines)]
    spare = jnp.zeros((LAST_ROWS - len(last), 128), F32)
    small[at : at + LAST_ROWS] = jnp.concatenate([*last, spare], 0)

    go(sums, fc1, qkv_sum, qkv, sums, patches, fc1, sums, qkv, fc1, sums, qkv)
    for kind in range(3):
        rows = slice(kind * HEAD_DIM, (kind + 1) * HEAD_DIM)
        qkv_out[kind] = jnp.concatenate([values[rows] for values in head_grads], 0).T


def tail(
    qkv_grad, weight_qkv, normed1, first, middle_grad, gain, fc1, early, table, bias
):
    cols, n, tokens = qkv_grad.shape
    model = weight_qkv.shape[1]
    own, part = tokens // 4, model // 4
    shared = lax.axis_size("batch") == 2
    rows = HALF if shared else n
    units = fc1.shape[0] * (2 if shared else 1)
    axes = tuple((name, lax.axis_size(name)) for name in ("row", "batch", "col"))
    small_rows = EARLY_ROWS + TABLE_ROWS + BIAS_ROWS + LAST_ROWS
    vmem = pl.BlockSpec(memory_space=pltpu.VMEM)
    return pl.pallas_call(
        partial(tail_kernel, axes),
        in_specs=[vmem] * 11,
        out_specs=[vmem] * 4,
        out_shape=[
            jax.ShapeDtypeStruct((tokens, part), F32),
            jax.ShapeDtypeStruct((3, part, 4 * HEAD_DIM), F32),
            jax.ShapeDtypeStruct((4 * units, part), F32),
            jax.ShapeDtypeStruct((small_rows, 128), F32),
        ],
        scratch_shapes=[
            pltpu.VMEM((3, model), F32),
            pltpu.VMEM((rows, model), BF16),
            *column_scratch(n, rows, model),
            *mix_scratch(own, model, True),
            *weight_scratch(rows, part),
            *weight_scratch(fc1.shape[0], part),
            *sum_scratch(small_rows, axes),
        ],
        compiler_params=pltpu.CompilerParams(
            collective_id=3, has_side_effects=True, vmem_limit_bytes=60 << 20
        ),
        name="tail",
    )(
        qkv_grad.reshape(cols * n, tokens), qkv_grad, weight_qkv, normed1, first, middle_grad, gain,
        fc1, early, table, bias,
    )


HIDDEN = 256
ROWS = 256


def hidden_kernel(x_ref, w1_ref, bias_ref, cot_ref, w2_ref, act_ref, grad_ref, bias_grad_ref):
    total = None
    for start in range(0, x_ref.shape[0], ROWS):
        rows = slice(start, start + ROWS)
        preact = mm_nt(x_ref[rows], w1_ref[...]) + bias_ref[...]
        act_grad = mm_nt(cot_ref[rows], w2_ref[...])
        below = 0.5 + 0.5 * lax.erf(preact * (0.5**0.5))
        density = jnp.exp(preact * preact * -0.5) * ((2 * math.pi) ** -0.5)
        act_ref[rows] = (preact * below).astype(BF16)
        grad = (act_grad * (below + preact * density)).astype(BF16)
        grad_ref[rows] = grad
        part = jnp.sum(grad.astype(F32), 0, keepdims=True)
        total = part if total is None else total + part
    bias_grad_ref[...] = total


def feed_forward(x, weights, bias, cotangent):
    tokens, model = x.shape
    hidden = weights.shape[1]
    step = HIDDEN if hidden % HIDDEN == 0 else hidden
    whole = pl.BlockSpec((tokens, model), lambda i: (0, 0), pipeline_mode=pl.Buffered(1))
    first, second = [pl.BlockSpec((None, step, model), lambda i, j=j: (j, i, 0)) for j in range(2)]
    vector = pl.BlockSpec((1, step), lambda i: (0, i))
    columns = pl.BlockSpec((tokens, step), lambda i: (0, i))
    return pl.pallas_call(
        hidden_kernel,
        grid=(hidden // step,),
        in_specs=[whole, first, vector, whole, second],
        out_specs=[columns, columns, vector],
        out_shape=[
            jax.ShapeDtypeStruct((tokens, hidden), BF16),
            jax.ShapeDtypeStruct((tokens, hidden), BF16),
            jax.ShapeDtypeStruct((1, hidden), F32),
        ],
        compiler_params=pltpu.CompilerParams(vmem_limit_bytes=40 << 20),
        cost_estimate=pl.CostEstimate(
            flops=4 * tokens * hidden * model,
            bytes_accessed=4 * (tokens + hidden) * model + 4 * tokens * hidden,
            transcendentals=2 * tokens * hidden,
        ),
        name="feed_forward",
    )(x, weights, bias, cotangent, weights)


def attention(qkv, table, proj, cotangent, weights):
    count, _, width = qkv.shape
    tokens = count * width
    images = lax.axis_size("batch")
    vmem = pl.BlockSpec(memory_space=pltpu.VMEM)
    return pl.pallas_call(
        partial(attend_kernel, images),
        in_specs=[*[vmem] * 4, pl.BlockSpec(memory_space=pl.ANY)],
        out_specs=[*[vmem] * 6, pl.BlockSpec(memory_space=pl.ANY)],
        out_shape=[
            jax.ShapeDtypeStruct((count, HEAD_DIM, width), BF16),
            jax.ShapeDtypeStruct(qkv.shape, BF16),
            jax.ShapeDtypeStruct((count, HEAD_DIM, width), F32),
            jax.ShapeDtypeStruct((count, 8, width), F32),
            jax.ShapeDtypeStruct((count, *proj.shape), BF16),
            jax.ShapeDtypeStruct((width, 4 * cotangent.shape[1]), BF16),
            jax.ShapeDtypeStruct((2, count, *weights.shape[1:]), BF16),
        ],
        scratch_shapes=[
            pltpu.VMEM((count, width, 256), BF16),
            pltpu.VMEM((count, 256, width), BF16),
            pltpu.VMEM((count, HEAD_DIM, width), F32),
            pltpu.VMEM((count, 8, width), F32),
            pltpu.VMEM((count, 8, width), F32),
            pltpu.VMEM((count, HEAD_DIM, width), BF16),
            pltpu.SemaphoreType.DMA((2, 3, 4)),
            pltpu.VMEM((4, *cotangent.shape), BF16),
            pltpu.SemaphoreType.DMA((2, 1, 3)),
            pltpu.SemaphoreType.DMA((2,)),
            pltpu.SemaphoreType.DMA((2, 2, 2, 3)),
            pltpu.SemaphoreType.DMA((2, 2, 3)),
        ],
        compiler_params=pltpu.CompilerParams(
            collective_id=5, has_side_effects=True, vmem_limit_bytes=48 << 20
        ),
        cost_estimate=pl.CostEstimate(
            flops=2 * tokens * tokens * 512,
            bytes_accessed=6 * tokens * HEAD_DIM * 2,
            transcendentals=tokens * tokens,
        ),
        name="attend",
    )(qkv, table, proj, cotangent, weights)


def attention_back(qkv, table, grad, exact, stat, proj, fc2, activated, weights, middle, bias_fc2):
    count, _, width = qkv.shape
    tokens = count * width
    images, part = lax.axis_size("batch"), fc2.shape[1] // 4
    vmem = pl.BlockSpec(memory_space=pltpu.VMEM)
    return pl.pallas_call(
        partial(attend_back_kernel, images),
        in_specs=[*[vmem] * 9, pl.BlockSpec(memory_space=pl.ANY), vmem, vmem],
        out_specs=[vmem] * 6,
        out_shape=[
            jax.ShapeDtypeStruct((count, 3 * HEAD_DIM, width), BF16),
            jax.ShapeDtypeStruct(table.shape[::-1], F32),
            jax.ShapeDtypeStruct((2, 128), F32),
            jax.ShapeDtypeStruct((4, proj.shape[1], part), F32),
            jax.ShapeDtypeStruct((4, fc2.shape[0], part), F32),
            jax.ShapeDtypeStruct((width, part), BF16),
        ],
        scratch_shapes=[
            *fetch_scratch(weights),
            pltpu.VMEM((384, 128), F32),
            pltpu.VMEM(proj.shape[1:], BF16),
            pltpu.VMEM(proj.shape, BF16),
            pltpu.VMEM((count, HEAD_DIM, width), BF16),
            pltpu.VMEM((count, width, 256), BF16),
            pltpu.VMEM((count, 256, width), BF16),
            pltpu.VMEM((count, width, 128), BF16),
            pltpu.VMEM((count, width, 128), F32),
            pltpu.VMEM((count, width, 128), F32),
            pltpu.VMEM((count, 256, width), F32),
            pltpu.VMEM((count, 256, width), BF16),
            pltpu.VMEM((count, 128, width), BF16),
            pltpu.VMEM((count, width, 128), BF16),
            pltpu.VMEM((count, width, 128), BF16),
            pltpu.VMEM((count, 3 * HEAD_DIM, width), BF16),
            pltpu.SemaphoreType.DMA((2, 4, 4)),
            *weight_scratch(fc2.shape[0], part),
            *weight_scratch(proj.shape[1], part),
            *mix_scratch(*middle.shape, True),
        ],
        compiler_params=pltpu.CompilerParams(
            collective_id=4, has_side_effects=True, vmem_limit_bytes=62 << 20
        ),
        cost_estimate=pl.CostEstimate(
            flops=2 * tokens * tokens * 1280,
            bytes_accessed=12 * tokens * HEAD_DIM * 2,
            transcendentals=tokens * tokens,
        ),
        name="attend_back",
    )(qkv, table, table.T, grad, exact, stat, proj, fc2, activated, weights, middle, bias_fc2)


def moments(values):
    center = jnp.mean(values, -1, keepdims=True)
    spread = jnp.mean(values * values, -1, keepdims=True)
    return center, lax.rsqrt(spread - center * center + EPSILON)


def shards(
    patches,
    qkv_weight,
    qv_bias,
    proj_weight,
    proj_bias,
    norm1_gain,
    norm1_shift,
    norm2_gain,
    norm2_shift,
    fc1_weight,
    fc1_bias,
    fc2_weight,
    fc2_bias,
    height_table,
    width_table,
    out_grad,
):
    rows, cols = lax.axis_size("row"), lax.axis_size("col")
    row, col = lax.axis_index("row"), lax.axis_index("col")
    width = patches.shape[1]
    part = patches.shape[2]
    model = part * rows
    own = width // rows
    hidden = fc1_bias.shape[0] // rows
    head = HEAD_DIM

    images = lax.axis_size("batch")

    vectors = jnp.stack([norm1_gain, norm1_shift, norm2_gain, norm2_shift, proj_bias, fc2_bias])
    vectors = jnp.concatenate([vectors, jnp.zeros((2, part), F32)], 0)
    bias_qkv = lax.dynamic_index_in_dim(qv_bias.reshape(2, rows, head), row, 1, keepdims=False)
    bias_qkv = jnp.stack([bias_qkv[0], jnp.zeros_like(bias_qkv[0]), bias_qkv[1]]).reshape(1, -1)
    bias_fc1 = lax.dynamic_index_in_dim(fc1_bias.reshape(rows, hidden), row, 0, keepdims=True)
    columns = jnp.concatenate([jnp.pad(bias_qkv, ((0, 0), (0, 256 - 3 * head))), bias_fc1], 1)
    columns = jnp.broadcast_to(columns, (8, 256 + hidden))
    local_qkv = qkv_weight.reshape(part, 3, rows, head).transpose(2, 1, 3, 0).reshape(rows, 3 * head, part)
    local_rest = jnp.concatenate(
        [
            proj_weight.reshape(rows, head, part),
            fc1_weight.T.reshape(rows, hidden, part),
            fc2_weight.reshape(rows, hidden, part),
        ],
        1,
    )
    qkv, normed1, first_own, weight_qkv, spread_rest, vectors, columns = start(
        patches[0], local_qkv, local_rest, vectors, columns
    )
    gain1, shift1, gain2, shift2, bias_proj, bias_fc2 = [vectors[i] for i in range(6)]
    weight_qkv = weight_qkv.reshape(cols * 3 * head, model)
    bias_fc1 = columns[:, 0, 256:].reshape(cols * hidden)

    zero_row = jnp.zeros((1, head), BF16)
    table = jnp.concatenate([height_table[::-1], zero_row, width_table[::-1], zero_row], 0)

    merged, qkv, exact, stat, weight_proj, cotangent, weights = attention(
        qkv, table, spread_rest[:head], out_grad[0], spread_rest[head:].reshape(2, hidden, model)
    )
    weight_proj = weight_proj.reshape(cols * head, model)
    merged = merged.reshape(cols * head, width)

    def contract_rows(left, right):
        return lax.dot_general(left, right, (((0,), (0,)), ((), ())), preferred_element_type=F32)

    def sum_columns(values):
        return lax.psum_scatter(values, "col", scatter_dimension=0, tiled=False)

    def tokens_of_row(values):
        return lax.dynamic_slice_in_dim(values, row * own, own, 0)

    own_shape = (own, model)
    vec2 = jnp.stack([gain2, shift2, bias_proj])
    normed2, middle, weights = row_mix(
        forward_finish, "middle_and_norm2", 1, merged, weight_proj,
        (vec2, first_own), [jax.ShapeDtypeStruct(own_shape, F32)], True, None, weights,
    )
    normed2 = normed2.reshape(width, model)
    weights = weights.reshape(2, cols * hidden, model)
    activated, preact_grad, fc1_bias_part = feed_forward(normed2, weights, bias_fc1[None], cotangent)
    fc2_grad = contract_rows(activated, cotangent).astype(BF16)
    fc2_grad, preact_grad = lax.optimization_barrier((fc2_grad, preact_grad))
    fc1_grad = contract_rows(preact_grad, normed2).astype(BF16).reshape(cols, hidden, model)

    own_and_sums = [jax.ShapeDtypeStruct(own_shape, F32), jax.ShapeDtypeStruct((3, model), F32)]
    branch_grad, middle_grad, sums2, fc1_grad = row_mix(
        backward_finish, "middle_grad", 2, preact_grad, weights,
        (vec2, middle, tokens_of_row(cotangent)), own_and_sums, False, fc1_grad,
    )
    branch_grad = branch_grad.reshape(width, model)

    merged_grad = mm_nt(weight_proj, branch_grad).astype(BF16).reshape(cols, head, width)
    proj_grad = mm(merged, branch_grad).astype(BF16)
    fc2_grad = sum_columns(fc2_grad.reshape(cols, hidden, model))
    early = jnp.concatenate(
        [
            lax.dynamic_update_slice(jnp.zeros((rows, cols * hidden), F32), fc1_bias_part, (row, 0)).reshape(-1),
            lax.dynamic_update_slice(
                jnp.zeros((model,), F32), jnp.sum(out_grad[0], 0, dtype=F32), (row * part,)
            ),
            sums2.reshape(-1),
        ]
    ).reshape(-1, 128)
    merged_grad, fc1_grad, proj_grad, fc2_grad, early = lax.optimization_barrier(
        (merged_grad, fc1_grad, proj_grad, fc2_grad, early)
    )
    fc1_grad = sum_columns(fc1_grad)
    qkv_grad, table_grad, bias_grad, proj_grad, fc2_grad, final = attention_back(
        qkv, table, merged_grad, exact, stat, proj_grad.reshape(cols, head, model), fc2_grad,
        activated, weights, middle, bias_fc2[None],
    )
    input_grad, qkv_weight_grad, fc1_grad, small = tail(
        qkv_grad, weight_qkv, normed1, first_own, middle_grad, gain1[None], fc1_grad, early, table_grad, bias_grad
    )

    def sum_images(values):
        return values if images == 2 else lax.psum(values.astype(BF16), "batch").astype(F32)

    fc2_grad = sum_images(fc2_grad).reshape(rows * hidden, part)
    proj_grad = sum_images(proj_grad).reshape(rows * head, part)
    fc1_grad = sum_images(fc1_grad).T
    qkv_weight_grad = sum_images(qkv_weight_grad).transpose(1, 0, 2)

    lines = model // 128
    fc1_bias_grad = small[: 4 * lines].reshape(rows, cols, hidden)
    fc1_bias_grad = lax.dynamic_index_in_dim(fc1_bias_grad, col, 1, keepdims=False).reshape(rows * hidden)
    fc2_bias_grad = small[4 * lines : 5 * lines].reshape(-1)
    gain2_grad, shift2_grad, proj_bias_grad = small[5 * lines : 8 * lines].reshape(3, model)
    at = EARLY_ROWS
    table_grad = jnp.concatenate([small[at : at + TABLE_ROWS // 2], small[at + TABLE_ROWS // 2 : at + TABLE_ROWS]], 1)
    table_grad = table_grad.T
    at += TABLE_ROWS
    bias_total = small[at : at + BIAS_ROWS].reshape(cols, rows, 2, 128)
    bias_total = lax.dynamic_index_in_dim(bias_total, col, 0, keepdims=False)[:, :, :head]
    bias_total = bias_total.transpose(1, 0, 2).reshape(2, rows * head)
    at += BIAS_ROWS
    gain1_grad, shift1_grad = small[at : at + 2 * lines].reshape(2, model)

    def features_of_row(values):
        return lax.dynamic_slice_in_dim(values, row * part, part, 0)

    side = 2 * GRID - 1
    return (
        final[None],
        input_grad[None],
        qkv_weight_grad,
        bias_total,
        proj_grad,
        features_of_row(proj_bias_grad),
        features_of_row(gain1_grad),
        features_of_row(shift1_grad),
        features_of_row(gain2_grad),
        features_of_row(shift2_grad),
        fc1_grad,
        fc1_bias_grad,
        fc2_grad,
        features_of_row(fc2_bias_grad),
        table_grad[:side][::-1],
        table_grad[2 * GRID : 2 * GRID + side][::-1],
    )


def solution(mesh):
    in_specs = (
        P("batch", "col", "row"),
        P("row", None, "col"),
        P(None, "col"),
        P("col", "row"),
        P("row"),
        P("row"),
        P("row"),
        P("row"),
        P("row"),
        P("row", "col"),
        P("col"),
        P("col", "row"),
        P("row"),
        P(),
        P(),
        P("batch", "col", "row"),
    )
    out_specs = (
        P("batch", "col", "row"),
        P("batch", "col", "row"),
        P("row", None, "col"),
        P(None, "col"),
        P("col", "row"),
        P("row"),
        P("row"),
        P("row"),
        P("row"),
        P("row"),
        P("row", "col"),
        P("col"),
        P("col", "row"),
        P("row"),
        P(),
        P(),
    )
    return jax.shard_map(shards, mesh=mesh, in_specs=in_specs, out_specs=out_specs, check_vma=False)
```

```python
import math
from functools import partial

import jax
import jax.numpy as jnp
from jax import lax
from jax.experimental import pallas as pl
from jax.experimental.pallas import tpu as pltpu
from jax.sharding import PartitionSpec as P

D = 1280
HEAD_DIM = 80
GRID = 64
EPSILON = 1e-06

LINES = 4
QUERIES = LINES * GRID
KEYS = 512
LOG2E = math.log2(math.e)
SCALE = HEAD_DIM**-0.5
BF16 = jnp.bfloat16
F32 = jnp.float32
MESH = pl.DeviceIdType.MESH


def mm(left, right):
    return jnp.dot(left, right, preferred_element_type=F32)


def mm_nt(left, right):
    return lax.dot_general(left, right, (((1,), (1,)), ((), ())), preferred_element_type=F32)


def split(values, parts):
    terms = []
    for _ in range(parts):
        term = values.astype(BF16)
        terms.append(term)
        values = values - term.astype(F32)
    return terms


def skew(values, shift):
    n = values.shape[1]
    for bit, rows in ((32, 96), (16, 80), (8, 72)):
        take = jnp.broadcast_to(shift, (rows, n)) & bit
        values = jnp.where(take != 0, values[bit : bit + rows], values[:rows])
    for bit in (4, 2, 1):
        take = jnp.broadcast_to(shift, values.shape) & bit
        values = jnp.where(take != 0, pltpu.roll(values, values.shape[0] - bit, 0), values)
    return values[:GRID]


def unskew(values, shift):
    n = values.shape[1]
    values = jnp.concatenate([values, jnp.zeros((8, n), F32)], 0)
    for bit in (1, 2, 4):
        take = jnp.broadcast_to(shift, values.shape) & bit
        values = jnp.where(take != 0, pltpu.roll(values, bit, 0), values)
    for bit in (8, 16, 32):
        zeros = jnp.zeros((bit, n), F32)
        take = jnp.broadcast_to(shift, (values.shape[0] + bit, n)) & bit
        values = jnp.where(
            take != 0,
            jnp.concatenate([zeros, values], 0),
            jnp.concatenate([values, zeros], 0),
        )
    return values


def token_shifts(step):
    lane = lax.broadcasted_iota(jnp.int32, (1, QUERIES), 1)
    return (GRID - 1) - (step * LINES + lane // GRID), (GRID - 1) - lane % GRID


def query_columns(q, tab, step, tail):
    shift_rows, shift_cols = token_shifts(step)
    both = mm(tab, q)
    rel_rows = skew(both[: 2 * GRID], shift_rows)
    rel_cols = skew(both[2 * GRID :], shift_cols)
    rel = jnp.concatenate([rel_rows, rel_cols], 0) * (1.0 / SCALE)
    return jnp.concatenate([rel.astype(BF16), q, tail], 0)


def col_peer(step):
    me = lax.axis_index("col")
    odd, high = step % 2, step // 2
    return lax.rem(me + odd - 2 * odd * lax.rem(me, 2) + 2 * high, 4)


def col_barrier():
    barrier = pltpu.get_barrier_semaphore()
    for step in range(1, 4):
        pl.semaphore_signal(barrier, device_id={"col": col_peer(step)}, device_id_type=MESH)
    pl.semaphore_wait(barrier, 3)


def col_copy(source, target, sems, kind, step):
    return pltpu.make_async_remote_copy(
        src_ref=source,
        dst_ref=target,
        send_sem=sems.at[0, kind, step],
        recv_sem=sems.at[1, kind, step],
        device_id={"col": col_peer(step)},
        device_id_type=MESH,
    )


class Chain:
    def __init__(self, view, sems, on_block=None):
        self.view, self.sems, self.on_block = view, sems, on_block
        self.me = lax.axis_index("col")

    def copy(self, way, hop):
        block = self.me + (hop - 1) * (2 * way - 1)
        return pltpu.make_async_remote_copy(
            src_ref=self.view(block),
            dst_ref=self.view(block),
            send_sem=self.sems.at[0, way, hop - 1],
            recv_sem=self.sems.at[1, way, hop - 1],
            device_id={"col": lax.rem(self.me + 1 + 2 * way, 4)},
            device_id_type=MESH,
        )

    def sends(self, way, hop):
        if way:
            return jnp.logical_and(self.me > 0, self.me + hop - 1 < 4)
        return jnp.logical_and(self.me < 3, self.me - hop + 1 >= 0)

    def each(self, hop, act):
        for way in range(2):

            @pl.when(self.me + hop < 4 if way else self.me - hop >= 0)
            def _():
                act(self.me + hop * (2 * way - 1), way, hop)

    def start(self, way, hop):
        @pl.when(self.sends(way, hop))
        def _():
            self.copy(way, hop).start()

    def begin(self, hop=1):
        for way in range(2):
            self.start(way, hop)

    def hop(self, hop, last=3, tell=True):
        def arrived(block, way, hop):
            self.copy(way, hop).wait_recv()

        self.each(hop, arrived)
        if hop < last:
            for way in range(2):
                self.start(way, hop + 1)
        if self.on_block and tell:
            self.each(hop, self.on_block)

    def end(self, hops=(1, 2, 3)):
        for hop in hops:
            for way in range(2):

                @pl.when(self.sends(way, hop))
                def _():
                    self.copy(way, hop).wait_send()


def image_copy(source, target, sems, *place):
    return pltpu.make_async_remote_copy(
        src_ref=source,
        dst_ref=target,
        send_sem=sems.at[(0, *place)],
        recv_sem=sems.at[(1, *place)],
        device_id={"batch": 1 - lax.axis_index("batch")},
        device_id_type=MESH,
    )


def weight_chains(weight_all, images, chain_sems, swap_sems):
    image = lax.axis_index("batch")

    def swap_copy(block, way, hop):
        return image_copy(weight_all.at[image, block], weight_all.at[image, block], swap_sems, way, hop - 1)

    def swap(block, way, hop):
        swap_copy(block, way, hop).start()

    def swapped(block, way, hop):
        swap_copy(block, way, hop).wait()

    shared = images == 2
    chains = [
        Chain(lambda i, which=which: weight_all.at[which, i], chain_sems.at[order], swap if shared else None)
        for order, which in enumerate([image] if shared else [0, 1])
    ]
    return chains, swapped if shared else None


HALF = 2 * HEAD_DIM


def half_start(image):
    return pl.multiple_of(image * (3 * HEAD_DIM - HALF_GRAD), 16)


HALF_GRAD = 128


def row_copy(source, target, sems, kind, order, peer):
    return pltpu.make_async_remote_copy(
        src_ref=source,
        dst_ref=target,
        send_sem=sems.at[0, kind, order],
        recv_sem=sems.at[1, kind, order],
        device_id={"row": peer},
        device_id_type=MESH,
    )


def beside(blocks):
    return jnp.concatenate([block.astype(F32) for block in blocks], 1)


def upright(blocks):
    return jnp.concatenate([block.astype(F32) for block in blocks], 0).T


def start_kernel(
    images, patches_ref, qkv_ref, proj_ref, fc1_ref, fc2_ref, vector_ref, column_ref,
    qkv_out, normed_out, first_out, weight_out, proj_out, rest_out, vectors_out, columns_out,
    patches_all, parts, rest_parts, vector_parts, halves, sems, col_sems, chain_sems, swap_sems,
):
    row, col, image = lax.axis_index("row"), lax.axis_index("col"), lax.axis_index("batch")
    near, far, diag = row_peers()
    own = first_out.shape[0]
    shared = images == 2
    meet(
        ("row", (near, far, diag)),
        ("col", [col_peer(step) for step in range(1, 4)]),
        ("batch", image_peers(images) if shared else ()),
    )

    def to_row(source, target, kind):
        copies = [row_copy(source(peer), target, sems, kind, i, peer) for i, peer in enumerate((near, far, diag))]
        for copy in copies:
            copy.start()
        return copies

    n, units = 3 * HEAD_DIM, fc1_ref.shape[1]
    weight_copies = to_row(lambda peer: qkv_ref.at[peer], parts.at[row, 0:n], 0)
    weight_copies += to_row(lambda peer: proj_ref.at[peer], parts.at[row, n : n + HEAD_DIM], 4)
    vector_copies = to_row(lambda peer: vector_ref, vector_parts.at[row], 1)
    to_near = row_copy(patches_ref, patches_all.at[row], sems, 2, 0, near)
    to_far = row_copy(patches_ref, patches_all.at[row], sems, 2, 1, far)
    to_near.start()
    column_copies = [col_copy(column_ref, columns_out.at[col], col_sems, 0, step) for step in range(1, 4)]
    for copy in column_copies:
        copy.start()
    parts[row, 0:n] = qkv_ref[row]
    parts[row, n : n + HEAD_DIM] = proj_ref[row]
    vector_parts[row] = vector_ref[...]
    patches_all[row] = patches_ref[...]
    columns_out[col] = column_ref[...]
    for copy in weight_copies:
        copy.wait()
    to_far.start()
    weight = beside([parts[i] for i in range(4)]).astype(BF16)

    def swap_copy(block, way, hop):
        return image_copy(halves.at[image, block], halves.at[image, block], swap_sems, way, hop - 1)

    def swap(block, way, hop):
        swap_copy(block, way, hop).start()

    halves[0, col] = weight[:HALF]
    halves[1, col] = weight[HALF:]
    orders = [image] if shared else [0, 1]
    chains = [
        Chain(lambda i, which=which: halves.at[which, i], chain_sems.at[order], swap if shared else None)
        for order, which in enumerate(orders)
    ]

    def product(block, way=0, hop=0):
        if hop and shared:
            swap_copy(block, way, hop).wait()
        weight_out[block, 0:HALF] = halves[0, block]
        weight_out[block, HALF:] = halves[1, block, 0 : n - HALF]
        proj_out[block] = halves[1, block, n - HALF :]
        bias = jnp.concatenate([columns_out[block][:, 0:256]] * 16, 0).T[:n, 0:1]
        qkv_out[block] = (mm_nt(weight_out[block], normed_out[...]) + bias).astype(BF16)

    for chain in chains:
        chain.begin()
    for copy in vector_copies + column_copies:
        copy.wait()
    vectors_out[...] = beside([vector_parts[i] for i in range(4)])
    to_far.wait_recv()
    pass_on = row_copy(patches_all.at[far], patches_all.at[far], sems, 2, 2, near)
    pass_on.start()
    rest_copies = to_row(lambda peer: fc1_ref.at[peer], rest_parts.at[row, 0:units], 3)
    rest_copies += to_row(lambda peer: fc2_ref.at[peer], rest_parts.at[row, units : 2 * units], 5)
    rest_parts[row, 0:units] = fc1_ref[row]
    rest_parts[row, units : 2 * units] = fc2_ref[row]
    for chain in chains:
        chain.hop(1)
    to_near.wait_recv()
    pass_on.wait_recv()
    for start in range(0, normed_out.shape[0], own):
        scaled, _ = normal(upright([patches_all[i, :, start : start + own] for i in range(4)]))
        normed_out[start : start + own] = (scaled * vectors_out[0:1] + vectors_out[1:2]).astype(BF16)
    for chain in chains:
        chain.hop(2)
    product(col)
    chains[0].each(1, product)
    for chain in chains:
        chain.hop(3)
    chains[0].each(2, product)
    mine = pl.ds(pl.multiple_of(row * own, own), own)
    first_out[...] = upright([patches_all[i, :, mine] for i in range(4)]).astype(BF16)
    for copy in rest_copies:
        copy.wait()
    rest_out[...] = beside([rest_parts[i] for i in range(4)]).astype(BF16)
    chains[0].each(3, product)
    for chain in chains:
        chain.end()
    for copy in (to_near, to_far, pass_on):
        copy.wait_send()


def start(patches, local_qkv, local_proj, local_fc1, local_fc2, vectors, columns):
    part, width = patches.shape
    n, model = local_qkv.shape[1], part * 4
    rest = local_fc1.shape[1] + local_fc2.shape[1]
    vmem = pl.BlockSpec(memory_space=pltpu.VMEM)
    return pl.pallas_call(
        partial(start_kernel, lax.axis_size("batch")),
        in_specs=[vmem] * 7,
        out_specs=[vmem] * 8,
        out_shape=[
            jax.ShapeDtypeStruct((4, n, width), BF16),
            jax.ShapeDtypeStruct((width, model), BF16),
            jax.ShapeDtypeStruct((width // 4, model), BF16),
            jax.ShapeDtypeStruct((4, n, model), BF16),
            jax.ShapeDtypeStruct((4, HEAD_DIM, model), BF16),
            jax.ShapeDtypeStruct((rest, model), BF16),
            jax.ShapeDtypeStruct((vectors.shape[0], model), F32),
            jax.ShapeDtypeStruct((4, *columns.shape), F32),
        ],
        scratch_shapes=[
            pltpu.VMEM((4, part, width), BF16),
            pltpu.VMEM((4, n + HEAD_DIM, part), BF16),
            pltpu.VMEM((4, rest, part), BF16),
            pltpu.VMEM((4, *vectors.shape), F32),
            pltpu.VMEM((2, 4, HALF, model), BF16),
            pltpu.SemaphoreType.DMA((2, 6, 3)),
            pltpu.SemaphoreType.DMA((2, 1, 4)),
            pltpu.SemaphoreType.DMA((2, 2, 2, 3)),
            pltpu.SemaphoreType.DMA((2, 2, 3)),
        ],
        compiler_params=pltpu.CompilerParams(
            collective_id=7, has_side_effects=True, vmem_limit_bytes=48 << 20
        ),
        name="start",
    )(patches, local_qkv, local_proj, local_fc1, local_fc2, vectors, columns)


CHAIN_TURNS = (6, 12)


def attend_kernel(
    images, given_ref, tab_ref, cot_ref, weight_ref,
    merged_ref, qkv_ref, exact_ref, stat_ref, cot_out, weight_all,
    kaug, columns, acc, top, total, box, sems, cot_parts, cot_sems, local_sems, chain_sems, swap_sems,
):
    me = lax.axis_index("col")
    width = given_ref.shape[2]
    blocks = width // QUERIES
    row, image = lax.axis_index("row"), lax.axis_index("batch")
    near, far, diag = row_peers()
    shared = images == 2
    meet(
        ("row", (near, far)),
        ("col", [col_peer(step) for step in range(1, 4)]),
        ("batch", image_peers(images) if shared else ()),
    )

    chains, swapped = weight_chains(weight_all, images, chain_sems, swap_sems)
    keep = [pltpu.make_async_copy(weight_ref.at[i], weight_all.at[i, me], local_sems.at[i]) for i in range(2)]
    for copy in keep:
        copy.start()

    def part_copy(step):
        return col_copy(given_ref.at[col_peer(step)], qkv_ref.at[me], sems, 0, step)

    def merged_copy(step):
        return col_copy(box.at[col_peer(step)], merged_ref.at[me], sems, 1, step)

    for step in (2, 1):
        part_copy(step).start()
    to_near = row_copy(cot_ref, cot_parts.at[row], cot_sems, 0, 0, near)
    to_far = row_copy(cot_ref, cot_parts.at[row], cot_sems, 0, 1, far)
    pass_on = row_copy(cot_parts.at[far], cot_parts.at[far], cot_sems, 0, 2, near)
    to_far.start()
    to_near.start()
    cot_parts[row] = cot_ref[...]
    qkv_ref[me] = given_ref[me]

    pad = jnp.zeros((128 - HEAD_DIM, width), F32)
    token = lax.broadcasted_iota(jnp.int32, (width, 2 * GRID), 0)
    lane = lax.broadcasted_iota(jnp.int32, (width, 2 * GRID), 1)
    tail = jnp.zeros((128 - HEAD_DIM, QUERIES), BF16)
    factor = SCALE * LOG2E

    def prepare(part):
        at = token + part * width
        hot = jnp.where(jnp.where(lane < GRID, at // GRID, at % GRID + GRID) == lane, 1.0, 0.0)
        key = qkv_ref[part, HEAD_DIM : 2 * HEAD_DIM]
        kaug[part, :, 0:128] = hot.astype(BF16)
        kaug[part, :, 128:256] = jnp.concatenate([key.astype(F32), pad], 0).T.astype(BF16)
        for block in range(blocks):
            at = slice(block * QUERIES, (block + 1) * QUERIES)
            columns[part, :, at] = query_columns(
                qkv_ref[part, 0:HEAD_DIM, at], tab_ref[...], part * blocks + block, tail
            )
        acc[part] = jnp.zeros((HEAD_DIM, width), F32)
        top[part] = jnp.full((8, width), -1e30, F32)
        total[part] = jnp.zeros((8, width), F32)

    def finish(part):
        whole, best = total[part, 0:1], top[part, 0:1]
        result = acc[part] * (1.0 / whole)
        exact_ref[part] = result
        box[part] = result.astype(BF16)
        stat_ref[part] = jnp.broadcast_to(best + jnp.log2(whole) * (1.0 / factor), (8, width))

    def pair(turn, carry):
        newest = (turn + 15) // 16 + (turn + 12) // 16 + (turn + 7) // 16
        place = turn - newest * newest
        q_step = jnp.where(place < newest, place, newest)
        k_step = jnp.where(place < newest, newest, place - newest)
        q_part, k_part = col_peer(q_step), col_peer(k_step)

        @pl.when(jnp.logical_and(place == 0, newest > 0))
        def _():
            part_copy(newest).wait_recv()

        @pl.when(place == 0)
        def _():
            prepare(col_peer(newest))

        @pl.when(turn == 1)
        def _():
            part_copy(3).start()

        @pl.when(turn == CHAIN_TURNS[0])
        def _():
            for chain in chains:
                chain.begin()

        @pl.when(turn == CHAIN_TURNS[1])
        def _():
            for chain in chains:
                chain.hop(1)
            to_far.wait_recv()
            pass_on.start()

        for block in range(blocks):
            at = slice(block * QUERIES, (block + 1) * QUERIES)
            best, whole, result = top[q_part, 0:1, at], total[q_part, 0:1, at], acc[q_part, :, at]
            for start in range(0, width, KEYS):
                keys = slice(start, start + KEYS)
                scores = mm(kaug[k_part, keys], columns[q_part, :, at])
                new_best = jnp.maximum(best, jnp.max(scores, 0, keepdims=True))
                weights = jnp.exp2((scores - new_best) * factor)
                keep = jnp.exp2((best - new_best) * factor)
                whole = whole * keep + jnp.sum(weights, 0, keepdims=True)
                value = qkv_ref[k_part, 2 * HEAD_DIM : 3 * HEAD_DIM, keys]
                result = result * keep + mm(value, weights.astype(BF16))
                best = new_best
            top[q_part, :, at] = jnp.broadcast_to(best, (8, QUERIES))
            total[q_part, :, at] = jnp.broadcast_to(whole, (8, QUERIES))
            acc[q_part, :, at] = result

        @pl.when(jnp.logical_and(turn >= 9, jnp.logical_or(place < 3, turn == 15)))
        def _():
            finish(q_part)

        @pl.when(jnp.logical_and(turn >= 9, jnp.logical_or(jnp.logical_and(turn > 9, place < 3), turn == 15)))
        def _():
            merged_copy(q_step).start()

        return carry

    for copy in keep:
        copy.wait()
    lax.fori_loop(0, 16, pair, 0)
    for chain in chains:
        chain.hop(2, 2, False)
    to_near.wait_recv()
    pass_on.wait_recv()
    for start in range(0, width, QUERIES):
        rows = slice(start, start + QUERIES)
        cot_out[rows] = upright([cot_parts[i, :, rows] for i in range(4)]).astype(BF16)
    merged_ref[me] = box[me]
    for chain in chains:
        chain.end((1, 2))
        if shared:
            chain.each(1, swapped)
    for copy in (to_near, to_far, pass_on):
        copy.wait_send()
    for step in range(1, 4):
        part_copy(step).wait_send()
        merged_copy(step).wait()


GRADS, QUERY_OUT, KEY_OUT = range(3)
KEY_ROWS = slice(HEAD_DIM, 3 * HEAD_DIM)


def attend_back_kernel(
    images, qkv_ref, tab_ref, tab_t_ref, given_ref, exact_ref, stat_ref, fc2_ref,
    activated_ref, weights_ref, middle_ref, bias_fc2_ref,
    out_ref, tab_grad_ref, bias_out, fc2_out, block_out,
    held, held_sem, bias_ref, grads, kaug, kaug_t, vaug, key_sum, value_sum, spread, columns,
    grad_columns, grad_rows, q_rows, box, sems, *weight_parts,
):
    me = lax.axis_index("col")
    width = qkv_ref.shape[2]
    blocks = width // QUERIES
    weight_copy = fetch(weights_ref, 1, (held, held_sem))
    weight_copy.start()
    meet(
        ("row", row_peers()),
        ("col", [col_peer(step) for step in range(1, 4)]),
        ("batch", image_peers(images) if images == 2 else ()),
    )

    def write_fc2(place, values):
        fc2_out[place] = values

    fc2 = weight_steps(fc2_ref, images, weight_parts[:4], write_fc2)

    def finish_block(total, piece, rows):
        return middle_ref[rows] + (total + bias_fc2_ref[0:1])

    block = row_mix_steps(activated_ref, held, block_out, finish_block, False, True, weight_parts[4:])

    def grad_copy(step):
        return col_copy(given_ref.at[col_peer(step)], grads.at[me], sems, GRADS, step)

    def query_copy(step):
        at = col_peer(step)
        return col_copy(box.at[at, 0:HEAD_DIM], out_ref.at[me, 0:HEAD_DIM], sems, QUERY_OUT, step)

    def key_copy(step):
        at = col_peer(step)
        return col_copy(box.at[at, KEY_ROWS], out_ref.at[me, KEY_ROWS], sems, KEY_OUT, step)

    for step in range(1, 4):
        grad_copy(step).start()
    next(fc2)
    grads[me] = given_ref[me]

    tail_row = lax.broadcasted_iota(jnp.int32, (128 - HEAD_DIM, width), 0)
    pad = jnp.where(tail_row < 3, 1.0, 0.0)
    token = lax.broadcasted_iota(jnp.int32, (width, 2 * GRID), 0)
    lane = lax.broadcasted_iota(jnp.int32, (width, 2 * GRID), 1)

    def fill(part, carry):
        at = token + part * width
        hot = jnp.where(jnp.where(lane < GRID, at // GRID, at % GRID + GRID) == lane, 1.0, 0.0)
        key, value = qkv_ref[part, HEAD_DIM : 2 * HEAD_DIM], qkv_ref[part, 2 * HEAD_DIM : 3 * HEAD_DIM]
        kaug[part, :, 0:128] = hot.astype(BF16)
        kaug[part, :, 128:256] = jnp.concatenate([key.astype(F32), pad], 0).T.astype(BF16)
        vaug[part] = jnp.concatenate([value.astype(F32), pad], 0).T.astype(BF16)
        kaug_t[part, 0:128] = hot.T.astype(BF16)
        kaug_t[part, 128:208] = key
        kaug_t[part, 208:256] = jnp.zeros((48, width), BF16)
        return carry

    lax.fori_loop(0, 4, fill, 0)
    key_sum[...] = jnp.zeros_like(key_sum)
    value_sum[...] = jnp.zeros_like(value_sum)
    spread[...] = jnp.zeros_like(spread)
    tab_grad_ref[...] = jnp.zeros_like(tab_grad_ref)
    bias_ref[...] = jnp.zeros_like(bias_ref)

    block_row = lax.broadcasted_iota(jnp.int32, (128 - HEAD_DIM, QUERIES), 0)

    def tail(row):
        out = jnp.zeros((128 - HEAD_DIM, QUERIES), F32)
        for place, term in enumerate(split(row, 3)):
            out = jnp.where(block_row == place, term.astype(F32), out)
        return out.astype(BF16)

    zero_tail = jnp.zeros((128 - HEAD_DIM, QUERIES), F32)

    def prepare(part):
        for block in range(blocks):
            at = slice(block * QUERIES, (block + 1) * QUERIES)
            q, grad = qkv_ref[part, 0:HEAD_DIM, at], grads[part, :, at]
            inner = jnp.sum(grad.astype(F32) * exact_ref[part, :, at], 0, keepdims=True)
            columns[part, :, at] = query_columns(
                q, tab_ref[...], part * blocks + block, tail(-stat_ref[part, 0:1, at])
            )
            grad_columns[part, :, at] = jnp.concatenate([grad, tail(-inner)], 0)
            grad_rows[part, at] = jnp.concatenate([grad.astype(F32), zero_tail], 0).T.astype(BF16)
            q_rows[part, at] = jnp.concatenate([q.astype(F32), zero_tail], 0).T.astype(BF16)

    def add_bias(first, values):
        total = jnp.sum(values.astype(F32), 1, keepdims=True)
        bias_ref[first : first + values.shape[0]] += jnp.broadcast_to(total, (values.shape[0], 128))

    def finish_queries(part):
        for block in range(blocks):
            at = slice(block * QUERIES, (block + 1) * QUERIES)
            rows, cols = token_shifts(part * blocks + block)
            lifted = jnp.concatenate(
                [unskew(spread[part, 0:GRID, at], rows), unskew(spread[part, GRID : 2 * GRID, at], cols)], 0
            )
            high, low = split(lifted, 2)
            query_grad = spread[part, 128 : 128 + HEAD_DIM, at] * SCALE
            query_grad = query_grad + (mm(tab_t_ref[...], high) + mm(tab_t_ref[...], low))
            q = qkv_ref[part, 0:HEAD_DIM, at]
            tab_grad_ref[...] += mm_nt(q, high) + mm_nt(q, low)
            box[part, 0:HEAD_DIM, at] = query_grad.astype(BF16)
        add_bias(0, box[part, 0:HEAD_DIM])

    def finish_keys(part):
        key_grad = (key_sum[part] * SCALE).T[:HEAD_DIM].astype(BF16)
        value_grad = value_sum[part].T[:HEAD_DIM].astype(BF16)
        box[part, HEAD_DIM : 2 * HEAD_DIM] = key_grad
        box[part, 2 * HEAD_DIM : 3 * HEAD_DIM] = value_grad
        add_bias(HEAD_DIM, key_grad)
        add_bias(2 * HEAD_DIM, value_grad)

    def pair(turn, carry):
        later = jnp.maximum(turn - 4, 0)
        q_step = jnp.where(turn < 4, 0, 1 + later % 3)
        k_step = jnp.where(turn < 4, 3 - turn, 3 - later // 3)
        q_part, k_part = col_peer(q_step), col_peer(k_step)

        @pl.when(jnp.logical_and(turn >= 4, turn < 7))
        def _():
            grad_copy(q_step).wait_recv()

        @pl.when(jnp.logical_or(turn == 0, jnp.logical_and(turn >= 4, turn < 7)))
        def _():
            prepare(q_part)

        for block in range(blocks):
            at = slice(block * QUERIES, (block + 1) * QUERIES)
            total = None
            for start in range(0, width, KEYS):
                keys = slice(start, start + KEYS)
                weights = jnp.exp2(mm(kaug[k_part, keys], columns[q_part, :, at]) * (SCALE * LOG2E))
                score_grad = (weights * mm(vaug[k_part, keys], grad_columns[q_part, :, at])).astype(BF16)
                value_sum[k_part, keys] += mm(weights.astype(BF16), grad_rows[q_part, at])
                key_sum[k_part, keys] += mm(score_grad, q_rows[q_part, at])
                result = mm(kaug_t[k_part, :, keys], score_grad)
                total = result if total is None else total + result
            spread[q_part, :, at] += total

        keys_done = jnp.logical_and(turn >= 4, q_step == 3)
        queries_done = jnp.logical_or(turn == 3, turn >= 13)

        @pl.when(keys_done)
        def _():
            finish_keys(k_part)

        @pl.when(jnp.logical_and(keys_done, k_step > 0))
        def _():
            key_copy(k_step).start()

        @pl.when(queries_done)
        def _():
            finish_queries(q_part)

        @pl.when(jnp.logical_and(queries_done, q_step > 0))
        def _():
            query_copy(q_step).start()

        return carry

    weight_copy.wait()
    next(block)
    next(block)
    lax.fori_loop(0, 4, pair, 0)
    next(block)
    next(block)
    lax.fori_loop(4, 8, pair, 0)
    next(fc2)
    next(block, None)
    lax.fori_loop(8, 16, pair, 0)
    next(fc2, None)
    out_ref[me] = box[me]
    for step in range(1, 4):
        grad_copy(step).wait_send()
        query_copy(step).wait()
        key_copy(step).wait()
    bias_out[0:1] = bias_ref[0:128].T[0:1]
    bias_out[1:2] = bias_ref[2 * HEAD_DIM : 2 * HEAD_DIM + 128].T[0:1]


MIX_SUBS = 2
TO_NEAR, PASS_ON, TO_FAR, OUT_NEAR, OUT_FAR, OUT_ON = range(6)


def normal(values):
    center, inv = moments(values)
    return (values - center) * inv, inv


def normal_back(grad, scaled, inv, gain):
    grad = grad * gain
    return inv * (
        grad
        - jnp.mean(grad, -1, keepdims=True)
        - scaled * jnp.mean(grad * scaled, -1, keepdims=True)
    )


def add_sums(sums_ref, piece, terms):
    for place, term in enumerate(terms):
        total = jnp.sum(term, 0, keepdims=True)
        if piece:
            total = total + sums_ref[place : place + 1]
        sums_ref[place : place + 1] = total


def forward_finish(total, piece, rows, vec_ref, first_ref, out_refs):
    middle = first_ref[rows].astype(F32) + (total + vec_ref[2:3])
    out_refs[0][rows] = middle
    scaled, _ = normal(middle)
    return (scaled * vec_ref[0:1] + vec_ref[1:2]).astype(BF16)


def backward_finish(total, piece, rows, vec_ref, first_ref, add_ref, out_refs):
    scaled, inv = normal(first_ref[rows].astype(F32))
    result = add_ref[rows].astype(F32) + normal_back(total, scaled, inv, vec_ref[0:1])
    branch = result.astype(BF16)
    out_refs[0][rows] = result
    add_sums(out_refs[1], piece, (total * scaled, total, branch.astype(F32)))
    return branch


def last_finish(total, piece, rows, vec_ref, first_ref, add_ref, out_refs):
    scaled, inv = normal(first_ref[rows].astype(F32))
    add_sums(out_refs[1], piece, (total * scaled, total))
    return add_ref[rows] + normal_back(total, scaled, inv, vec_ref[0:1])


def row_peers():
    me = lax.axis_index("row")
    near = me + 1 - 2 * lax.rem(me, 2)
    return near, lax.rem(me + 2, 4), lax.rem(near + 2, 4)


def meet(*groups):
    barrier = pltpu.get_barrier_semaphore()
    for axis, peers in groups:
        for peer in peers:
            pl.semaphore_signal(barrier, device_id={axis: peer}, device_id_type=MESH)
    pl.semaphore_wait(barrier, sum(len(peers) for _, peers in groups))


def row_mix_steps(left_ref, weight_ref, gathered, finish, left_t, to_features, scratch):
    far_keep, own_keep, out_box, in_box, sems, *more = scratch
    own = far_keep.shape[0]
    sub = own // MIX_SUBS
    me = lax.axis_index("row")
    near, far, diag = row_peers()
    started = []

    def send(source, target, kind, piece, peer):
        copy = pltpu.make_async_remote_copy(
            src_ref=source,
            dst_ref=target,
            send_sem=sems.at[0, kind, piece],
            recv_sem=sems.at[1, kind, piece],
            device_id={"row": peer},
            device_id_type=MESH,
        )
        copy.start()
        started.append(copy)
        return copy

    def product(owner, piece):
        at = pl.ds(pl.multiple_of(owner * own + piece * sub, sub), sub)
        if left_t:
            left = left_ref[:, at].astype(F32).T.astype(BF16)
        else:
            left = left_ref[at, :]
        return mm(left, weight_ref[...])

    pieces = [slice(piece * sub, (piece + 1) * sub) for piece in range(MIX_SUBS)]
    passed, direct, summed = [], [], []
    for piece, rows in enumerate(pieces):
        out_box[0, rows] = product(diag, piece).astype(BF16)
        passed.append(send(out_box.at[0, rows], in_box.at[0, rows], PASS_ON, piece, near))
        far_keep[rows] = product(far, piece)
    yield
    for piece, rows in enumerate(pieces):
        out_box[1, rows] = product(near, piece).astype(BF16)
        direct.append(send(out_box.at[1, rows], in_box.at[1, rows], TO_NEAR, piece, near))
        passed[piece].wait_recv()
        out_box[2, rows] = (far_keep[rows] + in_box[0, rows].astype(F32)).astype(BF16)
        summed.append(send(out_box.at[2, rows], in_box.at[2, rows], TO_FAR, piece, far))
    yield
    for piece, rows in enumerate(pieces):
        own_keep[rows] = product(me, piece)
    yield
    near_out, far_out, on_out = [], [], []
    for piece, rows in enumerate(pieces):
        direct[piece].wait_recv()
        summed[piece].wait_recv()
        total = own_keep[rows] + in_box[1, rows].astype(F32) + in_box[2, rows].astype(F32)
        result = finish(total, piece, rows)
        if to_features:
            boxes, arrived = more
            part = gathered.shape[0]
            for place in range(4):
                boxes[place, rows] = result[:, place * part : (place + 1) * part].astype(BF16)
            arrived[me, rows] = boxes[me, rows]
            for kind, peer, copies in (
                (OUT_NEAR, near, near_out), (OUT_FAR, far, far_out), (OUT_ON, diag, on_out)
            ):
                copies.append(send(boxes.at[peer, rows], arrived.at[me, rows], kind, piece, peer))
        else:
            gathered[me, rows] = result
            near_out.append(send(gathered.at[me, rows], gathered.at[me, rows], OUT_NEAR, piece, near))
            far_out.append(send(gathered.at[me, rows], gathered.at[me, rows], OUT_FAR, piece, far))
    yield
    for piece, rows in enumerate(pieces):
        far_out[piece].wait_recv()
        if not to_features:
            on_out.append(send(gathered.at[far, rows], gathered.at[far, rows], OUT_ON, piece, near))
    for copy in near_out + on_out:
        copy.wait_recv()
    if to_features:
        boxes, arrived = more
        for source in range(4):
            gathered[:, source * own : (source + 1) * own] = arrived[source].astype(F32).T.astype(gathered.dtype)
    for copy in started:
        copy.wait_send()


def mix_scratch(own, model, to_features):
    boxes = [pltpu.VMEM((4, own, model // 4), BF16)] * 2 if to_features else []
    return [
        pltpu.VMEM((own, model), F32),
        pltpu.VMEM((own, model), F32),
        pltpu.VMEM((3, own, model), BF16),
        pltpu.VMEM((3, own, model), BF16),
        pltpu.SemaphoreType.DMA((2, 6, MIX_SUBS)),
        *boxes,
    ]


def row_mix_kernel(finish, extra, outs, left_t, share, images, left_ref, weight_ref, *refs):
    extra_refs, refs = refs[:extra], refs[extra:]
    if images:
        refs = refs[1:]
    if share:
        share_ref, refs = refs[0], refs[1:]
    (gathered, *out_refs), scratch = refs[:outs], refs[outs:]
    if len(weight_ref.shape) == 3:
        *scratch, held, held_sem = scratch
        copy = fetch(weight_ref, 0, (held, held_sem))
        copy.start()
    near, far, _ = row_peers()
    meet(
        ("row", (near, far)),
        ("col", [col_peer(step) for step in range(1, 4)] if images else ()),
        ("batch", image_peers(2) if share or images == 2 else ()),
    )
    if images:
        *out_refs, weight_all = out_refs
        *scratch, chain_sems, pass_sems = scratch
        chains, swapped = weight_chains(weight_all, images, chain_sems, pass_sems)
        for chain in chains:
            chain.begin(3)
            if swapped:
                chain.each(2, chain.on_block)
    if share:
        *out_refs, share_out = out_refs
        *scratch, got, swap_sems = scratch
        image, half = lax.axis_index("batch"), got.shape[1]
        given = pl.ds(pl.multiple_of((1 - image) * half, 16), half)
        kept = pl.ds(pl.multiple_of(image * half, 16), half)
        swap = image_copy(share_ref.at[:, given], got, swap_sems, 0)
        swap.start()

    def last(total, piece, rows):
        return finish(total, piece, rows, *extra_refs, out_refs)

    if len(weight_ref.shape) == 3:
        copy.wait()
        weight_ref = held
    for stage, _ in enumerate(row_mix_steps(left_ref, weight_ref, gathered, last, left_t, False, scratch)):
        if images and stage == 3:
            for chain in chains:
                chain.hop(3)
    if images:
        for chain in chains:
            chain.end((3,))
            if swapped:
                chain.each(2, swapped)
                chain.each(3, swapped)
    if share:
        swap.wait()
        for place in range(4):
            both = share_ref[place, kept].astype(F32) + got[place].astype(F32)
            share_out[place] = both.astype(BF16)


def fetch(stack_ref, which, scratch):
    return pltpu.make_async_copy(stack_ref.at[which], scratch[0], scratch[1])


def fetch_scratch(stack):
    return [pltpu.VMEM(stack.shape[1:], stack.dtype), pltpu.SemaphoreType.DMA(())]


def row_mix(finish, name, number, left, weight, extra, out_shapes, left_t, share=None, passing=None):
    tokens = left.shape[1] if left_t else left.shape[0]
    model = weight.shape[-1]
    own = tokens // 4
    vmem = pl.BlockSpec(memory_space=pltpu.VMEM)
    shared = share is not None and lax.axis_size("batch") == 2
    specs, outs, scratch = [vmem] * (2 + len(extra)), [*out_shapes], mix_scratch(own, model, False)
    operands = (left, weight, *extra)
    if shared:
        cols, n, _ = share.shape
        specs.append(vmem)
        operands = (*operands, share)
        outs.append(jax.ShapeDtypeStruct((cols, n // 2, model), BF16))
        scratch += [pltpu.VMEM((cols, n // 2, model), BF16), pltpu.SemaphoreType.DMA((2, 1))]
    out_specs = [vmem] * (1 + len(outs))
    alias, images = {}, 0
    if passing is not None:
        images = lax.axis_size("batch")
        alias = {len(operands): len(out_specs)}
        operands = (*operands, passing)
        specs.append(pl.BlockSpec(memory_space=pl.ANY))
        out_specs.append(pl.BlockSpec(memory_space=pl.ANY))
        outs.append(jax.ShapeDtypeStruct(passing.shape, passing.dtype))
        scratch += [pltpu.SemaphoreType.DMA((2, 2, 2, 3)), pltpu.SemaphoreType.DMA((2, 2, 3))]
    if weight.ndim == 3:
        specs[1] = pl.BlockSpec(memory_space=pl.ANY)
        scratch += fetch_scratch(weight)
    results = pl.pallas_call(
        partial(row_mix_kernel, finish, len(extra), 1 + len(outs), left_t, shared, images),
        out_shape=[jax.ShapeDtypeStruct((4, own, model), BF16), *outs],
        in_specs=specs,
        out_specs=out_specs,
        input_output_aliases=alias,
        scratch_shapes=scratch,
        compiler_params=pltpu.CompilerParams(
            collective_id=number, has_side_effects=True, vmem_limit_bytes=48 << 20
        ),
        cost_estimate=pl.CostEstimate(
            flops=2 * tokens * model * model, bytes_accessed=16 * own * model, transcendentals=0
        ),
        name=name,
    )(*operands)
    return results if share is None or shared else (*results, share)


def weight_steps(values_ref, images, scratch, write, joined=False):
    boxes, arrived, other, sems = scratch
    me, part = lax.axis_index("row"), boxes.shape[2]
    for place in range(4):
        boxes[place] = values_ref[:, place * part : (place + 1) * part]
    arrived[me] = boxes[me]
    copies = []
    for order, peer in enumerate(row_peers()):
        copy = pltpu.make_async_remote_copy(
            src_ref=boxes.at[peer],
            dst_ref=arrived.at[me],
            send_sem=sems.at[0, order],
            recv_sem=sems.at[1, order],
            device_id={"row": peer},
            device_id_type=MESH,
        )
        copy.start()
        copies.append(copy)
    yield
    for copy in copies:
        copy.wait()
    if images == 2:
        swap = pltpu.make_async_remote_copy(
            src_ref=arrived,
            dst_ref=other,
            send_sem=sems.at[0, 3],
            recv_sem=sems.at[1, 3],
            device_id={"batch": 1 - lax.axis_index("batch")},
            device_id_type=MESH,
        )
        swap.start()
        yield
        swap.wait()
        for place in range(4):
            if joined:
                write(place, arrived[place].astype(F32), other[place].astype(F32))
            else:
                write(place, arrived[place].astype(F32) + other[place].astype(F32))
    else:
        yield
        for place in range(4):
            write(place, arrived[place].astype(F32))


def weight_scratch(n, part):
    return [*[pltpu.VMEM((4, n, part), BF16)] * 3, pltpu.SemaphoreType.DMA((2, 4))]


def image_peers(images):
    me = lax.axis_index("batch")
    return [lax.rem(me + step, images) for step in range(1, images)]


def sum_steps(total, axes, scratch):
    *slots, sends, recvs = scratch
    for order, (name, size) in enumerate(axes):
        me, slot = lax.axis_index(name), slots[order]
        slot[me] = total[...]
        copies = []
        for step in range(1, size):
            copy = pltpu.make_async_remote_copy(
                src_ref=total,
                dst_ref=slot.at[me],
                send_sem=sends.at[order, step],
                recv_sem=recvs.at[order, step],
                device_id={name: lax.rem(me + step, size)},
                device_id_type=MESH,
            )
            copy.start()
            copies.append(copy)
        yield
        for copy in copies:
            copy.wait()
        whole = slot[0]
        for source in range(1, size):
            whole = whole + slot[source]
        total[...] = whole


def sum_scratch(rows, axes):
    most = max(size for _, size in axes)
    return [
        *[pltpu.VMEM((size, rows, 128), F32) for _, size in axes],
        *[pltpu.SemaphoreType.DMA((len(axes), most))] * 2,
    ]


def column_steps(images, grad_ref, normed_ref, out, scratch):
    keep, give, got, box, arrived, sems, swap_sems = scratch
    image, rows = lax.axis_index("batch"), out.shape[0]
    shared = images == 2
    swaps = {}
    for step in (1, 2, 3, 0):
        keep[step] = mm(grad_ref[col_peer(step)], normed_ref[...])
        if shared:
            give[step] = keep[step, pl.ds(half_start(1 - image), rows)].astype(BF16)
            swaps[step] = image_copy(give.at[step], got.at[step], swap_sems, step)
            swaps[step].start()
    yield

    def total(step):
        if not shared:
            return keep[step]
        swaps[step].wait()
        return keep[step, pl.ds(half_start(image), rows)] + got[step].astype(F32)

    copies = []
    for step in range(1, 4):
        box[step - 1] = total(step).astype(BF16)
        copy = col_copy(box.at[step - 1], arrived.at[step - 1], sems, 0, step)
        copy.start()
        copies.append(copy)
    yield
    whole = total(0)
    for step, copy in enumerate(copies):
        copy.wait()
        whole = whole + arrived[step].astype(F32)
    out[...] = whole.astype(BF16)


def column_scratch(n, rows, model):
    return [
        pltpu.VMEM((4, n, model), F32),
        *[pltpu.VMEM((4, rows, model), BF16)] * 2,
        *[pltpu.VMEM((3, rows, model), BF16)] * 2,
        pltpu.SemaphoreType.DMA((2, 1, 4)),
        pltpu.SemaphoreType.DMA((2, 4)),
    ]


EARLY_ROWS, TABLE_ROWS, BIAS_ROWS, LAST_ROWS = 80, 160, 32, 24


def tail_kernel(
    axes,
    qkv_grad_ref, grads_ref, weight_qkv_ref, normed1_ref, first_ref, middle_grad_ref, gain_ref,
    fc1_ref, proj_ref, early_ref, table_ref, bias_ref, patches_out, qkv_out, fc1_out, proj_out, small,
    *scratch,
):
    sums1, qkv_rows, *scratch = scratch
    col_scratch, scratch = scratch[:7], scratch[7:]
    mix, qkv_scratch, fc1_scratch, sum_parts = scratch[:7], scratch[7:11], scratch[11:15], scratch[15:20]
    proj_rows, proj_box, proj_sems, *proj_scratch = scratch[20:]
    row, col = lax.axis_index("row"), lax.axis_index("col")
    images = dict(axes)["batch"]
    meet(
        ("row", row_peers()),
        ("col", [col_peer(step) for step in range(1, 4)]),
        ("batch", image_peers(images)),
    )

    def finish1(total, piece, rows):
        return last_finish(total, piece, rows, gain_ref, first_ref, middle_grad_ref, (None, sums1))

    image = lax.axis_index("batch")
    shared = images == 2

    def write_fc1(place, values, others=None):
        n = values.shape[0]
        if others is None:
            fc1_out[place * n : (place + 1) * n] = values
        else:
            fc1_out[pl.ds(pl.multiple_of((2 * place + image) * n, 8), n)] = values
            fc1_out[pl.ds(pl.multiple_of((2 * place + 1 - image) * n, 8), n)] = others

    def write_proj(place, values):
        proj_out[place] = values

    def proj_steps():
        copies = []
        for step in range(1, 4):
            copies.append(col_copy(proj_ref.at[col_peer(step)], proj_box.at[col], proj_sems, 0, step))
            copies[-1].start()
        proj_box[col] = proj_ref[col]
        yield
        for copy in copies:
            copy.wait()
        total = proj_box[0].astype(F32)
        for source in range(1, 4):
            total = total + proj_box[source].astype(F32)
        proj_rows[...] = total.astype(BF16)
        yield from weight_steps(proj_rows, images, proj_scratch, write_proj)

    head_grads = []

    def write_qkv(place, values, others=None):
        if others is not None:
            first, second = jnp.where(image == 0, values, others), jnp.where(image == 0, others, values)
            values = jnp.concatenate([first[: 3 * HEAD_DIM - HALF_GRAD], second], 0)
        head_grads.append(values)

    qkv_sum = column_steps(images, grads_ref, normed1_ref, qkv_rows, col_scratch)
    patches = row_mix_steps(qkv_grad_ref, weight_qkv_ref, patches_out, finish1, True, True, mix)
    fc1 = weight_steps(fc1_ref, images, fc1_scratch, write_fc1, shared)
    qkv = weight_steps(qkv_rows, images, qkv_scratch, write_qkv, shared)
    sums = sum_steps(small, axes, sum_parts)

    def go(*steps):
        for step in steps:
            next(step, None)

    proj = proj_steps()
    go(proj, qkv_sum, patches, patches, patches, proj, qkv_sum, patches)

    small[0:EARLY_ROWS] = early_ref[...]
    at = EARLY_ROWS
    for half in range(2):
        small[at : at + TABLE_ROWS // 2] = table_ref[:, half * 128 : (half + 1) * 128]
        at += TABLE_ROWS // 2
    place = lax.broadcasted_iota(jnp.int32, (BIAS_ROWS, 128), 0) - 2 * (col * 4 + row)
    small[at : at + BIAS_ROWS] = jnp.where(
        place == 0, bias_ref[0:1], jnp.where(place == 1, bias_ref[1:2], 0.0)
    )
    at += BIAS_ROWS
    lines = sums1.shape[1] // 128
    last = [sums1[i : i + 1, j * 128 : (j + 1) * 128] for i in range(2) for j in range(lines)]
    spare = jnp.zeros((LAST_ROWS - len(last), 128), F32)
    small[at : at + LAST_ROWS] = jnp.concatenate([*last, spare], 0)

    go(sums, fc1, proj, qkv_sum, qkv, sums, patches, fc1, proj, sums, qkv, fc1, sums, qkv)
    for kind in range(3):
        rows = slice(kind * HEAD_DIM, (kind + 1) * HEAD_DIM)
        qkv_out[kind] = jnp.concatenate([values[rows] for values in head_grads], 0).T


def tail(
    qkv_grad, weight_qkv, normed1, first, middle_grad, gain, fc1, proj, early, table, bias
):
    cols, n, tokens = qkv_grad.shape
    model = weight_qkv.shape[1]
    own, part = tokens // 4, model // 4
    shared = lax.axis_size("batch") == 2
    rows = HALF_GRAD if shared else n
    units = fc1.shape[0] * (2 if shared else 1)
    axes = tuple((name, lax.axis_size(name)) for name in ("row", "batch", "col"))
    small_rows = EARLY_ROWS + TABLE_ROWS + BIAS_ROWS + LAST_ROWS
    vmem = pl.BlockSpec(memory_space=pltpu.VMEM)
    return pl.pallas_call(
        partial(tail_kernel, axes),
        in_specs=[vmem] * 12,
        out_specs=[vmem] * 5,
        out_shape=[
            jax.ShapeDtypeStruct((part, tokens), F32),
            jax.ShapeDtypeStruct((3, part, 4 * HEAD_DIM), F32),
            jax.ShapeDtypeStruct((4 * units, part), F32),
            jax.ShapeDtypeStruct((4, proj.shape[1], part), F32),
            jax.ShapeDtypeStruct((small_rows, 128), F32),
        ],
        scratch_shapes=[
            pltpu.VMEM((3, model), F32),
            pltpu.VMEM((rows, model), BF16),
            *column_scratch(n, rows, model),
            *mix_scratch(own, model, True),
            *weight_scratch(rows, part),
            *weight_scratch(fc1.shape[0], part),
            *sum_scratch(small_rows, axes),
            pltpu.VMEM(proj.shape[1:], BF16),
            pltpu.VMEM(proj.shape, BF16),
            pltpu.SemaphoreType.DMA((2, 1, 4)),
            *weight_scratch(proj.shape[1], part),
        ],
        compiler_params=pltpu.CompilerParams(
            collective_id=3, has_side_effects=True, vmem_limit_bytes=60 << 20
        ),
        name="tail",
    )(
        qkv_grad.reshape(cols * n, tokens), qkv_grad, weight_qkv, normed1, first, middle_grad, gain,
        fc1, proj, early, table, bias,
    )


HIDDEN = 256
ROWS = 256


def hidden_kernel(x_ref, w1_ref, bias_ref, cot_ref, w2_ref, act_ref, grad_ref, bias_grad_ref):
    total = None
    for start in range(0, x_ref.shape[0], ROWS):
        rows = slice(start, start + ROWS)
        preact = mm_nt(x_ref[rows], w1_ref[...]) + bias_ref[...]
        act_grad = mm_nt(cot_ref[rows], w2_ref[...])
        below = 0.5 + 0.5 * lax.erf(preact * (0.5**0.5))
        density = jnp.exp(preact * preact * -0.5) * ((2 * math.pi) ** -0.5)
        act_ref[rows] = (preact * below).astype(BF16)
        grad = (act_grad * (below + preact * density)).astype(BF16)
        grad_ref[rows] = grad
        part = jnp.sum(grad.astype(F32), 0, keepdims=True)
        total = part if total is None else total + part
    bias_grad_ref[...] = total


def feed_forward(x, weights, bias, cotangent):
    tokens, model = x.shape
    hidden = weights.shape[1]
    step = HIDDEN if hidden % HIDDEN == 0 else hidden
    whole = pl.BlockSpec((tokens, model), lambda i: (0, 0), pipeline_mode=pl.Buffered(1))
    first, second = [pl.BlockSpec((None, step, model), lambda i, j=j: (j, i, 0)) for j in range(2)]
    vector = pl.BlockSpec((1, step), lambda i: (0, i))
    columns = pl.BlockSpec((tokens, step), lambda i: (0, i))
    return pl.pallas_call(
        hidden_kernel,
        grid=(hidden // step,),
        in_specs=[whole, first, vector, whole, second],
        out_specs=[columns, columns, vector],
        out_shape=[
            jax.ShapeDtypeStruct((tokens, hidden), BF16),
            jax.ShapeDtypeStruct((tokens, hidden), BF16),
            jax.ShapeDtypeStruct((1, hidden), F32),
        ],
        compiler_params=pltpu.CompilerParams(vmem_limit_bytes=40 << 20),
        cost_estimate=pl.CostEstimate(
            flops=4 * tokens * hidden * model,
            bytes_accessed=4 * (tokens + hidden) * model + 4 * tokens * hidden,
            transcendentals=2 * tokens * hidden,
        ),
        name="feed_forward",
    )(x, weights, bias, cotangent, weights)


def attention(qkv, table, cotangent, weights):
    count, _, width = qkv.shape
    tokens = count * width
    images = lax.axis_size("batch")
    vmem = pl.BlockSpec(memory_space=pltpu.VMEM)
    return pl.pallas_call(
        partial(attend_kernel, images),
        in_specs=[*[vmem] * 3, pl.BlockSpec(memory_space=pl.ANY)],
        out_specs=[*[vmem] * 5, pl.BlockSpec(memory_space=pl.ANY)],
        out_shape=[
            jax.ShapeDtypeStruct((count, HEAD_DIM, width), BF16),
            jax.ShapeDtypeStruct(qkv.shape, BF16),
            jax.ShapeDtypeStruct((count, HEAD_DIM, width), F32),
            jax.ShapeDtypeStruct((count, 8, width), F32),
            jax.ShapeDtypeStruct((width, 4 * cotangent.shape[0]), BF16),
            jax.ShapeDtypeStruct((2, count, *weights.shape[1:]), BF16),
        ],
        scratch_shapes=[
            pltpu.VMEM((count, width, 256), BF16),
            pltpu.VMEM((count, 256, width), BF16),
            pltpu.VMEM((count, HEAD_DIM, width), F32),
            pltpu.VMEM((count, 8, width), F32),
            pltpu.VMEM((count, 8, width), F32),
            pltpu.VMEM((count, HEAD_DIM, width), BF16),
            pltpu.SemaphoreType.DMA((2, 3, 4)),
            pltpu.VMEM((4, *cotangent.shape), BF16),
            pltpu.SemaphoreType.DMA((2, 1, 3)),
            pltpu.SemaphoreType.DMA((2,)),
            pltpu.SemaphoreType.DMA((2, 2, 2, 3)),
            pltpu.SemaphoreType.DMA((2, 2, 3)),
        ],
        compiler_params=pltpu.CompilerParams(
            collective_id=5, has_side_effects=True, vmem_limit_bytes=48 << 20
        ),
        cost_estimate=pl.CostEstimate(
            flops=2 * tokens * tokens * 512,
            bytes_accessed=6 * tokens * HEAD_DIM * 2,
            transcendentals=tokens * tokens,
        ),
        name="attend",
    )(qkv, table, cotangent, weights)


def attention_back(qkv, table, grad, exact, stat, fc2, activated, weights, middle, bias_fc2):
    count, _, width = qkv.shape
    tokens = count * width
    images, part = lax.axis_size("batch"), fc2.shape[1] // 4
    vmem = pl.BlockSpec(memory_space=pltpu.VMEM)
    return pl.pallas_call(
        partial(attend_back_kernel, images),
        in_specs=[*[vmem] * 8, pl.BlockSpec(memory_space=pl.ANY), vmem, vmem],
        out_specs=[vmem] * 5,
        out_shape=[
            jax.ShapeDtypeStruct((count, 3 * HEAD_DIM, width), BF16),
            jax.ShapeDtypeStruct(table.shape[::-1], F32),
            jax.ShapeDtypeStruct((2, 128), F32),
            jax.ShapeDtypeStruct((4, fc2.shape[0], part), F32),
            jax.ShapeDtypeStruct((part, width), BF16),
        ],
        scratch_shapes=[
            *fetch_scratch(weights),
            pltpu.VMEM((384, 128), F32),
            pltpu.VMEM((count, HEAD_DIM, width), BF16),
            pltpu.VMEM((count, width, 256), BF16),
            pltpu.VMEM((count, 256, width), BF16),
            pltpu.VMEM((count, width, 128), BF16),
            pltpu.VMEM((count, width, 128), F32),
            pltpu.VMEM((count, width, 128), F32),
            pltpu.VMEM((count, 256, width), F32),
            pltpu.VMEM((count, 256, width), BF16),
            pltpu.VMEM((count, 128, width), BF16),
            pltpu.VMEM((count, width, 128), BF16),
            pltpu.VMEM((count, width, 128), BF16),
            pltpu.VMEM((count, 3 * HEAD_DIM, width), BF16),
            pltpu.SemaphoreType.DMA((2, 3, 4)),
            *weight_scratch(fc2.shape[0], part),
            *mix_scratch(*middle.shape, True),
        ],
        compiler_params=pltpu.CompilerParams(
            collective_id=4, has_side_effects=True, vmem_limit_bytes=62 << 20
        ),
        cost_estimate=pl.CostEstimate(
            flops=2 * tokens * tokens * 1280,
            bytes_accessed=12 * tokens * HEAD_DIM * 2,
            transcendentals=tokens * tokens,
        ),
        name="attend_back",
    )(qkv, table, table.T, grad, exact, stat, fc2, activated, weights, middle, bias_fc2)


def moments(values):
    center = jnp.mean(values, -1, keepdims=True)
    spread = jnp.mean(values * values, -1, keepdims=True)
    return center, lax.rsqrt(spread - center * center + EPSILON)


def shards(
    patches,
    qkv_weight,
    qv_bias,
    proj_weight,
    proj_bias,
    norm1_gain,
    norm1_shift,
    norm2_gain,
    norm2_shift,
    fc1_weight,
    fc1_bias,
    fc2_weight,
    fc2_bias,
    height_table,
    width_table,
    out_grad,
):
    rows, cols = lax.axis_size("row"), lax.axis_size("col")
    row, col = lax.axis_index("row"), lax.axis_index("col")
    width = patches.shape[1]
    part = patches.shape[2]
    model = part * rows
    own = width // rows
    hidden = fc1_bias.shape[0] // rows
    head = HEAD_DIM

    images = lax.axis_size("batch")

    vectors = jnp.stack([norm1_gain, norm1_shift, norm2_gain, norm2_shift, proj_bias, fc2_bias])
    vectors = jnp.concatenate([vectors, jnp.zeros((2, part), F32)], 0)
    bias_qkv = lax.dynamic_index_in_dim(qv_bias.reshape(2, rows, head), row, 1, keepdims=False)
    bias_qkv = jnp.stack([bias_qkv[0], jnp.zeros_like(bias_qkv[0]), bias_qkv[1]]).reshape(1, -1)
    bias_fc1 = lax.dynamic_index_in_dim(fc1_bias.reshape(rows, hidden), row, 0, keepdims=True)
    columns = jnp.concatenate([jnp.pad(bias_qkv, ((0, 0), (0, 256 - 3 * head))), bias_fc1], 1)
    columns = jnp.broadcast_to(columns, (8, 256 + hidden))
    local_qkv = qkv_weight.reshape(part, 3, rows, head).transpose(2, 1, 3, 0).reshape(rows, 3 * head, part)
    qkv, normed1, first_own, weight_qkv, weight_proj, local_rest, vectors, columns = start(
        patches[0].T,
        local_qkv,
        proj_weight.reshape(rows, head, part),
        fc1_weight.T.reshape(rows, hidden, part),
        fc2_weight.reshape(rows, hidden, part),
        vectors,
        columns,
    )
    gain1, shift1, gain2, shift2, bias_proj, bias_fc2 = [vectors[i] for i in range(6)]
    weight_qkv = weight_qkv.reshape(cols * 3 * head, model)
    bias_fc1 = columns[:, 0, 256:].reshape(cols * hidden)

    zero_row = jnp.zeros((1, head), BF16)
    table = jnp.concatenate([height_table[::-1], zero_row, width_table[::-1], zero_row], 0)

    merged, qkv, exact, stat, cotangent, weights = attention(
        qkv, table, out_grad[0].T, local_rest.reshape(2, hidden, model)
    )
    weight_proj = weight_proj.reshape(cols * head, model)
    merged = merged.reshape(cols * head, width)

    def contract_rows(left, right):
        return lax.dot_general(left, right, (((0,), (0,)), ((), ())), preferred_element_type=F32)

    def sum_columns(values):
        return lax.psum_scatter(values, "col", scatter_dimension=0, tiled=False)

    def tokens_of_row(values):
        return lax.dynamic_slice_in_dim(values, row * own, own, 0)

    own_shape = (own, model)
    vec2 = jnp.stack([gain2, shift2, bias_proj])
    normed2, middle, weights = row_mix(
        forward_finish, "middle_and_norm2", 1, merged, weight_proj,
        (vec2, first_own), [jax.ShapeDtypeStruct(own_shape, F32)], True, None, weights,
    )
    normed2 = normed2.reshape(width, model)
    weights = weights.reshape(2, cols * hidden, model)
    activated, preact_grad, fc1_bias_part = feed_forward(normed2, weights, bias_fc1[None], cotangent)
    fc2_grad = contract_rows(activated, cotangent).astype(BF16)
    fc2_grad, preact_grad = lax.optimization_barrier((fc2_grad, preact_grad))
    fc1_grad = contract_rows(preact_grad, normed2).astype(BF16).reshape(cols, hidden, model)

    own_and_sums = [jax.ShapeDtypeStruct(own_shape, F32), jax.ShapeDtypeStruct((3, model), F32)]
    branch_grad, middle_grad, sums2, fc1_grad = row_mix(
        backward_finish, "middle_grad", 2, preact_grad, weights,
        (vec2, middle, tokens_of_row(cotangent)), own_and_sums, False, fc1_grad,
    )
    branch_grad = branch_grad.reshape(width, model)

    merged_grad = mm_nt(weight_proj, branch_grad).astype(BF16).reshape(cols, head, width)
    proj_grad = mm(merged, branch_grad).astype(BF16)
    fc2_grad = sum_columns(fc2_grad.reshape(cols, hidden, model))
    early = jnp.concatenate(
        [
            lax.dynamic_update_slice(jnp.zeros((rows, cols * hidden), F32), fc1_bias_part, (row, 0)).reshape(-1),
            lax.dynamic_update_slice(
                jnp.zeros((model,), F32), jnp.sum(out_grad[0], 0, dtype=F32), (row * part,)
            ),
            sums2.reshape(-1),
        ]
    ).reshape(-1, 128)
    merged_grad, fc1_grad, proj_grad, fc2_grad, early = lax.optimization_barrier(
        (merged_grad, fc1_grad, proj_grad, fc2_grad, early)
    )
    fc1_grad = sum_columns(fc1_grad)
    qkv_grad, table_grad, bias_grad, fc2_grad, final = attention_back(
        qkv, table, merged_grad, exact, stat, fc2_grad, activated, weights, middle, bias_fc2[None]
    )
    input_grad, qkv_weight_grad, fc1_grad, proj_grad, small = tail(
        qkv_grad, weight_qkv, normed1, first_own, middle_grad, gain1[None],
        fc1_grad, proj_grad.reshape(cols, head, model), early, table_grad, bias_grad,
    )

    def sum_images(values):
        return values if images == 2 else lax.psum(values.astype(BF16), "batch").astype(F32)

    fc2_grad = sum_images(fc2_grad).reshape(rows * hidden, part)
    proj_grad = sum_images(proj_grad).reshape(rows * head, part)
    fc1_grad = sum_images(fc1_grad).T
    qkv_weight_grad = sum_images(qkv_weight_grad).transpose(1, 0, 2)

    lines = model // 128
    fc1_bias_grad = small[: 4 * lines].reshape(rows, cols, hidden)
    fc1_bias_grad = lax.dynamic_index_in_dim(fc1_bias_grad, col, 1, keepdims=False).reshape(rows * hidden)
    fc2_bias_grad = small[4 * lines : 5 * lines].reshape(-1)
    gain2_grad, shift2_grad, proj_bias_grad = small[5 * lines : 8 * lines].reshape(3, model)
    at = EARLY_ROWS
    table_grad = jnp.concatenate([small[at : at + TABLE_ROWS // 2], small[at + TABLE_ROWS // 2 : at + TABLE_ROWS]], 1)
    table_grad = table_grad.T
    at += TABLE_ROWS
    bias_total = small[at : at + BIAS_ROWS].reshape(cols, rows, 2, 128)
    bias_total = lax.dynamic_index_in_dim(bias_total, col, 0, keepdims=False)[:, :, :head]
    bias_total = bias_total.transpose(1, 0, 2).reshape(2, rows * head)
    at += BIAS_ROWS
    gain1_grad, shift1_grad = small[at : at + 2 * lines].reshape(2, model)

    def features_of_row(values):
        return lax.dynamic_slice_in_dim(values, row * part, part, 0)

    side = 2 * GRID - 1
    return (
        final.T[None],
        input_grad.T[None],
        qkv_weight_grad,
        bias_total,
        proj_grad,
        features_of_row(proj_bias_grad),
        features_of_row(gain1_grad),
        features_of_row(shift1_grad),
        features_of_row(gain2_grad),
        features_of_row(shift2_grad),
        fc1_grad,
        fc1_bias_grad,
        fc2_grad,
        features_of_row(fc2_bias_grad),
        table_grad[:side][::-1],
        table_grad[2 * GRID : 2 * GRID + side][::-1],
    )


def solution(mesh):
    in_specs = (
        P("batch", "col", "row"),
        P("row", None, "col"),
        P(None, "col"),
        P("col", "row"),
        P("row"),
        P("row"),
        P("row"),
        P("row"),
        P("row"),
        P("row", "col"),
        P("col"),
        P("col", "row"),
        P("row"),
        P(),
        P(),
        P("batch", "col", "row"),
    )
    out_specs = (
        P("batch", "col", "row"),
        P("batch", "col", "row"),
        P("row", None, "col"),
        P(None, "col"),
        P("col", "row"),
        P("row"),
        P("row"),
        P("row"),
        P("row"),
        P("row"),
        P("row", "col"),
        P("col"),
        P("col", "row"),
        P("row"),
        P(),
        P(),
    )
    return jax.shard_map(shards, mesh=mesh, in_specs=in_specs, out_specs=out_specs, check_vma=False)
```

```python
import math
from functools import partial

import jax
import jax.numpy as jnp
from jax import lax
from jax.experimental import pallas as pl
from jax.experimental.pallas import tpu as pltpu
from jax.sharding import PartitionSpec as P

D = 1280
HEAD_DIM = 80
GRID = 64
EPSILON = 1e-06

LINES = 4
QUERIES = LINES * GRID
KEYS = 512
LOG2E = math.log2(math.e)
SCALE = HEAD_DIM**-0.5
BF16 = jnp.bfloat16
F32 = jnp.float32
MESH = pl.DeviceIdType.MESH


def mm(left, right):
    return jnp.dot(left, right, preferred_element_type=F32)


def mm_nt(left, right):
    return lax.dot_general(left, right, (((1,), (1,)), ((), ())), preferred_element_type=F32)


def split(values, parts):
    terms = []
    for _ in range(parts):
        term = values.astype(BF16)
        terms.append(term)
        values = values - term.astype(F32)
    return terms


def backwards(rows, columns):
    first = lax.broadcasted_iota(jnp.int32, (rows, columns), 0)
    second = lax.broadcasted_iota(jnp.int32, (rows, columns), 1)
    return jnp.where(first + second == 2 * GRID - 2, 1.0, 0.0).astype(BF16)


def fill_tables(height_ref, width_ref, tab_t):
    flip = backwards(2 * GRID - 1, 2 * GRID)
    tab_t[:, : 2 * GRID] = mm(height_ref[...], flip).astype(BF16)
    tab_t[:, 2 * GRID :] = mm(width_ref[...], flip).astype(BF16)


def skew(values, shift):
    n = values.shape[1]
    for bit, rows in ((32, 96), (16, 80), (8, 72)):
        take = jnp.broadcast_to(shift, (rows, n)) & bit
        values = jnp.where(take != 0, values[bit : bit + rows], values[:rows])
    for bit in (4, 2, 1):
        take = jnp.broadcast_to(shift, values.shape) & bit
        values = jnp.where(take != 0, pltpu.roll(values, values.shape[0] - bit, 0), values)
    return values[:GRID]


def unskew(values, shift):
    n = values.shape[1]
    values = jnp.concatenate([values, jnp.zeros((8, n), F32)], 0)
    for bit in (1, 2, 4):
        take = jnp.broadcast_to(shift, values.shape) & bit
        values = jnp.where(take != 0, pltpu.roll(values, bit, 0), values)
    for bit in (8, 16, 32):
        zeros = jnp.zeros((bit, n), F32)
        take = jnp.broadcast_to(shift, (values.shape[0] + bit, n)) & bit
        values = jnp.where(
            take != 0,
            jnp.concatenate([zeros, values], 0),
            jnp.concatenate([values, zeros], 0),
        )
    return values


def token_shifts(step):
    lane = lax.broadcasted_iota(jnp.int32, (1, QUERIES), 1)
    return (GRID - 1) - (step * LINES + lane // GRID), (GRID - 1) - lane % GRID


def query_columns(q, tab, step, tail):
    shift_rows, shift_cols = token_shifts(step)
    both = mm(tab, q)
    rel_rows = skew(both[: 2 * GRID], shift_rows)
    rel_cols = skew(both[2 * GRID :], shift_cols)
    rel = jnp.concatenate([rel_rows, rel_cols], 0) * (1.0 / SCALE)
    return jnp.concatenate([rel.astype(BF16), q, tail], 0)


def col_peer(step):
    me = lax.axis_index("col")
    odd, high = step % 2, step // 2
    return lax.rem(me + odd - 2 * odd * lax.rem(me, 2) + 2 * high, 4)


def col_barrier():
    barrier = pltpu.get_barrier_semaphore()
    for step in range(1, 4):
        pl.semaphore_signal(barrier, device_id={"col": col_peer(step)}, device_id_type=MESH)
    pl.semaphore_wait(barrier, 3)


def col_copy(source, target, sems, kind, step):
    return pltpu.make_async_remote_copy(
        src_ref=source,
        dst_ref=target,
        send_sem=sems.at[0, kind, step],
        recv_sem=sems.at[1, kind, step],
        device_id={"col": col_peer(step)},
        device_id_type=MESH,
    )


class Chain:
    def __init__(self, view, sems, on_block=None):
        self.view, self.sems, self.on_block = view, sems, on_block
        self.me = lax.axis_index("col")

    def copy(self, way, hop):
        block = self.me + (hop - 1) * (2 * way - 1)
        return pltpu.make_async_remote_copy(
            src_ref=self.view(block),
            dst_ref=self.view(block),
            send_sem=self.sems.at[0, way, hop - 1],
            recv_sem=self.sems.at[1, way, hop - 1],
            device_id={"col": lax.rem(self.me + 1 + 2 * way, 4)},
            device_id_type=MESH,
        )

    def sends(self, way, hop):
        if way:
            return jnp.logical_and(self.me > 0, self.me + hop - 1 < 4)
        return jnp.logical_and(self.me < 3, self.me - hop + 1 >= 0)

    def each(self, hop, act):
        for way in range(2):

            @pl.when(self.me + hop < 4 if way else self.me - hop >= 0)
            def _():
                act(self.me + hop * (2 * way - 1), way, hop)

    def start(self, way, hop):
        @pl.when(self.sends(way, hop))
        def _():
            self.copy(way, hop).start()

    def begin(self, hop=1):
        for way in range(2):
            self.start(way, hop)

    def hop(self, hop, last=3, tell=True):
        def arrived(block, way, hop):
            self.copy(way, hop).wait_recv()

        self.each(hop, arrived)
        if hop < last:
            for way in range(2):
                self.start(way, hop + 1)
        if self.on_block and tell:
            self.each(hop, self.on_block)

    def end(self, hops=(1, 2, 3)):
        for hop in hops:
            for way in range(2):

                @pl.when(self.sends(way, hop))
                def _():
                    self.copy(way, hop).wait_send()


def image_copy(source, target, sems, *place):
    return pltpu.make_async_remote_copy(
        src_ref=source,
        dst_ref=target,
        send_sem=sems.at[(0, *place)],
        recv_sem=sems.at[(1, *place)],
        device_id={"batch": 1 - lax.axis_index("batch")},
        device_id_type=MESH,
    )


def weight_chains(weight_all, images, chain_sems, swap_sems):
    image = lax.axis_index("batch")

    def swap_copy(block, way, hop):
        return image_copy(weight_all.at[image, block], weight_all.at[image, block], swap_sems, way, hop - 1)

    def swap(block, way, hop):
        swap_copy(block, way, hop).start()

    def swapped(block, way, hop):
        swap_copy(block, way, hop).wait()

    shared = images == 2
    chains = [
        Chain(lambda i, which=which: weight_all.at[which, i], chain_sems.at[order], swap if shared else None)
        for order, which in enumerate([image] if shared else [0, 1])
    ]
    return chains, swapped if shared else None


HALF = 2 * HEAD_DIM


def half_start(image):
    return pl.multiple_of(image * (3 * HEAD_DIM - HALF_GRAD), 16)


HALF_GRAD = 128


def row_copy(source, target, sems, kind, order, peer):
    return pltpu.make_async_remote_copy(
        src_ref=source,
        dst_ref=target,
        send_sem=sems.at[0, kind, order],
        recv_sem=sems.at[1, kind, order],
        device_id={"row": peer},
        device_id_type=MESH,
    )


def beside(blocks):
    return jnp.concatenate([block.astype(F32) for block in blocks], 1)


def upright(blocks):
    return jnp.concatenate([block.astype(F32) for block in blocks], 0).T


def start_kernel(
    images, patches_ref, qkv_ref, proj_ref, fc1_ref, fc2_ref, qv_bias_ref, fc1_bias_ref, v0, v1, v2, v3, v4, v5,
    qkv_out, normed_out, first_out, weight_out, proj_out, rest_out, vectors_out, columns_out,
    patches_all, parts, rest_parts, rest_own, column_ref, vector_ref, vector_parts, halves, sems, col_sems, chain_sems, swap_sems,
):
    row, col, image = lax.axis_index("row"), lax.axis_index("col"), lax.axis_index("batch")
    near, far, diag = row_peers()
    own = first_out.shape[0]
    shared = images == 2
    meet(
        ("row", (near, far, diag)),
        ("col", [col_peer(step) for step in range(1, 4)]),
        ("batch", image_peers(images) if shared else ()),
    )

    def to_row(source, target, kind):
        copies = [row_copy(source(peer), target, sems, kind, i, peer) for i, peer in enumerate((near, far, diag))]
        for copy in copies:
            copy.start()
        return copies

    n, units = 3 * HEAD_DIM, fc1_ref.shape[1] // 4

    def mine(values, size):
        piece = values[:, :size]
        for place in range(1, 4):
            piece = jnp.where(row == place, values[:, place * size : (place + 1) * size], piece)
        return piece

    bias = mine(qv_bias_ref[...], HEAD_DIM)
    bias = [bias[0:1], jnp.zeros((1, HEAD_DIM), F32), bias[1:2], jnp.zeros((1, 256 - n), F32)]
    bias = jnp.concatenate([*bias, mine(fc1_bias_ref[...].reshape(1, -1), units)], 1)
    column_ref[...] = jnp.broadcast_to(bias, column_ref.shape)
    vectors = [ref[...].reshape(1, -1) for ref in (v0, v1, v2, v3, v4, v5)]
    vector_ref[...] = jnp.concatenate([*vectors, *vectors[:2]], 0)
    weight_copies = to_row(lambda peer: qkv_ref.at[peer], parts.at[row, 0:n], 0)
    weight_copies += to_row(lambda peer: proj_ref.at[peer], parts.at[row, n : n + HEAD_DIM], 4)
    vector_copies = to_row(lambda peer: vector_ref, vector_parts.at[row], 1)
    to_near = row_copy(patches_ref, patches_all.at[row], sems, 2, 0, near)
    to_far = row_copy(patches_ref, patches_all.at[row], sems, 2, 1, far)
    to_near.start()
    column_copies = [col_copy(column_ref, columns_out.at[col], col_sems, 0, step) for step in range(1, 4)]
    for copy in column_copies:
        copy.start()
    parts[row, 0:n] = qkv_ref[row]
    parts[row, n : n + HEAD_DIM] = proj_ref[row]
    vector_parts[row] = vector_ref[...]
    patches_all[row] = patches_ref[...]
    columns_out[col] = column_ref[...]
    for copy in weight_copies:
        copy.wait()
    to_far.start()
    weight = beside([parts[i] for i in range(4)]).astype(BF16)

    def swap_copy(block, way, hop):
        return image_copy(halves.at[image, block], halves.at[image, block], swap_sems, way, hop - 1)

    def swap(block, way, hop):
        swap_copy(block, way, hop).start()

    halves[0, col] = weight[:HALF]
    halves[1, col] = weight[HALF:]
    orders = [image] if shared else [0, 1]
    chains = [
        Chain(lambda i, which=which: halves.at[which, i], chain_sems.at[order], swap if shared else None)
        for order, which in enumerate(orders)
    ]

    def product(block, way=0, hop=0):
        if hop and shared:
            swap_copy(block, way, hop).wait()
        weight_out[block, 0:HALF] = halves[0, block]
        weight_out[block, HALF:] = halves[1, block, 0 : n - HALF]
        proj_out[block] = halves[1, block, n - HALF :]
        bias = jnp.concatenate([columns_out[block][:, 0:256]] * 16, 0).T[:n, 0:1]
        qkv_out[block] = (mm_nt(weight_out[block], normed_out[...]) + bias).astype(BF16)

    for chain in chains:
        chain.begin()
    for copy in vector_copies + column_copies:
        copy.wait()
    vectors_out[...] = beside([vector_parts[i] for i in range(4)])
    to_far.wait_recv()
    pass_on = row_copy(patches_all.at[far], patches_all.at[far], sems, 2, 2, near)
    pass_on.start()
    for which, ref in enumerate((fc1_ref, fc2_ref)):
        for place in range(4):
            block = ref[:, place * units : (place + 1) * units].astype(F32).T
            rest_own[place, which * units : (which + 1) * units] = block.astype(BF16)
    rest_copies = to_row(lambda peer: rest_own.at[peer], rest_parts.at[row], 3)
    rest_parts[row] = rest_own[row]
    for chain in chains:
        chain.hop(1)
    to_near.wait_recv()
    pass_on.wait_recv()
    for start in range(0, normed_out.shape[0], own):
        scaled, _ = normal(upright([patches_all[i, :, start : start + own] for i in range(4)]))
        normed_out[start : start + own] = (scaled * vectors_out[0:1] + vectors_out[1:2]).astype(BF16)
    for chain in chains:
        chain.hop(2)
    product(col)
    chains[0].each(1, product)
    for chain in chains:
        chain.hop(3)
    chains[0].each(2, product)
    mine = pl.ds(pl.multiple_of(row * own, own), own)
    first_out[...] = upright([patches_all[i, :, mine] for i in range(4)]).astype(BF16)
    for copy in rest_copies:
        copy.wait()
    rest_out[...] = beside([rest_parts[i] for i in range(4)]).astype(BF16)
    chains[0].each(3, product)
    for chain in chains:
        chain.end()
    for copy in (to_near, to_far, pass_on):
        copy.wait_send()


def start(patches, local_qkv, local_proj, local_fc1, local_fc2, qv_bias, fc1_bias, *vectors):
    columns = (8, 256 + fc1_bias.shape[0] // 4)
    part, width = patches.shape
    n, model = local_qkv.shape[1], part * 4
    rest = 2 * (local_fc1.shape[1] // 4)
    vmem = pl.BlockSpec(memory_space=pltpu.VMEM)
    return pl.pallas_call(
        partial(start_kernel, lax.axis_size("batch")),
        in_specs=[vmem] * 13,
        out_specs=[vmem] * 8,
        out_shape=[
            jax.ShapeDtypeStruct((4, n, width), BF16),
            jax.ShapeDtypeStruct((width, model), BF16),
            jax.ShapeDtypeStruct((width // 4, model), BF16),
            jax.ShapeDtypeStruct((4, n, model), BF16),
            jax.ShapeDtypeStruct((4, HEAD_DIM, model), BF16),
            jax.ShapeDtypeStruct((rest, model), BF16),
            jax.ShapeDtypeStruct((8, model), F32),
            jax.ShapeDtypeStruct((4, *columns), F32),
        ],
        scratch_shapes=[
            pltpu.VMEM((4, part, width), BF16),
            pltpu.VMEM((4, n + HEAD_DIM, part), BF16),
            *[pltpu.VMEM((4, rest, part), BF16)] * 2,
            pltpu.VMEM(columns, F32),
            pltpu.VMEM((8, part), F32),
            pltpu.VMEM((4, 8, part), F32),
            pltpu.VMEM((2, 4, HALF, model), BF16),
            pltpu.SemaphoreType.DMA((2, 6, 3)),
            pltpu.SemaphoreType.DMA((2, 1, 4)),
            pltpu.SemaphoreType.DMA((2, 2, 2, 3)),
            pltpu.SemaphoreType.DMA((2, 2, 3)),
        ],
        compiler_params=pltpu.CompilerParams(
            collective_id=7, has_side_effects=True, vmem_limit_bytes=48 << 20
        ),
        name="start",
    )(patches, local_qkv, local_proj, local_fc1, local_fc2, qv_bias, fc1_bias, *vectors)


CHAIN_TURNS = (6, 12)


def attend_kernel(
    images, given_ref, height_ref, width_ref, cot_ref, weight_ref,
    merged_ref, qkv_ref, exact_ref, stat_ref, cot_out, weight_all,
    kaug, columns, acc, top, total, box, sems, cot_parts, cot_sems, local_sems, chain_sems, swap_sems,
    tab_t, tab_ref,
):
    me = lax.axis_index("col")
    width = given_ref.shape[2]
    blocks = width // QUERIES
    row, image = lax.axis_index("row"), lax.axis_index("batch")
    near, far, diag = row_peers()
    shared = images == 2
    meet(
        ("row", (near, far)),
        ("col", [col_peer(step) for step in range(1, 4)]),
        ("batch", image_peers(images) if shared else ()),
    )

    chains, swapped = weight_chains(weight_all, images, chain_sems, swap_sems)
    keep = [pltpu.make_async_copy(weight_ref.at[i], weight_all.at[i, me], local_sems.at[i]) for i in range(2)]
    for copy in keep:
        copy.start()

    def part_copy(step):
        return col_copy(given_ref.at[col_peer(step)], qkv_ref.at[me], sems, 0, step)

    def merged_copy(step):
        return col_copy(box.at[col_peer(step)], merged_ref.at[me], sems, 1, step)

    for step in (2, 1):
        part_copy(step).start()
    to_near = row_copy(cot_ref, cot_parts.at[row], cot_sems, 0, 0, near)
    to_far = row_copy(cot_ref, cot_parts.at[row], cot_sems, 0, 1, far)
    pass_on = row_copy(cot_parts.at[far], cot_parts.at[far], cot_sems, 0, 2, near)
    to_far.start()
    to_near.start()
    cot_parts[row] = cot_ref[...]
    qkv_ref[me] = given_ref[me]

    pad = jnp.zeros((128 - HEAD_DIM, width), F32)
    token = lax.broadcasted_iota(jnp.int32, (width, 2 * GRID), 0)
    lane = lax.broadcasted_iota(jnp.int32, (width, 2 * GRID), 1)
    tail = jnp.zeros((128 - HEAD_DIM, QUERIES), BF16)
    fill_tables(height_ref, width_ref, tab_t)
    tab_ref[...] = tab_t[...].astype(F32).T.astype(BF16)
    factor = SCALE * LOG2E

    def prepare(part):
        at = token + part * width
        hot = jnp.where(jnp.where(lane < GRID, at // GRID, at % GRID + GRID) == lane, 1.0, 0.0)
        key = qkv_ref[part, HEAD_DIM : 2 * HEAD_DIM]
        kaug[part, :, 0:128] = hot.astype(BF16)
        kaug[part, :, 128:256] = jnp.concatenate([key.astype(F32), pad], 0).T.astype(BF16)
        for block in range(blocks):
            at = slice(block * QUERIES, (block + 1) * QUERIES)
            columns[part, :, at] = query_columns(
                qkv_ref[part, 0:HEAD_DIM, at], tab_ref[...], part * blocks + block, tail
            )
        acc[part] = jnp.zeros((HEAD_DIM, width), F32)
        top[part] = jnp.full((8, width), -1e30, F32)
        total[part] = jnp.zeros((8, width), F32)

    def finish(part):
        whole, best = total[part, 0:1], top[part, 0:1]
        result = acc[part] * (1.0 / whole)
        exact_ref[part] = result
        box[part] = result.astype(BF16)
        stat_ref[part] = jnp.broadcast_to(best + jnp.log2(whole) * (1.0 / factor), (8, width))

    def pair(turn, carry):
        newest = (turn + 15) // 16 + (turn + 12) // 16 + (turn + 7) // 16
        place = turn - newest * newest
        q_step = jnp.where(place < newest, place, newest)
        k_step = jnp.where(place < newest, newest, place - newest)
        q_part, k_part = col_peer(q_step), col_peer(k_step)

        @pl.when(jnp.logical_and(place == 0, newest > 0))
        def _():
            part_copy(newest).wait_recv()

        @pl.when(place == 0)
        def _():
            prepare(col_peer(newest))

        @pl.when(turn == 1)
        def _():
            part_copy(3).start()

        @pl.when(turn == CHAIN_TURNS[0])
        def _():
            for chain in chains:
                chain.begin()

        @pl.when(turn == CHAIN_TURNS[1])
        def _():
            for chain in chains:
                chain.hop(1)
            to_far.wait_recv()
            pass_on.start()

        for block in range(blocks):
            at = slice(block * QUERIES, (block + 1) * QUERIES)
            best, whole, result = top[q_part, 0:1, at], total[q_part, 0:1, at], acc[q_part, :, at]
            for start in range(0, width, KEYS):
                keys = slice(start, start + KEYS)
                scores = mm(kaug[k_part, keys], columns[q_part, :, at])
                new_best = jnp.maximum(best, jnp.max(scores, 0, keepdims=True))
                weights = jnp.exp2((scores - new_best) * factor)
                keep = jnp.exp2((best - new_best) * factor)
                whole = whole * keep + jnp.sum(weights, 0, keepdims=True)
                value = qkv_ref[k_part, 2 * HEAD_DIM : 3 * HEAD_DIM, keys]
                result = result * keep + mm(value, weights.astype(BF16))
                best = new_best
            top[q_part, :, at] = jnp.broadcast_to(best, (8, QUERIES))
            total[q_part, :, at] = jnp.broadcast_to(whole, (8, QUERIES))
            acc[q_part, :, at] = result

        @pl.when(jnp.logical_and(turn >= 9, jnp.logical_or(place < 3, turn == 15)))
        def _():
            finish(q_part)

        @pl.when(jnp.logical_and(turn >= 9, jnp.logical_or(jnp.logical_and(turn > 9, place < 3), turn == 15)))
        def _():
            merged_copy(q_step).start()

        return carry

    for copy in keep:
        copy.wait()
    lax.fori_loop(0, 16, pair, 0)
    for chain in chains:
        chain.hop(2, 2, False)
    to_near.wait_recv()
    pass_on.wait_recv()
    for start in range(0, width, QUERIES):
        rows = slice(start, start + QUERIES)
        cot_out[rows] = upright([cot_parts[i, :, rows] for i in range(4)]).astype(BF16)
    merged_ref[me] = box[me]
    for chain in chains:
        chain.end((1, 2))
        if shared:
            chain.each(1, swapped)
    for copy in (to_near, to_far, pass_on):
        copy.wait_send()
    for step in range(1, 4):
        part_copy(step).wait_send()
        merged_copy(step).wait()


GRADS, QUERY_OUT, KEY_OUT = range(3)
KEY_ROWS = slice(HEAD_DIM, 3 * HEAD_DIM)


def attend_back_kernel(
    images, qkv_ref, height_ref, width_ref, given_ref, exact_ref, stat_ref, fc2_ref,
    activated_ref, weights_ref, middle_ref, bias_fc2_ref,
    out_ref, tab_grad_ref, bias_out, fc2_out, block_out,
    tab_t_ref, tab_ref, held, held_sem, bias_ref, grads, kaug, kaug_t, vaug, key_sum, value_sum, spread, columns,
    grad_columns, grad_rows, q_rows, box, sems, *weight_parts,
):
    me = lax.axis_index("col")
    width = qkv_ref.shape[2]
    blocks = width // QUERIES
    weight_copy = fetch(weights_ref, 1, (held, held_sem))
    weight_copy.start()
    meet(
        ("row", row_peers()),
        ("col", [col_peer(step) for step in range(1, 4)]),
        ("batch", image_peers(images) if images == 2 else ()),
    )

    fc2_grads = []

    def write_fc2(place, values):
        fc2_grads.append(values)

    fc2 = weight_steps(fc2_ref, images, weight_parts[:4], write_fc2)

    def finish_block(total, piece, rows):
        return middle_ref[rows] + (total + bias_fc2_ref[0:1])

    block = row_mix_steps(activated_ref, held, block_out, finish_block, False, True, weight_parts[4:])

    def grad_copy(step):
        return col_copy(given_ref.at[col_peer(step)], grads.at[me], sems, GRADS, step)

    def query_copy(step):
        at = col_peer(step)
        return col_copy(box.at[at, 0:HEAD_DIM], out_ref.at[me, 0:HEAD_DIM], sems, QUERY_OUT, step)

    def key_copy(step):
        at = col_peer(step)
        return col_copy(box.at[at, KEY_ROWS], out_ref.at[me, KEY_ROWS], sems, KEY_OUT, step)

    for step in range(1, 4):
        grad_copy(step).start()
    next(fc2)
    grads[me] = given_ref[me]

    fill_tables(height_ref, width_ref, tab_t_ref)
    tab_ref[...] = tab_t_ref[...].astype(F32).T.astype(BF16)
    tail_row = lax.broadcasted_iota(jnp.int32, (128 - HEAD_DIM, width), 0)
    pad = jnp.where(tail_row < 3, 1.0, 0.0)
    token = lax.broadcasted_iota(jnp.int32, (width, 2 * GRID), 0)
    lane = lax.broadcasted_iota(jnp.int32, (width, 2 * GRID), 1)

    def fill(part, carry):
        at = token + part * width
        hot = jnp.where(jnp.where(lane < GRID, at // GRID, at % GRID + GRID) == lane, 1.0, 0.0)
        key, value = qkv_ref[part, HEAD_DIM : 2 * HEAD_DIM], qkv_ref[part, 2 * HEAD_DIM : 3 * HEAD_DIM]
        kaug[part, :, 0:128] = hot.astype(BF16)
        kaug[part, :, 128:256] = jnp.concatenate([key.astype(F32), pad], 0).T.astype(BF16)
        vaug[part] = jnp.concatenate([value.astype(F32), pad], 0).T.astype(BF16)
        kaug_t[part, 0:128] = hot.T.astype(BF16)
        kaug_t[part, 128:208] = key
        kaug_t[part, 208:256] = jnp.zeros((48, width), BF16)
        return carry

    lax.fori_loop(0, 4, fill, 0)
    key_sum[...] = jnp.zeros_like(key_sum)
    value_sum[...] = jnp.zeros_like(value_sum)
    spread[...] = jnp.zeros_like(spread)
    tab_grad_ref[...] = jnp.zeros_like(tab_grad_ref)
    bias_ref[...] = jnp.zeros_like(bias_ref)

    block_row = lax.broadcasted_iota(jnp.int32, (128 - HEAD_DIM, QUERIES), 0)

    def tail(row):
        out = jnp.zeros((128 - HEAD_DIM, QUERIES), F32)
        for place, term in enumerate(split(row, 3)):
            out = jnp.where(block_row == place, term.astype(F32), out)
        return out.astype(BF16)

    zero_tail = jnp.zeros((128 - HEAD_DIM, QUERIES), F32)

    def prepare(part):
        for block in range(blocks):
            at = slice(block * QUERIES, (block + 1) * QUERIES)
            q, grad = qkv_ref[part, 0:HEAD_DIM, at], grads[part, :, at]
            inner = jnp.sum(grad.astype(F32) * exact_ref[part, :, at], 0, keepdims=True)
            columns[part, :, at] = query_columns(
                q, tab_ref[...], part * blocks + block, tail(-stat_ref[part, 0:1, at])
            )
            grad_columns[part, :, at] = jnp.concatenate([grad, tail(-inner)], 0)
            grad_rows[part, at] = jnp.concatenate([grad.astype(F32), zero_tail], 0).T.astype(BF16)
            q_rows[part, at] = jnp.concatenate([q.astype(F32), zero_tail], 0).T.astype(BF16)

    def add_bias(first, values):
        total = jnp.sum(values.astype(F32), 1, keepdims=True)
        bias_ref[first : first + values.shape[0]] += jnp.broadcast_to(total, (values.shape[0], 128))

    def finish_queries(part):
        for block in range(blocks):
            at = slice(block * QUERIES, (block + 1) * QUERIES)
            rows, cols = token_shifts(part * blocks + block)
            lifted = jnp.concatenate(
                [unskew(spread[part, 0:GRID, at], rows), unskew(spread[part, GRID : 2 * GRID, at], cols)], 0
            )
            high, low = split(lifted, 2)
            query_grad = spread[part, 128 : 128 + HEAD_DIM, at] * SCALE
            query_grad = query_grad + (mm(tab_t_ref[...], high) + mm(tab_t_ref[...], low))
            q = qkv_ref[part, 0:HEAD_DIM, at]
            tab_grad_ref[...] += mm_nt(q, high) + mm_nt(q, low)
            box[part, 0:HEAD_DIM, at] = query_grad.astype(BF16)
        add_bias(0, box[part, 0:HEAD_DIM])

    def finish_keys(part):
        key_grad = (key_sum[part] * SCALE).T[:HEAD_DIM].astype(BF16)
        value_grad = value_sum[part].T[:HEAD_DIM].astype(BF16)
        box[part, HEAD_DIM : 2 * HEAD_DIM] = key_grad
        box[part, 2 * HEAD_DIM : 3 * HEAD_DIM] = value_grad
        add_bias(HEAD_DIM, key_grad)
        add_bias(2 * HEAD_DIM, value_grad)

    def pair(turn, carry):
        later = jnp.maximum(turn - 4, 0)
        q_step = jnp.where(turn < 4, 0, 1 + later % 3)
        k_step = jnp.where(turn < 4, 3 - turn, 3 - later // 3)
        q_part, k_part = col_peer(q_step), col_peer(k_step)

        @pl.when(jnp.logical_and(turn >= 4, turn < 7))
        def _():
            grad_copy(q_step).wait_recv()

        @pl.when(jnp.logical_or(turn == 0, jnp.logical_and(turn >= 4, turn < 7)))
        def _():
            prepare(q_part)

        for block in range(blocks):
            at = slice(block * QUERIES, (block + 1) * QUERIES)
            total = None
            for start in range(0, width, KEYS):
                keys = slice(start, start + KEYS)
                weights = jnp.exp2(mm(kaug[k_part, keys], columns[q_part, :, at]) * (SCALE * LOG2E))
                score_grad = (weights * mm(vaug[k_part, keys], grad_columns[q_part, :, at])).astype(BF16)
                value_sum[k_part, keys] += mm(weights.astype(BF16), grad_rows[q_part, at])
                key_sum[k_part, keys] += mm(score_grad, q_rows[q_part, at])
                result = mm(kaug_t[k_part, :, keys], score_grad)
                total = result if total is None else total + result
            spread[q_part, :, at] += total

        keys_done = jnp.logical_and(turn >= 4, q_step == 3)
        queries_done = jnp.logical_or(turn == 3, turn >= 13)

        @pl.when(keys_done)
        def _():
            finish_keys(k_part)

        @pl.when(jnp.logical_and(keys_done, k_step > 0))
        def _():
            key_copy(k_step).start()

        @pl.when(queries_done)
        def _():
            finish_queries(q_part)

        @pl.when(jnp.logical_and(queries_done, q_step > 0))
        def _():
            query_copy(q_step).start()

        return carry

    weight_copy.wait()
    next(block)
    next(block)
    lax.fori_loop(0, 4, pair, 0)
    next(block)
    next(block)
    next(fc2)
    lax.fori_loop(4, 9, pair, 0)
    next(block, None)
    next(fc2, None)
    fc2_out[...] = jnp.concatenate(fc2_grads, 0).T
    lax.fori_loop(9, 16, pair, 0)
    out_ref[me] = box[me]
    for step in range(1, 4):
        grad_copy(step).wait_send()
        query_copy(step).wait()
        key_copy(step).wait()
    bias_out[0:1] = bias_ref[0:128].T[0:1]
    bias_out[1:2] = bias_ref[2 * HEAD_DIM : 2 * HEAD_DIM + 128].T[0:1]


MIX_SUBS = 2
TO_NEAR, PASS_ON, TO_FAR, OUT_NEAR, OUT_FAR, OUT_ON = range(6)


def normal(values):
    center, inv = moments(values)
    return (values - center) * inv, inv


def normal_back(grad, scaled, inv, gain):
    grad = grad * gain
    return inv * (
        grad
        - jnp.mean(grad, -1, keepdims=True)
        - scaled * jnp.mean(grad * scaled, -1, keepdims=True)
    )


def add_sums(sums_ref, piece, terms):
    for place, term in enumerate(terms):
        total = jnp.sum(term, 0, keepdims=True)
        if piece:
            total = total + sums_ref[place : place + 1]
        sums_ref[place : place + 1] = total


def forward_finish(total, piece, rows, vec_ref, first_ref, out_refs):
    middle = first_ref[rows].astype(F32) + (total + vec_ref[2:3])
    out_refs[0][rows] = middle
    scaled, _ = normal(middle)
    return (scaled * vec_ref[0:1] + vec_ref[1:2]).astype(BF16)


def backward_finish(total, piece, rows, vec_ref, first_ref, add_ref, out_refs):
    scaled, inv = normal(first_ref[rows].astype(F32))
    result = add_ref[rows].astype(F32) + normal_back(total, scaled, inv, vec_ref[0:1])
    branch = result.astype(BF16)
    out_refs[0][rows] = result
    add_sums(out_refs[1], piece, (total * scaled, total, branch.astype(F32)))
    return branch


def last_finish(total, piece, rows, vec_ref, first_ref, add_ref, out_refs):
    scaled, inv = normal(first_ref[rows].astype(F32))
    add_sums(out_refs[1], piece, (total * scaled, total))
    return add_ref[rows] + normal_back(total, scaled, inv, vec_ref[0:1])


def row_peers():
    me = lax.axis_index("row")
    near = me + 1 - 2 * lax.rem(me, 2)
    return near, lax.rem(me + 2, 4), lax.rem(near + 2, 4)


def meet(*groups):
    barrier = pltpu.get_barrier_semaphore()
    for axis, peers in groups:
        for peer in peers:
            pl.semaphore_signal(barrier, device_id={axis: peer}, device_id_type=MESH)
    pl.semaphore_wait(barrier, sum(len(peers) for _, peers in groups))


def row_mix_steps(left_ref, weight_ref, gathered, finish, left_t, to_features, scratch):
    far_keep, own_keep, out_box, in_box, sems, *more = scratch
    own = far_keep.shape[0]
    sub = own // MIX_SUBS
    me = lax.axis_index("row")
    near, far, diag = row_peers()
    started = []

    def send(source, target, kind, piece, peer):
        copy = pltpu.make_async_remote_copy(
            src_ref=source,
            dst_ref=target,
            send_sem=sems.at[0, kind, piece],
            recv_sem=sems.at[1, kind, piece],
            device_id={"row": peer},
            device_id_type=MESH,
        )
        copy.start()
        started.append(copy)
        return copy

    def product(owner, piece):
        at = pl.ds(pl.multiple_of(owner * own + piece * sub, sub), sub)
        if left_t:
            left = left_ref[:, at].astype(F32).T.astype(BF16)
        else:
            left = left_ref[at, :]
        return mm(left, weight_ref[...])

    pieces = [slice(piece * sub, (piece + 1) * sub) for piece in range(MIX_SUBS)]
    passed, direct, summed = [], [], []
    for piece, rows in enumerate(pieces):
        out_box[0, rows] = product(diag, piece).astype(BF16)
        passed.append(send(out_box.at[0, rows], in_box.at[0, rows], PASS_ON, piece, near))
        far_keep[rows] = product(far, piece)
    yield
    for piece, rows in enumerate(pieces):
        out_box[1, rows] = product(near, piece).astype(BF16)
        direct.append(send(out_box.at[1, rows], in_box.at[1, rows], TO_NEAR, piece, near))
        passed[piece].wait_recv()
        out_box[2, rows] = (far_keep[rows] + in_box[0, rows].astype(F32)).astype(BF16)
        summed.append(send(out_box.at[2, rows], in_box.at[2, rows], TO_FAR, piece, far))
    yield
    for piece, rows in enumerate(pieces):
        own_keep[rows] = product(me, piece)
    yield
    near_out, far_out, on_out = [], [], []
    for piece, rows in enumerate(pieces):
        direct[piece].wait_recv()
        summed[piece].wait_recv()
        total = own_keep[rows] + in_box[1, rows].astype(F32) + in_box[2, rows].astype(F32)
        result = finish(total, piece, rows)
        if to_features:
            boxes, arrived = more
            part = gathered.shape[0]
            for place in range(4):
                boxes[place, rows] = result[:, place * part : (place + 1) * part].astype(BF16)
            arrived[me, rows] = boxes[me, rows]
            for kind, peer, copies in (
                (OUT_NEAR, near, near_out), (OUT_FAR, far, far_out), (OUT_ON, diag, on_out)
            ):
                copies.append(send(boxes.at[peer, rows], arrived.at[me, rows], kind, piece, peer))
        else:
            gathered[me, rows] = result
            near_out.append(send(gathered.at[me, rows], gathered.at[me, rows], OUT_NEAR, piece, near))
            far_out.append(send(gathered.at[me, rows], gathered.at[me, rows], OUT_FAR, piece, far))
    yield
    for piece, rows in enumerate(pieces):
        far_out[piece].wait_recv()
        if not to_features:
            on_out.append(send(gathered.at[far, rows], gathered.at[far, rows], OUT_ON, piece, near))
    for copy in near_out + on_out:
        copy.wait_recv()
    if to_features:
        boxes, arrived = more
        for source in range(4):
            gathered[:, source * own : (source + 1) * own] = arrived[source].astype(F32).T.astype(gathered.dtype)
    for copy in started:
        copy.wait_send()


def mix_scratch(own, model, to_features):
    boxes = [pltpu.VMEM((4, own, model // 4), BF16)] * 2 if to_features else []
    return [
        pltpu.VMEM((own, model), F32),
        pltpu.VMEM((own, model), F32),
        pltpu.VMEM((3, own, model), BF16),
        pltpu.VMEM((3, own, model), BF16),
        pltpu.SemaphoreType.DMA((2, 6, MIX_SUBS)),
        *boxes,
    ]


def row_mix_kernel(finish, extra, outs, left_t, share, images, left_ref, weight_ref, *refs):
    extra_refs, refs = refs[:extra], refs[extra:]
    if images:
        refs = refs[1:]
    if share:
        share_ref, refs = refs[0], refs[1:]
    (gathered, *out_refs), scratch = refs[:outs], refs[outs:]
    if len(weight_ref.shape) == 3:
        *scratch, held, held_sem = scratch
        copy = fetch(weight_ref, 0, (held, held_sem))
        copy.start()
    near, far, _ = row_peers()
    meet(
        ("row", (near, far)),
        ("col", [col_peer(step) for step in range(1, 4)] if images else ()),
        ("batch", image_peers(2) if share or images == 2 else ()),
    )
    if images:
        *out_refs, weight_all = out_refs
        *scratch, chain_sems, pass_sems = scratch
        chains, swapped = weight_chains(weight_all, images, chain_sems, pass_sems)
        for chain in chains:
            chain.begin(3)
            if swapped:
                chain.each(2, chain.on_block)
    if share:
        *out_refs, share_out = out_refs
        *scratch, got, swap_sems = scratch
        image, half = lax.axis_index("batch"), got.shape[1]
        given = pl.ds(pl.multiple_of((1 - image) * half, 16), half)
        kept = pl.ds(pl.multiple_of(image * half, 16), half)
        swap = image_copy(share_ref.at[:, given], got, swap_sems, 0)
        swap.start()

    def last(total, piece, rows):
        return finish(total, piece, rows, *extra_refs, out_refs)

    if len(weight_ref.shape) == 3:
        copy.wait()
        weight_ref = held
    for stage, _ in enumerate(row_mix_steps(left_ref, weight_ref, gathered, last, left_t, False, scratch)):
        if images and stage == 3:
            for chain in chains:
                chain.hop(3)
    if images:
        for chain in chains:
            chain.end((3,))
            if swapped:
                chain.each(2, swapped)
                chain.each(3, swapped)
    if share:
        swap.wait()
        for place in range(4):
            both = share_ref[place, kept].astype(F32) + got[place].astype(F32)
            share_out[place] = both.astype(BF16)


def fetch(stack_ref, which, scratch):
    return pltpu.make_async_copy(stack_ref.at[which], scratch[0], scratch[1])


def fetch_scratch(stack):
    return [pltpu.VMEM(stack.shape[1:], stack.dtype), pltpu.SemaphoreType.DMA(())]


def row_mix(finish, name, number, left, weight, extra, out_shapes, left_t, share=None, passing=None):
    tokens = left.shape[1] if left_t else left.shape[0]
    model = weight.shape[-1]
    own = tokens // 4
    vmem = pl.BlockSpec(memory_space=pltpu.VMEM)
    shared = share is not None and lax.axis_size("batch") == 2
    specs, outs, scratch = [vmem] * (2 + len(extra)), [*out_shapes], mix_scratch(own, model, False)
    operands = (left, weight, *extra)
    if shared:
        cols, n, _ = share.shape
        specs.append(vmem)
        operands = (*operands, share)
        outs.append(jax.ShapeDtypeStruct((cols, n // 2, model), BF16))
        scratch += [pltpu.VMEM((cols, n // 2, model), BF16), pltpu.SemaphoreType.DMA((2, 1))]
    out_specs = [vmem] * (1 + len(outs))
    alias, images = {}, 0
    if passing is not None:
        images = lax.axis_size("batch")
        alias = {len(operands): len(out_specs)}
        operands = (*operands, passing)
        specs.append(pl.BlockSpec(memory_space=pl.ANY))
        out_specs.append(pl.BlockSpec(memory_space=pl.ANY))
        outs.append(jax.ShapeDtypeStruct(passing.shape, passing.dtype))
        scratch += [pltpu.SemaphoreType.DMA((2, 2, 2, 3)), pltpu.SemaphoreType.DMA((2, 2, 3))]
    if weight.ndim == 3:
        specs[1] = pl.BlockSpec(memory_space=pl.ANY)
        scratch += fetch_scratch(weight)
    results = pl.pallas_call(
        partial(row_mix_kernel, finish, len(extra), 1 + len(outs), left_t, shared, images),
        out_shape=[jax.ShapeDtypeStruct((4, own, model), BF16), *outs],
        in_specs=specs,
        out_specs=out_specs,
        input_output_aliases=alias,
        scratch_shapes=scratch,
        compiler_params=pltpu.CompilerParams(
            collective_id=number, has_side_effects=True, vmem_limit_bytes=48 << 20
        ),
        cost_estimate=pl.CostEstimate(
            flops=2 * tokens * model * model, bytes_accessed=16 * own * model, transcendentals=0
        ),
        name=name,
    )(*operands)
    return results if share is None or shared else (*results, share)


def weight_steps(values_ref, images, scratch, write, joined=False):
    boxes, arrived, other, sems = scratch
    me, part = lax.axis_index("row"), boxes.shape[2]
    for place in range(4):
        boxes[place] = values_ref[:, place * part : (place + 1) * part]
    arrived[me] = boxes[me]
    copies = []
    for order, peer in enumerate(row_peers()):
        copy = pltpu.make_async_remote_copy(
            src_ref=boxes.at[peer],
            dst_ref=arrived.at[me],
            send_sem=sems.at[0, order],
            recv_sem=sems.at[1, order],
            device_id={"row": peer},
            device_id_type=MESH,
        )
        copy.start()
        copies.append(copy)
    yield
    for copy in copies:
        copy.wait()
    if images == 2:
        swap = pltpu.make_async_remote_copy(
            src_ref=arrived,
            dst_ref=other,
            send_sem=sems.at[0, 3],
            recv_sem=sems.at[1, 3],
            device_id={"batch": 1 - lax.axis_index("batch")},
            device_id_type=MESH,
        )
        swap.start()
        yield
        swap.wait()
        for place in range(4):
            if joined:
                write(place, arrived[place].astype(F32), other[place].astype(F32))
            else:
                write(place, arrived[place].astype(F32) + other[place].astype(F32))
    else:
        yield
        for place in range(4):
            write(place, arrived[place].astype(F32))


def weight_scratch(n, part):
    return [*[pltpu.VMEM((4, n, part), BF16)] * 3, pltpu.SemaphoreType.DMA((2, 4))]


def image_peers(images):
    me = lax.axis_index("batch")
    return [lax.rem(me + step, images) for step in range(1, images)]


def sum_steps(total, axes, scratch):
    *slots, sends, recvs = scratch
    for order, (name, size) in enumerate(axes):
        me, slot = lax.axis_index(name), slots[order]
        slot[me] = total[...]
        copies = []
        for step in range(1, size):
            copy = pltpu.make_async_remote_copy(
                src_ref=total,
                dst_ref=slot.at[me],
                send_sem=sends.at[order, step],
                recv_sem=recvs.at[order, step],
                device_id={name: lax.rem(me + step, size)},
                device_id_type=MESH,
            )
            copy.start()
            copies.append(copy)
        yield
        for copy in copies:
            copy.wait()
        whole = slot[0]
        for source in range(1, size):
            whole = whole + slot[source]
        total[...] = whole


def sum_scratch(rows, axes):
    most = max(size for _, size in axes)
    return [
        *[pltpu.VMEM((size, rows, 128), F32) for _, size in axes],
        *[pltpu.SemaphoreType.DMA((len(axes), most))] * 2,
    ]


def column_steps(images, grad_ref, normed_ref, out, scratch):
    keep, give, got, box, arrived, sems, swap_sems = scratch
    image, rows = lax.axis_index("batch"), out.shape[0]
    shared = images == 2
    swaps = {}
    for step in (1, 2, 3, 0):
        keep[step] = mm(grad_ref[col_peer(step)], normed_ref[...])
        if shared:
            give[step] = keep[step, pl.ds(half_start(1 - image), rows)].astype(BF16)
            swaps[step] = image_copy(give.at[step], got.at[step], swap_sems, step)
            swaps[step].start()
    yield

    def total(step):
        if not shared:
            return keep[step]
        swaps[step].wait()
        return keep[step, pl.ds(half_start(image), rows)] + got[step].astype(F32)

    copies = []
    for step in range(1, 4):
        box[step - 1] = total(step).astype(BF16)
        copy = col_copy(box.at[step - 1], arrived.at[step - 1], sems, 0, step)
        copy.start()
        copies.append(copy)
    yield
    whole = total(0)
    for step, copy in enumerate(copies):
        copy.wait()
        whole = whole + arrived[step].astype(F32)
    out[...] = whole.astype(BF16)


def column_scratch(n, rows, model):
    return [
        pltpu.VMEM((4, n, model), F32),
        *[pltpu.VMEM((4, rows, model), BF16)] * 2,
        *[pltpu.VMEM((3, rows, model), BF16)] * 2,
        pltpu.SemaphoreType.DMA((2, 1, 4)),
        pltpu.SemaphoreType.DMA((2, 4)),
    ]


EARLY_ROWS, TABLE_ROWS, BIAS_ROWS, LAST_ROWS = 80, 160, 32, 24


def tail_kernel(
    axes,
    qkv_grad_ref, grads_ref, weight_qkv_ref, normed1_ref, first_ref, middle_grad_ref, gain_ref,
    fc1_ref, proj_ref, early_ref, table_ref, bias_ref, patches_out, qkv_out, fc1_out, proj_out, tables_out, small, *rest,
):
    vector_outs, (sums1, qkv_rows, *scratch) = rest[:6], rest[6:]
    col_scratch, scratch = scratch[:7], scratch[7:]
    mix, qkv_scratch, fc1_scratch, sum_parts = scratch[:7], scratch[7:11], scratch[11:15], scratch[15:20]
    proj_rows, proj_box, proj_sems, fc1_rows, *proj_scratch = scratch[20:]
    row, col = lax.axis_index("row"), lax.axis_index("col")
    images = dict(axes)["batch"]
    meet(
        ("row", row_peers()),
        ("col", [col_peer(step) for step in range(1, 4)]),
        ("batch", image_peers(images)),
    )

    def finish1(total, piece, rows):
        return last_finish(total, piece, rows, gain_ref, first_ref, middle_grad_ref, (None, sums1))

    image = lax.axis_index("batch")
    shared = images == 2

    def write_fc1(place, values, others=None):
        n = values.shape[0]
        if others is None:
            fc1_rows[place * n : (place + 1) * n] = values
        else:
            fc1_rows[pl.ds(pl.multiple_of((2 * place + image) * n, 8), n)] = values
            fc1_rows[pl.ds(pl.multiple_of((2 * place + 1 - image) * n, 8), n)] = others

    def write_proj(place, values):
        proj_out[place] = values

    def proj_steps():
        copies = []
        for step in range(1, 4):
            copies.append(col_copy(proj_ref.at[col_peer(step)], proj_box.at[col], proj_sems, 0, step))
            copies[-1].start()
        proj_box[col] = proj_ref[col]
        yield
        for copy in copies:
            copy.wait()
        total = proj_box[0].astype(F32)
        for source in range(1, 4):
            total = total + proj_box[source].astype(F32)
        proj_rows[...] = total.astype(BF16)
        yield from weight_steps(proj_rows, images, proj_scratch, write_proj)

    head_grads = []

    def write_qkv(place, values, others=None):
        if others is not None:
            first, second = jnp.where(image == 0, values, others), jnp.where(image == 0, others, values)
            values = jnp.concatenate([first[: 3 * HEAD_DIM - HALF_GRAD], second], 0)
        head_grads.append(values)

    qkv_sum = column_steps(images, grads_ref, normed1_ref, qkv_rows, col_scratch)
    patches = row_mix_steps(qkv_grad_ref, weight_qkv_ref, patches_out, finish1, True, True, mix)
    fc1 = weight_steps(fc1_ref, images, fc1_scratch, write_fc1, shared)
    qkv = weight_steps(qkv_rows, images, qkv_scratch, write_qkv, shared)
    sums = sum_steps(small, axes, sum_parts)

    def go(*steps):
        for step in steps:
            next(step, None)

    proj = proj_steps()
    go(proj, qkv_sum, patches, patches, patches, proj, qkv_sum, patches)

    small[0:EARLY_ROWS] = early_ref[...]
    at = EARLY_ROWS
    for half in range(2):
        small[at : at + TABLE_ROWS // 2] = table_ref[:, half * 128 : (half + 1) * 128]
        at += TABLE_ROWS // 2
    place = lax.broadcasted_iota(jnp.int32, (BIAS_ROWS, 128), 0) - 2 * (col * 4 + row)
    small[at : at + BIAS_ROWS] = jnp.where(
        place == 0, bias_ref[0:1], jnp.where(place == 1, bias_ref[1:2], 0.0)
    )
    at += BIAS_ROWS
    lines = sums1.shape[1] // 128
    last = [sums1[i : i + 1, j * 128 : (j + 1) * 128] for i in range(2) for j in range(lines)]
    spare = jnp.zeros((LAST_ROWS - len(last), 128), F32)
    small[at : at + LAST_ROWS] = jnp.concatenate([*last, spare], 0)

    go(sums, fc1, proj, qkv_sum, qkv, sums, patches, fc1, proj, sums, qkv, fc1, sums, qkv)
    firsts = [lines * i for i in (5, 6, 7, 4)] + [EARLY_ROWS + TABLE_ROWS + BIAS_ROWS + lines * i for i in range(2)]
    part = vector_outs[0].shape[0]
    for first, out in zip(firsts, vector_outs):
        whole = jnp.concatenate([small[first + i : first + i + 1] for i in range(lines)], 1)
        mine = whole[:, :part]
        for place in range(1, 4):
            mine = jnp.where(row == place, whole[:, place * part : (place + 1) * part], mine)
        out[...] = mine.reshape(part)
    fc1_out[...] = fc1_rows[...].T
    flip = backwards(2 * GRID, 2 * GRID - 1)
    for half in range(2):
        table = small[EARLY_ROWS + half * HEAD_DIM : EARLY_ROWS + (half + 1) * HEAD_DIM]
        tables_out[half] = sum(mm(term, flip) for term in split(table, 3))
    for kind in range(3):
        rows = slice(kind * HEAD_DIM, (kind + 1) * HEAD_DIM)
        qkv_out[kind] = jnp.concatenate([values[rows] for values in head_grads], 0).T


def tail(
    qkv_grad, weight_qkv, normed1, first, middle_grad, gain, fc1, proj, early, table, bias
):
    cols, n, tokens = qkv_grad.shape
    model = weight_qkv.shape[1]
    own, part = tokens // 4, model // 4
    shared = lax.axis_size("batch") == 2
    rows = HALF_GRAD if shared else n
    units = fc1.shape[0] * (2 if shared else 1)
    axes = tuple((name, lax.axis_size(name)) for name in ("row", "batch", "col"))
    small_rows = EARLY_ROWS + TABLE_ROWS + BIAS_ROWS + LAST_ROWS
    vmem = pl.BlockSpec(memory_space=pltpu.VMEM)
    return pl.pallas_call(
        partial(tail_kernel, axes),
        in_specs=[vmem] * 12,
        out_specs=[vmem] * 12,
        out_shape=[
            jax.ShapeDtypeStruct((part, tokens), F32),
            jax.ShapeDtypeStruct((3, part, 4 * HEAD_DIM), F32),
            jax.ShapeDtypeStruct((part, 4 * units), F32),
            jax.ShapeDtypeStruct((4, proj.shape[1], part), F32),
            jax.ShapeDtypeStruct((2, HEAD_DIM, 2 * GRID - 1), F32),
            jax.ShapeDtypeStruct((small_rows, 128), F32),
            *[jax.ShapeDtypeStruct((part,), F32)] * 6,
        ],
        scratch_shapes=[
            pltpu.VMEM((3, model), F32),
            pltpu.VMEM((rows, model), BF16),
            *column_scratch(n, rows, model),
            *mix_scratch(own, model, True),
            *weight_scratch(rows, part),
            *weight_scratch(fc1.shape[0], part),
            *sum_scratch(small_rows, axes),
            pltpu.VMEM(proj.shape[1:], BF16),
            pltpu.VMEM(proj.shape, BF16),
            pltpu.SemaphoreType.DMA((2, 1, 4)),
            pltpu.VMEM((4 * units, part), F32),
            *weight_scratch(proj.shape[1], part),
        ],
        compiler_params=pltpu.CompilerParams(
            collective_id=3, has_side_effects=True, vmem_limit_bytes=60 << 20
        ),
        name="tail",
    )(
        qkv_grad.reshape(cols * n, tokens), qkv_grad, weight_qkv, normed1, first, middle_grad, gain,
        fc1, proj, early, table, bias,
    )


HIDDEN = 256
ROWS = 256


def hidden_kernel(x_ref, w1_ref, bias_ref, cot_ref, w2_ref, act_ref, grad_ref, bias_grad_ref):
    total = None
    for start in range(0, x_ref.shape[0], ROWS):
        rows = slice(start, start + ROWS)
        preact = mm_nt(x_ref[rows], w1_ref[...]) + bias_ref[...]
        act_grad = mm_nt(cot_ref[rows], w2_ref[...])
        below = 0.5 + 0.5 * lax.erf(preact * (0.5**0.5))
        density = jnp.exp(preact * preact * -0.5) * ((2 * math.pi) ** -0.5)
        act_ref[rows] = (preact * below).astype(BF16)
        grad = (act_grad * (below + preact * density)).astype(BF16)
        grad_ref[rows] = grad
        part = jnp.sum(grad.astype(F32), 0, keepdims=True)
        total = part if total is None else total + part
    bias_grad_ref[...] = total


def feed_forward(x, weights, bias, cotangent):
    tokens, model = x.shape
    hidden = weights.shape[1]
    step = HIDDEN if hidden % HIDDEN == 0 else hidden
    whole = pl.BlockSpec((tokens, model), lambda i: (0, 0), pipeline_mode=pl.Buffered(1))
    first, second = [pl.BlockSpec((None, step, model), lambda i, j=j: (j, i, 0)) for j in range(2)]
    vector = pl.BlockSpec((1, step), lambda i: (0, i))
    columns = pl.BlockSpec((tokens, step), lambda i: (0, i))
    return pl.pallas_call(
        hidden_kernel,
        grid=(hidden // step,),
        in_specs=[whole, first, vector, whole, second],
        out_specs=[columns, columns, vector],
        out_shape=[
            jax.ShapeDtypeStruct((tokens, hidden), BF16),
            jax.ShapeDtypeStruct((tokens, hidden), BF16),
            jax.ShapeDtypeStruct((1, hidden), F32),
        ],
        compiler_params=pltpu.CompilerParams(vmem_limit_bytes=40 << 20),
        cost_estimate=pl.CostEstimate(
            flops=4 * tokens * hidden * model,
            bytes_accessed=4 * (tokens + hidden) * model + 4 * tokens * hidden,
            transcendentals=2 * tokens * hidden,
        ),
        name="feed_forward",
    )(x, weights, bias, cotangent, weights)


def table_scratch():
    return [pltpu.VMEM((HEAD_DIM, 4 * GRID), BF16), pltpu.VMEM((4 * GRID, HEAD_DIM), BF16)]


def attention(qkv, height, span, cotangent, weights):
    count, _, width = qkv.shape
    tokens = count * width
    images = lax.axis_size("batch")
    vmem = pl.BlockSpec(memory_space=pltpu.VMEM)
    return pl.pallas_call(
        partial(attend_kernel, images),
        in_specs=[*[vmem] * 4, pl.BlockSpec(memory_space=pl.ANY)],
        out_specs=[*[vmem] * 5, pl.BlockSpec(memory_space=pl.ANY)],
        out_shape=[
            jax.ShapeDtypeStruct((count, HEAD_DIM, width), BF16),
            jax.ShapeDtypeStruct(qkv.shape, BF16),
            jax.ShapeDtypeStruct((count, HEAD_DIM, width), F32),
            jax.ShapeDtypeStruct((count, 8, width), F32),
            jax.ShapeDtypeStruct((width, 4 * cotangent.shape[0]), BF16),
            jax.ShapeDtypeStruct((2, count, *weights.shape[1:]), BF16),
        ],
        scratch_shapes=[
            pltpu.VMEM((count, width, 256), BF16),
            pltpu.VMEM((count, 256, width), BF16),
            pltpu.VMEM((count, HEAD_DIM, width), F32),
            pltpu.VMEM((count, 8, width), F32),
            pltpu.VMEM((count, 8, width), F32),
            pltpu.VMEM((count, HEAD_DIM, width), BF16),
            pltpu.SemaphoreType.DMA((2, 3, 4)),
            pltpu.VMEM((4, *cotangent.shape), BF16),
            pltpu.SemaphoreType.DMA((2, 1, 3)),
            pltpu.SemaphoreType.DMA((2,)),
            pltpu.SemaphoreType.DMA((2, 2, 2, 3)),
            pltpu.SemaphoreType.DMA((2, 2, 3)),
            *table_scratch(),
        ],
        compiler_params=pltpu.CompilerParams(
            collective_id=5, has_side_effects=True, vmem_limit_bytes=48 << 20
        ),
        cost_estimate=pl.CostEstimate(
            flops=2 * tokens * tokens * 512,
            bytes_accessed=6 * tokens * HEAD_DIM * 2,
            transcendentals=tokens * tokens,
        ),
        name="attend",
    )(qkv, height, span, cotangent, weights)


def attention_back(qkv, height, span, grad, exact, stat, fc2, activated, weights, middle, bias_fc2):
    count, _, width = qkv.shape
    tokens = count * width
    images, part = lax.axis_size("batch"), fc2.shape[1] // 4
    vmem = pl.BlockSpec(memory_space=pltpu.VMEM)
    return pl.pallas_call(
        partial(attend_back_kernel, images),
        in_specs=[*[vmem] * 8, pl.BlockSpec(memory_space=pl.ANY), vmem, vmem],
        out_specs=[vmem] * 5,
        out_shape=[
            jax.ShapeDtypeStruct((count, 3 * HEAD_DIM, width), BF16),
            jax.ShapeDtypeStruct((HEAD_DIM, 4 * GRID), F32),
            jax.ShapeDtypeStruct((2, 128), F32),
            jax.ShapeDtypeStruct((part, 4 * fc2.shape[0]), F32),
            jax.ShapeDtypeStruct((part, width), BF16),
        ],
        scratch_shapes=[
            *table_scratch(),
            *fetch_scratch(weights),
            pltpu.VMEM((384, 128), F32),
            pltpu.VMEM((count, HEAD_DIM, width), BF16),
            pltpu.VMEM((count, width, 256), BF16),
            pltpu.VMEM((count, 256, width), BF16),
            pltpu.VMEM((count, width, 128), BF16),
            pltpu.VMEM((count, width, 128), F32),
            pltpu.VMEM((count, width, 128), F32),
            pltpu.VMEM((count, 256, width), F32),
            pltpu.VMEM((count, 256, width), BF16),
            pltpu.VMEM((count, 128, width), BF16),
            pltpu.VMEM((count, width, 128), BF16),
            pltpu.VMEM((count, width, 128), BF16),
            pltpu.VMEM((count, 3 * HEAD_DIM, width), BF16),
            pltpu.SemaphoreType.DMA((2, 3, 4)),
            *weight_scratch(fc2.shape[0], part),
            *mix_scratch(*middle.shape, True),
        ],
        compiler_params=pltpu.CompilerParams(
            collective_id=4, has_side_effects=True, vmem_limit_bytes=62 << 20
        ),
        cost_estimate=pl.CostEstimate(
            flops=2 * tokens * tokens * 1280,
            bytes_accessed=12 * tokens * HEAD_DIM * 2,
            transcendentals=tokens * tokens,
        ),
        name="attend_back",
    )(qkv, height, span, grad, exact, stat, fc2, activated, weights, middle, bias_fc2)


def moments(values):
    center = jnp.mean(values, -1, keepdims=True)
    spread = jnp.mean(values * values, -1, keepdims=True)
    return center, lax.rsqrt(spread - center * center + EPSILON)


def shards(
    patches,
    qkv_weight,
    qv_bias,
    proj_weight,
    proj_bias,
    norm1_gain,
    norm1_shift,
    norm2_gain,
    norm2_shift,
    fc1_weight,
    fc1_bias,
    fc2_weight,
    fc2_bias,
    height_table,
    width_table,
    out_grad,
):
    rows, cols = lax.axis_size("row"), lax.axis_size("col")
    row, col = lax.axis_index("row"), lax.axis_index("col")
    width = patches.shape[1]
    part = patches.shape[2]
    model = part * rows
    own = width // rows
    hidden = fc1_bias.shape[0] // rows
    head = HEAD_DIM

    images = lax.axis_size("batch")

    local_qkv = qkv_weight.reshape(part, 3, rows, head).transpose(2, 1, 3, 0).reshape(rows, 3 * head, part)
    qkv, normed1, first_own, weight_qkv, weight_proj, local_rest, vectors, columns = start(
        patches[0].T,
        local_qkv,
        proj_weight.reshape(rows, head, part),
        fc1_weight,
        fc2_weight.T,
        qv_bias,
        fc1_bias,
        norm1_gain,
        norm1_shift,
        norm2_gain,
        norm2_shift,
        proj_bias,
        fc2_bias,
    )
    gain1, shift1, gain2, shift2, bias_proj, bias_fc2 = [vectors[i] for i in range(6)]
    weight_qkv = weight_qkv.reshape(cols * 3 * head, model)
    bias_fc1 = columns[:, 0, 256:].reshape(cols * hidden)

    height, span = height_table.T, width_table.T

    merged, qkv, exact, stat, cotangent, weights = attention(
        qkv, height, span, out_grad[0].T, local_rest.reshape(2, hidden, model)
    )
    weight_proj = weight_proj.reshape(cols * head, model)
    merged = merged.reshape(cols * head, width)

    def contract_rows(left, right):
        return lax.dot_general(left, right, (((0,), (0,)), ((), ())), preferred_element_type=F32)

    def sum_columns(values):
        return lax.psum_scatter(values, "col", scatter_dimension=0, tiled=False)

    def tokens_of_row(values):
        return lax.dynamic_slice_in_dim(values, row * own, own, 0)

    own_shape = (own, model)
    vec2 = jnp.stack([gain2, shift2, bias_proj])
    normed2, middle, weights = row_mix(
        forward_finish, "middle_and_norm2", 1, merged, weight_proj,
        (vec2, first_own), [jax.ShapeDtypeStruct(own_shape, F32)], True, None, weights,
    )
    normed2 = normed2.reshape(width, model)
    weights = weights.reshape(2, cols * hidden, model)
    activated, preact_grad, fc1_bias_part = feed_forward(normed2, weights, bias_fc1[None], cotangent)
    fc2_grad = contract_rows(activated, cotangent).astype(BF16)
    fc2_grad, preact_grad = lax.optimization_barrier((fc2_grad, preact_grad))
    fc1_grad = contract_rows(preact_grad, normed2).astype(BF16).reshape(cols, hidden, model)

    own_and_sums = [jax.ShapeDtypeStruct(own_shape, F32), jax.ShapeDtypeStruct((3, model), F32)]
    branch_grad, middle_grad, sums2, fc1_grad = row_mix(
        backward_finish, "middle_grad", 2, preact_grad, weights,
        (vec2, middle, tokens_of_row(cotangent)), own_and_sums, False, fc1_grad,
    )
    branch_grad = branch_grad.reshape(width, model)

    merged_grad = mm_nt(weight_proj, branch_grad).astype(BF16).reshape(cols, head, width)
    proj_grad = mm(merged, branch_grad).astype(BF16)
    fc2_grad = sum_columns(fc2_grad.reshape(cols, hidden, model))
    early = jnp.concatenate(
        [
            lax.dynamic_update_slice(jnp.zeros((rows, cols * hidden), F32), fc1_bias_part, (row, 0)).reshape(-1),
            lax.dynamic_update_slice(
                jnp.zeros((model,), F32), jnp.sum(out_grad[0], 0, dtype=F32), (row * part,)
            ),
            sums2.reshape(-1),
        ]
    ).reshape(-1, 128)
    merged_grad, fc1_grad, proj_grad, fc2_grad, early = lax.optimization_barrier(
        (merged_grad, fc1_grad, proj_grad, fc2_grad, early)
    )
    fc1_grad = sum_columns(fc1_grad)
    qkv_grad, table_grad, bias_grad, fc2_grad, final = attention_back(
        qkv, height, span, merged_grad, exact, stat, fc2_grad, activated, weights, middle, bias_fc2[None]
    )
    input_grad, qkv_weight_grad, fc1_grad, proj_grad, tables, small, *vector_grads = tail(
        qkv_grad, weight_qkv, normed1, first_own, middle_grad, gain1[None],
        fc1_grad, proj_grad.reshape(cols, head, model), early, table_grad, bias_grad,
    )

    def sum_images(values):
        return values if images == 2 else lax.psum(values.astype(BF16), "batch").astype(F32)

    fc2_grad = sum_images(fc2_grad).T
    proj_grad = sum_images(proj_grad).reshape(rows * head, part)
    fc1_grad = sum_images(fc1_grad)
    qkv_weight_grad = sum_images(qkv_weight_grad).transpose(1, 0, 2)

    lines = model // 128
    fc1_bias_grad = small[: 4 * lines].reshape(rows, cols, hidden)
    fc1_bias_grad = lax.dynamic_index_in_dim(fc1_bias_grad, col, 1, keepdims=False).reshape(rows * hidden)
    gain2_grad, shift2_grad, proj_bias_grad, fc2_bias_grad, gain1_grad, shift1_grad = vector_grads
    at = EARLY_ROWS
    at += TABLE_ROWS
    bias_total = small[at : at + BIAS_ROWS].reshape(cols, rows, 2, 128)
    bias_total = lax.dynamic_index_in_dim(bias_total, col, 0, keepdims=False)[:, :, :head]
    bias_total = bias_total.transpose(1, 0, 2).reshape(2, rows * head)

    return (
        final.T[None],
        input_grad.T[None],
        qkv_weight_grad,
        bias_total,
        proj_grad,
        proj_bias_grad,
        gain1_grad,
        shift1_grad,
        gain2_grad,
        shift2_grad,
        fc1_grad,
        fc1_bias_grad,
        fc2_grad,
        fc2_bias_grad,
        tables[0].T,
        tables[1].T,
    )


def solution(mesh):
    in_specs = (
        P("batch", "col", "row"),
        P("row", None, "col"),
        P(None, "col"),
        P("col", "row"),
        P("row"),
        P("row"),
        P("row"),
        P("row"),
        P("row"),
        P("row", "col"),
        P("col"),
        P("col", "row"),
        P("row"),
        P(),
        P(),
        P("batch", "col", "row"),
    )
    out_specs = (
        P("batch", "col", "row"),
        P("batch", "col", "row"),
        P("row", None, "col"),
        P(None, "col"),
        P("col", "row"),
        P("row"),
        P("row"),
        P("row"),
        P("row"),
        P("row"),
        P("row", "col"),
        P("col"),
        P("col", "row"),
        P("row"),
        P(),
        P(),
    )
    return jax.shard_map(shards, mesh=mesh, in_specs=in_specs, out_specs=out_specs, check_vma=False)
```

```python
import math
from functools import partial

import jax
import jax.numpy as jnp
from jax import lax
from jax.experimental import pallas as pl
from jax.experimental.pallas import tpu as pltpu
from jax.sharding import PartitionSpec as P

D = 1280
HEAD_DIM = 80
GRID = 64
EPSILON = 1e-06

LINES = 4
QUERIES = LINES * GRID
KEYS = 512
LOG2E = math.log2(math.e)
SCALE = HEAD_DIM**-0.5
BF16 = jnp.bfloat16
F32 = jnp.float32
MESH = pl.DeviceIdType.MESH


def mm(left, right):
    return jnp.dot(left, right, preferred_element_type=F32)


def mm_nt(left, right):
    return lax.dot_general(left, right, (((1,), (1,)), ((), ())), preferred_element_type=F32)


def split(values, parts):
    terms = []
    for _ in range(parts):
        term = values.astype(BF16)
        terms.append(term)
        values = values - term.astype(F32)
    return terms


def backwards(rows, columns):
    first = lax.broadcasted_iota(jnp.int32, (rows, columns), 0)
    second = lax.broadcasted_iota(jnp.int32, (rows, columns), 1)
    return jnp.where(first + second == 2 * GRID - 2, 1.0, 0.0).astype(BF16)


def fill_tables(height_ref, width_ref, tab_t):
    flip = backwards(2 * GRID - 1, 2 * GRID)
    tab_t[:, : 2 * GRID] = mm(height_ref[...], flip).astype(BF16)
    tab_t[:, 2 * GRID :] = mm(width_ref[...], flip).astype(BF16)


def skew(values, shift):
    n = values.shape[1]
    for bit, rows in ((32, 96), (16, 80), (8, 72)):
        take = jnp.broadcast_to(shift, (rows, n)) & bit
        values = jnp.where(take != 0, values[bit : bit + rows], values[:rows])
    for bit in (4, 2, 1):
        take = jnp.broadcast_to(shift, values.shape) & bit
        values = jnp.where(take != 0, pltpu.roll(values, values.shape[0] - bit, 0), values)
    return values[:GRID]


def unskew(values, shift):
    n = values.shape[1]
    values = jnp.concatenate([values, jnp.zeros((8, n), F32)], 0)
    for bit in (1, 2, 4):
        take = jnp.broadcast_to(shift, values.shape) & bit
        values = jnp.where(take != 0, pltpu.roll(values, bit, 0), values)
    for bit in (8, 16, 32):
        zeros = jnp.zeros((bit, n), F32)
        take = jnp.broadcast_to(shift, (values.shape[0] + bit, n)) & bit
        values = jnp.where(
            take != 0,
            jnp.concatenate([zeros, values], 0),
            jnp.concatenate([values, zeros], 0),
        )
    return values


def token_shifts(step):
    lane = lax.broadcasted_iota(jnp.int32, (1, QUERIES), 1)
    return (GRID - 1) - (step * LINES + lane // GRID), (GRID - 1) - lane % GRID


def query_columns(q, tab, step, tail):
    shift_rows, shift_cols = token_shifts(step)
    both = mm(tab, q)
    rel_rows = skew(both[: 2 * GRID], shift_rows)
    rel_cols = skew(both[2 * GRID :], shift_cols)
    rel = jnp.concatenate([rel_rows, rel_cols], 0) * (1.0 / SCALE)
    return jnp.concatenate([rel.astype(BF16), q, tail], 0)


def col_peer(step):
    me = lax.axis_index("col")
    odd, high = step % 2, step // 2
    return lax.rem(me + odd - 2 * odd * lax.rem(me, 2) + 2 * high, 4)


def col_barrier():
    barrier = pltpu.get_barrier_semaphore()
    for step in range(1, 4):
        pl.semaphore_signal(barrier, device_id={"col": col_peer(step)}, device_id_type=MESH)
    pl.semaphore_wait(barrier, 3)


def col_copy(source, target, sems, kind, step):
    return pltpu.make_async_remote_copy(
        src_ref=source,
        dst_ref=target,
        send_sem=sems.at[0, kind, step],
        recv_sem=sems.at[1, kind, step],
        device_id={"col": col_peer(step)},
        device_id_type=MESH,
    )


class Chain:
    def __init__(self, view, sems, on_block=None):
        self.view, self.sems, self.on_block = view, sems, on_block
        self.me = lax.axis_index("col")

    def copy(self, way, hop):
        block = self.me + (hop - 1) * (2 * way - 1)
        return pltpu.make_async_remote_copy(
            src_ref=self.view(block),
            dst_ref=self.view(block),
            send_sem=self.sems.at[0, way, hop - 1],
            recv_sem=self.sems.at[1, way, hop - 1],
            device_id={"col": lax.rem(self.me + 1 + 2 * way, 4)},
            device_id_type=MESH,
        )

    def sends(self, way, hop):
        if way:
            return jnp.logical_and(self.me > 0, self.me + hop - 1 < 4)
        return jnp.logical_and(self.me < 3, self.me - hop + 1 >= 0)

    def each(self, hop, act):
        for way in range(2):

            @pl.when(self.me + hop < 4 if way else self.me - hop >= 0)
            def _():
                act(self.me + hop * (2 * way - 1), way, hop)

    def start(self, way, hop):
        @pl.when(self.sends(way, hop))
        def _():
            self.copy(way, hop).start()

    def begin(self, hop=1):
        for way in range(2):
            self.start(way, hop)

    def hop(self, hop, last=3, tell=True):
        def arrived(block, way, hop):
            self.copy(way, hop).wait_recv()

        self.each(hop, arrived)
        if hop < last:
            for way in range(2):
                self.start(way, hop + 1)
        if self.on_block and tell:
            self.each(hop, self.on_block)

    def end(self, hops=(1, 2, 3)):
        for hop in hops:
            for way in range(2):

                @pl.when(self.sends(way, hop))
                def _():
                    self.copy(way, hop).wait_send()


def image_copy(source, target, sems, *place):
    return pltpu.make_async_remote_copy(
        src_ref=source,
        dst_ref=target,
        send_sem=sems.at[(0, *place)],
        recv_sem=sems.at[(1, *place)],
        device_id={"batch": 1 - lax.axis_index("batch")},
        device_id_type=MESH,
    )


def weight_chains(weight_all, images, chain_sems, swap_sems):
    image = lax.axis_index("batch")

    def swap_copy(block, way, hop):
        return image_copy(weight_all.at[image, block], weight_all.at[image, block], swap_sems, way, hop - 1)

    def swap(block, way, hop):
        swap_copy(block, way, hop).start()

    def swapped(block, way, hop):
        swap_copy(block, way, hop).wait()

    shared = images == 2
    chains = [
        Chain(lambda i, which=which: weight_all.at[which, i], chain_sems.at[order], swap if shared else None)
        for order, which in enumerate([image] if shared else [0, 1])
    ]
    return chains, swapped if shared else None


HALF = 2 * HEAD_DIM


def half_start(image):
    return pl.multiple_of(image * (3 * HEAD_DIM - HALF_GRAD), 16)


HALF_GRAD = 128


def row_copy(source, target, sems, kind, order, peer):
    return pltpu.make_async_remote_copy(
        src_ref=source,
        dst_ref=target,
        send_sem=sems.at[0, kind, order],
        recv_sem=sems.at[1, kind, order],
        device_id={"row": peer},
        device_id_type=MESH,
    )


def beside(blocks):
    return jnp.concatenate([block.astype(F32) for block in blocks], 1)


def upright(blocks):
    return jnp.concatenate([block.astype(F32) for block in blocks], 0).T


def start_kernel(
    images, patches_ref, qkv_ref, proj_ref, fc1_ref, fc2_ref, qv_bias_ref, fc1_bias_ref, v0, v1, v2, v3, v4, v5,
    qkv_out, normed_out, first_out, weight_out, proj_out, rest_out, vectors_out, columns_out,
    patches_all, parts, rest_parts, rest_own, column_ref, vector_ref, vector_parts, halves, sems, col_sems, chain_sems, swap_sems,
):
    row, col, image = lax.axis_index("row"), lax.axis_index("col"), lax.axis_index("batch")
    near, far, diag = row_peers()
    own = first_out.shape[0]
    shared = images == 2
    meet(
        ("row", (near, far, diag)),
        ("col", [col_peer(step) for step in range(1, 4)]),
        ("batch", image_peers(images) if shared else ()),
    )

    def to_row(source, target, kind):
        copies = [row_copy(source(peer), target, sems, kind, i, peer) for i, peer in enumerate((near, far, diag))]
        for copy in copies:
            copy.start()
        return copies

    n, units = 3 * HEAD_DIM, fc1_ref.shape[1] // 4

    def mine(values, size):
        piece = values[:, :size]
        for place in range(1, 4):
            piece = jnp.where(row == place, values[:, place * size : (place + 1) * size], piece)
        return piece

    bias = mine(qv_bias_ref[...], HEAD_DIM)
    bias = [bias[0:1], jnp.zeros((1, HEAD_DIM), F32), bias[1:2], jnp.zeros((1, 256 - n), F32)]
    bias = jnp.concatenate([*bias, mine(fc1_bias_ref[...].reshape(1, -1), units)], 1)
    column_ref[...] = jnp.broadcast_to(bias, column_ref.shape)
    vectors = [ref[...].reshape(1, -1) for ref in (v0, v1, v2, v3, v4, v5)]
    vector_ref[...] = jnp.concatenate([*vectors, *vectors[:2]], 0)
    weight_copies = to_row(lambda peer: qkv_ref.at[peer], parts.at[row, 0:n], 0)
    weight_copies += to_row(lambda peer: proj_ref.at[peer], parts.at[row, n : n + HEAD_DIM], 4)
    vector_copies = to_row(lambda peer: vector_ref, vector_parts.at[row], 1)
    to_near = row_copy(patches_ref, patches_all.at[row], sems, 2, 0, near)
    to_far = row_copy(patches_ref, patches_all.at[row], sems, 2, 1, far)
    to_near.start()
    column_copies = [col_copy(column_ref, columns_out.at[col], col_sems, 0, step) for step in range(1, 4)]
    for copy in column_copies:
        copy.start()
    parts[row, 0:n] = qkv_ref[row]
    parts[row, n : n + HEAD_DIM] = proj_ref[row]
    vector_parts[row] = vector_ref[...]
    patches_all[row] = patches_ref[...]
    columns_out[col] = column_ref[...]
    for copy in weight_copies:
        copy.wait()
    to_far.start()
    weight = beside([parts[i] for i in range(4)]).astype(BF16)

    def swap_copy(block, way, hop):
        return image_copy(halves.at[image, block], halves.at[image, block], swap_sems, way, hop - 1)

    def swap(block, way, hop):
        swap_copy(block, way, hop).start()

    halves[0, col] = weight[:HALF]
    halves[1, col] = weight[HALF:]
    orders = [image] if shared else [0, 1]
    chains = [
        Chain(lambda i, which=which: halves.at[which, i], chain_sems.at[order], swap if shared else None)
        for order, which in enumerate(orders)
    ]

    def product(block, way=0, hop=0):
        if hop and shared:
            swap_copy(block, way, hop).wait()
        weight_out[block, 0:HALF] = halves[0, block]
        weight_out[block, HALF:] = halves[1, block, 0 : n - HALF]
        proj_out[block] = halves[1, block, n - HALF :]
        bias = jnp.concatenate([columns_out[block][:, 0:256]] * 16, 0).T[:n, 0:1]
        qkv_out[block] = (mm_nt(weight_out[block], normed_out[...]) + bias).astype(BF16)

    for chain in chains:
        chain.begin()
    for copy in vector_copies + column_copies:
        copy.wait()
    vectors_out[...] = beside([vector_parts[i] for i in range(4)])
    to_far.wait_recv()
    pass_on = row_copy(patches_all.at[far], patches_all.at[far], sems, 2, 2, near)
    pass_on.start()
    for which, ref in enumerate((fc1_ref, fc2_ref)):
        for place in range(4):
            block = ref[:, place * units : (place + 1) * units].astype(F32).T
            rest_own[place, which * units : (which + 1) * units] = block.astype(BF16)
    rest_copies = to_row(lambda peer: rest_own.at[peer], rest_parts.at[row], 3)
    rest_parts[row] = rest_own[row]
    for chain in chains:
        chain.hop(1)
    to_near.wait_recv()
    pass_on.wait_recv()
    for start in range(0, normed_out.shape[0], own):
        scaled, _ = normal(upright([patches_all[i, :, start : start + own] for i in range(4)]))
        normed_out[start : start + own] = (scaled * vectors_out[0:1] + vectors_out[1:2]).astype(BF16)
    for chain in chains:
        chain.hop(2)
    product(col)
    chains[0].each(1, product)
    for chain in chains:
        chain.hop(3)
    chains[0].each(2, product)
    mine = pl.ds(pl.multiple_of(row * own, own), own)
    first_out[...] = upright([patches_all[i, :, mine] for i in range(4)]).astype(BF16)
    for copy in rest_copies:
        copy.wait()
    rest_out[...] = beside([rest_parts[i] for i in range(4)]).astype(BF16)
    chains[0].each(3, product)
    for chain in chains:
        chain.end()
    for copy in (to_near, to_far, pass_on):
        copy.wait_send()


def start(patches, local_qkv, local_proj, local_fc1, local_fc2, qv_bias, fc1_bias, *vectors):
    columns = (8, 256 + fc1_bias.shape[0] // 4)
    part, width = patches.shape
    n, model = local_qkv.shape[1], part * 4
    rest = 2 * (local_fc1.shape[1] // 4)
    vmem = pl.BlockSpec(memory_space=pltpu.VMEM)
    return pl.pallas_call(
        partial(start_kernel, lax.axis_size("batch")),
        in_specs=[vmem] * 13,
        out_specs=[vmem] * 8,
        out_shape=[
            jax.ShapeDtypeStruct((4, n, width), BF16),
            jax.ShapeDtypeStruct((width, model), BF16),
            jax.ShapeDtypeStruct((width // 4, model), BF16),
            jax.ShapeDtypeStruct((4, n, model), BF16),
            jax.ShapeDtypeStruct((4, HEAD_DIM, model), BF16),
            jax.ShapeDtypeStruct((rest, model), BF16),
            jax.ShapeDtypeStruct((8, model), F32),
            jax.ShapeDtypeStruct((4, *columns), F32),
        ],
        scratch_shapes=[
            pltpu.VMEM((4, part, width), BF16),
            pltpu.VMEM((4, n + HEAD_DIM, part), BF16),
            *[pltpu.VMEM((4, rest, part), BF16)] * 2,
            pltpu.VMEM(columns, F32),
            pltpu.VMEM((8, part), F32),
            pltpu.VMEM((4, 8, part), F32),
            pltpu.VMEM((2, 4, HALF, model), BF16),
            pltpu.SemaphoreType.DMA((2, 6, 3)),
            pltpu.SemaphoreType.DMA((2, 1, 4)),
            pltpu.SemaphoreType.DMA((2, 2, 2, 3)),
            pltpu.SemaphoreType.DMA((2, 2, 3)),
        ],
        compiler_params=pltpu.CompilerParams(
            collective_id=7, has_side_effects=True, vmem_limit_bytes=48 << 20
        ),
        name="start",
    )(patches, local_qkv, local_proj, local_fc1, local_fc2, qv_bias, fc1_bias, *vectors)


CHAIN_TURNS = (6, 12)


def attend_kernel(
    images, given_ref, height_ref, width_ref, cot_ref, weight_ref,
    merged_ref, qkv_ref, exact_ref, stat_ref, cot_out, cot_own, weight_all,
    kaug, columns, acc, top, total, box, sems, cot_parts, cot_sems, local_sems, chain_sems, swap_sems,
    tab_t, tab_ref,
):
    me = lax.axis_index("col")
    width = given_ref.shape[2]
    blocks = width // QUERIES
    row, image = lax.axis_index("row"), lax.axis_index("batch")
    near, far, diag = row_peers()
    shared = images == 2
    meet(
        ("row", (near, far)),
        ("col", [col_peer(step) for step in range(1, 4)]),
        ("batch", image_peers(images) if shared else ()),
    )

    chains, swapped = weight_chains(weight_all, images, chain_sems, swap_sems)
    keep = [pltpu.make_async_copy(weight_ref.at[i], weight_all.at[i, me], local_sems.at[i]) for i in range(2)]
    for copy in keep:
        copy.start()

    def part_copy(step):
        return col_copy(given_ref.at[col_peer(step)], qkv_ref.at[me], sems, 0, step)

    def merged_copy(step):
        return col_copy(box.at[col_peer(step)], merged_ref.at[me], sems, 1, step)

    for step in (2, 1):
        part_copy(step).start()
    to_near = row_copy(cot_ref, cot_parts.at[row], cot_sems, 0, 0, near)
    to_far = row_copy(cot_ref, cot_parts.at[row], cot_sems, 0, 1, far)
    pass_on = row_copy(cot_parts.at[far], cot_parts.at[far], cot_sems, 0, 2, near)
    to_far.start()
    to_near.start()
    cot_parts[row] = cot_ref[...]
    qkv_ref[me] = given_ref[me]

    pad = jnp.zeros((128 - HEAD_DIM, width), F32)
    token = lax.broadcasted_iota(jnp.int32, (width, 2 * GRID), 0)
    lane = lax.broadcasted_iota(jnp.int32, (width, 2 * GRID), 1)
    tail = jnp.zeros((128 - HEAD_DIM, QUERIES), BF16)
    fill_tables(height_ref, width_ref, tab_t)
    tab_ref[...] = tab_t[...].astype(F32).T.astype(BF16)
    factor = SCALE * LOG2E

    def prepare(part):
        at = token + part * width
        hot = jnp.where(jnp.where(lane < GRID, at // GRID, at % GRID + GRID) == lane, 1.0, 0.0)
        key = qkv_ref[part, HEAD_DIM : 2 * HEAD_DIM]
        kaug[part, :, 0:128] = hot.astype(BF16)
        kaug[part, :, 128:256] = jnp.concatenate([key.astype(F32), pad], 0).T.astype(BF16)
        for block in range(blocks):
            at = slice(block * QUERIES, (block + 1) * QUERIES)
            columns[part, :, at] = query_columns(
                qkv_ref[part, 0:HEAD_DIM, at], tab_ref[...], part * blocks + block, tail
            )
        acc[part] = jnp.zeros((HEAD_DIM, width), F32)
        top[part] = jnp.full((8, width), -1e30, F32)
        total[part] = jnp.zeros((8, width), F32)

    def finish(part):
        whole, best = total[part, 0:1], top[part, 0:1]
        result = acc[part] * (1.0 / whole)
        exact_ref[part] = result
        box[part] = result.astype(BF16)
        stat_ref[part] = jnp.broadcast_to(best + jnp.log2(whole) * (1.0 / factor), (8, width))

    def pair(turn, carry):
        newest = (turn + 15) // 16 + (turn + 12) // 16 + (turn + 7) // 16
        place = turn - newest * newest
        q_step = jnp.where(place < newest, place, newest)
        k_step = jnp.where(place < newest, newest, place - newest)
        q_part, k_part = col_peer(q_step), col_peer(k_step)

        @pl.when(jnp.logical_and(place == 0, newest > 0))
        def _():
            part_copy(newest).wait_recv()

        @pl.when(place == 0)
        def _():
            prepare(col_peer(newest))

        @pl.when(turn == 1)
        def _():
            part_copy(3).start()

        @pl.when(turn == CHAIN_TURNS[0])
        def _():
            for chain in chains:
                chain.begin()

        @pl.when(turn == CHAIN_TURNS[1])
        def _():
            for chain in chains:
                chain.hop(1)
            to_far.wait_recv()
            pass_on.start()

        for block in range(blocks):
            at = slice(block * QUERIES, (block + 1) * QUERIES)
            best, whole, result = top[q_part, 0:1, at], total[q_part, 0:1, at], acc[q_part, :, at]
            for start in range(0, width, KEYS):
                keys = slice(start, start + KEYS)
                scores = mm(kaug[k_part, keys], columns[q_part, :, at])
                new_best = jnp.maximum(best, jnp.max(scores, 0, keepdims=True))
                weights = jnp.exp2((scores - new_best) * factor)
                keep = jnp.exp2((best - new_best) * factor)
                whole = whole * keep + jnp.sum(weights, 0, keepdims=True)
                value = qkv_ref[k_part, 2 * HEAD_DIM : 3 * HEAD_DIM, keys]
                result = result * keep + mm(value, weights.astype(BF16))
                best = new_best
            top[q_part, :, at] = jnp.broadcast_to(best, (8, QUERIES))
            total[q_part, :, at] = jnp.broadcast_to(whole, (8, QUERIES))
            acc[q_part, :, at] = result

        @pl.when(jnp.logical_and(turn >= 9, jnp.logical_or(place < 3, turn == 15)))
        def _():
            finish(q_part)

        @pl.when(jnp.logical_and(turn >= 9, jnp.logical_or(jnp.logical_and(turn > 9, place < 3), turn == 15)))
        def _():
            merged_copy(q_step).start()

        return carry

    for copy in keep:
        copy.wait()
    lax.fori_loop(0, 16, pair, 0)
    for chain in chains:
        chain.hop(2, 2, False)
    to_near.wait_recv()
    pass_on.wait_recv()
    for start in range(0, width, QUERIES):
        rows = slice(start, start + QUERIES)
        cot_out[rows] = upright([cot_parts[i, :, rows] for i in range(4)]).astype(BF16)
    own = cot_own.shape[0]
    cot_own[...] = cot_out[pl.ds(pl.multiple_of(row * own, own), own)]
    merged_ref[me] = box[me]
    for chain in chains:
        chain.end((1, 2))
        if shared:
            chain.each(1, swapped)
    for copy in (to_near, to_far, pass_on):
        copy.wait_send()
    for step in range(1, 4):
        part_copy(step).wait_send()
        merged_copy(step).wait()


GRADS, QUERY_OUT, KEY_OUT = range(3)
KEY_ROWS = slice(HEAD_DIM, 3 * HEAD_DIM)


def attend_back_kernel(
    images, qkv_ref, height_ref, width_ref, given_ref, exact_ref, stat_ref, fc2_ref,
    activated_ref, weights_ref, middle_ref, bias_fc2_ref,
    out_ref, tab_grad_ref, bias_out, fc2_out, block_out,
    tab_t_ref, tab_ref, held, held_sem, bias_ref, grads, kaug, kaug_t, vaug, key_sum, value_sum, spread, columns,
    grad_columns, grad_rows, q_rows, box, sems, *weight_parts,
):
    me = lax.axis_index("col")
    width = qkv_ref.shape[2]
    blocks = width // QUERIES
    weight_copy = fetch(weights_ref, 1, (held, held_sem))
    weight_copy.start()
    meet(
        ("row", row_peers()),
        ("col", [col_peer(step) for step in range(1, 4)]),
        ("batch", image_peers(images) if images == 2 else ()),
    )

    fc2_grads = []

    def write_fc2(place, values):
        fc2_grads.append(values)

    fc2 = weight_steps(fc2_ref, images, weight_parts[:4], write_fc2)

    def finish_block(total, piece, rows):
        return middle_ref[rows] + (total + bias_fc2_ref[0:1])

    block = row_mix_steps(activated_ref, held, block_out, finish_block, False, True, weight_parts[4:])

    def grad_copy(step):
        return col_copy(given_ref.at[col_peer(step)], grads.at[me], sems, GRADS, step)

    def query_copy(step):
        at = col_peer(step)
        return col_copy(box.at[at, 0:HEAD_DIM], out_ref.at[me, 0:HEAD_DIM], sems, QUERY_OUT, step)

    def key_copy(step):
        at = col_peer(step)
        return col_copy(box.at[at, KEY_ROWS], out_ref.at[me, KEY_ROWS], sems, KEY_OUT, step)

    for step in range(1, 4):
        grad_copy(step).start()
    next(fc2)
    grads[me] = given_ref[me]

    fill_tables(height_ref, width_ref, tab_t_ref)
    tab_ref[...] = tab_t_ref[...].astype(F32).T.astype(BF16)
    tail_row = lax.broadcasted_iota(jnp.int32, (128 - HEAD_DIM, width), 0)
    pad = jnp.where(tail_row < 3, 1.0, 0.0)
    token = lax.broadcasted_iota(jnp.int32, (width, 2 * GRID), 0)
    lane = lax.broadcasted_iota(jnp.int32, (width, 2 * GRID), 1)

    def fill(part, carry):
        at = token + part * width
        hot = jnp.where(jnp.where(lane < GRID, at // GRID, at % GRID + GRID) == lane, 1.0, 0.0)
        key, value = qkv_ref[part, HEAD_DIM : 2 * HEAD_DIM], qkv_ref[part, 2 * HEAD_DIM : 3 * HEAD_DIM]
        kaug[part, :, 0:128] = hot.astype(BF16)
        kaug[part, :, 128:256] = jnp.concatenate([key.astype(F32), pad], 0).T.astype(BF16)
        vaug[part] = jnp.concatenate([value.astype(F32), pad], 0).T.astype(BF16)
        kaug_t[part, 0:128] = hot.T.astype(BF16)
        kaug_t[part, 128:208] = key
        kaug_t[part, 208:256] = jnp.zeros((48, width), BF16)
        return carry

    lax.fori_loop(0, 4, fill, 0)
    key_sum[...] = jnp.zeros_like(key_sum)
    value_sum[...] = jnp.zeros_like(value_sum)
    spread[...] = jnp.zeros_like(spread)
    tab_grad_ref[...] = jnp.zeros_like(tab_grad_ref)
    bias_ref[...] = jnp.zeros_like(bias_ref)

    block_row = lax.broadcasted_iota(jnp.int32, (128 - HEAD_DIM, QUERIES), 0)

    def tail(row):
        out = jnp.zeros((128 - HEAD_DIM, QUERIES), F32)
        for place, term in enumerate(split(row, 3)):
            out = jnp.where(block_row == place, term.astype(F32), out)
        return out.astype(BF16)

    zero_tail = jnp.zeros((128 - HEAD_DIM, QUERIES), F32)

    def prepare(part):
        for block in range(blocks):
            at = slice(block * QUERIES, (block + 1) * QUERIES)
            q, grad = qkv_ref[part, 0:HEAD_DIM, at], grads[part, :, at]
            inner = jnp.sum(grad.astype(F32) * exact_ref[part, :, at], 0, keepdims=True)
            columns[part, :, at] = query_columns(
                q, tab_ref[...], part * blocks + block, tail(-stat_ref[part, 0:1, at])
            )
            grad_columns[part, :, at] = jnp.concatenate([grad, tail(-inner)], 0)
            grad_rows[part, at] = jnp.concatenate([grad.astype(F32), zero_tail], 0).T.astype(BF16)
            q_rows[part, at] = jnp.concatenate([q.astype(F32), zero_tail], 0).T.astype(BF16)

    def add_bias(first, values):
        total = jnp.sum(values.astype(F32), 1, keepdims=True)
        bias_ref[first : first + values.shape[0]] += jnp.broadcast_to(total, (values.shape[0], 128))

    def finish_queries(part):
        for block in range(blocks):
            at = slice(block * QUERIES, (block + 1) * QUERIES)
            rows, cols = token_shifts(part * blocks + block)
            lifted = jnp.concatenate(
                [unskew(spread[part, 0:GRID, at], rows), unskew(spread[part, GRID : 2 * GRID, at], cols)], 0
            )
            high, low = split(lifted, 2)
            query_grad = spread[part, 128 : 128 + HEAD_DIM, at] * SCALE
            query_grad = query_grad + (mm(tab_t_ref[...], high) + mm(tab_t_ref[...], low))
            q = qkv_ref[part, 0:HEAD_DIM, at]
            tab_grad_ref[...] += mm_nt(q, high) + mm_nt(q, low)
            box[part, 0:HEAD_DIM, at] = query_grad.astype(BF16)
        add_bias(0, box[part, 0:HEAD_DIM])

    def finish_keys(part):
        key_grad = (key_sum[part] * SCALE).T[:HEAD_DIM].astype(BF16)
        value_grad = value_sum[part].T[:HEAD_DIM].astype(BF16)
        box[part, HEAD_DIM : 2 * HEAD_DIM] = key_grad
        box[part, 2 * HEAD_DIM : 3 * HEAD_DIM] = value_grad
        add_bias(HEAD_DIM, key_grad)
        add_bias(2 * HEAD_DIM, value_grad)

    def pair(turn, carry):
        later = jnp.maximum(turn - 4, 0)
        q_step = jnp.where(turn < 4, 0, 1 + later % 3)
        k_step = jnp.where(turn < 4, 3 - turn, 3 - later // 3)
        q_part, k_part = col_peer(q_step), col_peer(k_step)

        @pl.when(jnp.logical_and(turn >= 4, turn < 7))
        def _():
            grad_copy(q_step).wait_recv()

        @pl.when(jnp.logical_or(turn == 0, jnp.logical_and(turn >= 4, turn < 7)))
        def _():
            prepare(q_part)

        for block in range(blocks):
            at = slice(block * QUERIES, (block + 1) * QUERIES)
            total = None
            for start in range(0, width, KEYS):
                keys = slice(start, start + KEYS)
                weights = jnp.exp2(mm(kaug[k_part, keys], columns[q_part, :, at]) * (SCALE * LOG2E))
                score_grad = (weights * mm(vaug[k_part, keys], grad_columns[q_part, :, at])).astype(BF16)
                value_sum[k_part, keys] += mm(weights.astype(BF16), grad_rows[q_part, at])
                key_sum[k_part, keys] += mm(score_grad, q_rows[q_part, at])
                result = mm(kaug_t[k_part, :, keys], score_grad)
                total = result if total is None else total + result
            spread[q_part, :, at] += total

        keys_done = jnp.logical_and(turn >= 4, q_step == 3)
        queries_done = jnp.logical_or(turn == 3, turn >= 13)

        @pl.when(keys_done)
        def _():
            finish_keys(k_part)

        @pl.when(jnp.logical_and(keys_done, k_step > 0))
        def _():
            key_copy(k_step).start()

        @pl.when(queries_done)
        def _():
            finish_queries(q_part)

        @pl.when(jnp.logical_and(queries_done, q_step > 0))
        def _():
            query_copy(q_step).start()

        return carry

    weight_copy.wait()
    next(block)
    next(block)
    lax.fori_loop(0, 4, pair, 0)
    next(block)
    next(block)
    next(fc2)
    lax.fori_loop(4, 9, pair, 0)
    next(block, None)
    next(fc2, None)
    fc2_out[...] = jnp.concatenate(fc2_grads, 0).T
    lax.fori_loop(9, 16, pair, 0)
    out_ref[me] = box[me]
    for step in range(1, 4):
        grad_copy(step).wait_send()
        query_copy(step).wait()
        key_copy(step).wait()
    bias_out[0:1] = bias_ref[0:128].T[0:1]
    bias_out[1:2] = bias_ref[2 * HEAD_DIM : 2 * HEAD_DIM + 128].T[0:1]


MIX_SUBS = 2
TO_NEAR, PASS_ON, TO_FAR, OUT_NEAR, OUT_FAR, OUT_ON = range(6)


def normal(values):
    center, inv = moments(values)
    return (values - center) * inv, inv


def normal_back(grad, scaled, inv, gain):
    grad = grad * gain
    return inv * (
        grad
        - jnp.mean(grad, -1, keepdims=True)
        - scaled * jnp.mean(grad * scaled, -1, keepdims=True)
    )


def add_sums(sums_ref, piece, terms):
    for place, term in enumerate(terms):
        total = jnp.sum(term, 0, keepdims=True)
        if piece:
            total = total + sums_ref[place : place + 1]
        sums_ref[place : place + 1] = total


def forward_finish(total, piece, rows, vec_ref, first_ref, out_refs):
    middle = first_ref[rows].astype(F32) + (total + vec_ref[2:3])
    out_refs[0][rows] = middle
    scaled, _ = normal(middle)
    return (scaled * vec_ref[0:1] + vec_ref[1:2]).astype(BF16)


def backward_finish(total, piece, rows, vec_ref, first_ref, add_ref, out_refs):
    scaled, inv = normal(first_ref[rows].astype(F32))
    result = add_ref[rows].astype(F32) + normal_back(total, scaled, inv, vec_ref[0:1])
    branch = result.astype(BF16)
    out_refs[0][rows] = result
    add_sums(out_refs[1], piece, (total * scaled, total, branch.astype(F32)))
    return branch


def last_finish(total, piece, rows, vec_ref, first_ref, add_ref, out_refs):
    scaled, inv = normal(first_ref[rows].astype(F32))
    add_sums(out_refs[1], piece, (total * scaled, total))
    return add_ref[rows] + normal_back(total, scaled, inv, vec_ref[0:1])


def row_peers():
    me = lax.axis_index("row")
    near = me + 1 - 2 * lax.rem(me, 2)
    return near, lax.rem(me + 2, 4), lax.rem(near + 2, 4)


def meet(*groups):
    barrier = pltpu.get_barrier_semaphore()
    for axis, peers in groups:
        for peer in peers:
            pl.semaphore_signal(barrier, device_id={axis: peer}, device_id_type=MESH)
    pl.semaphore_wait(barrier, sum(len(peers) for _, peers in groups))


def row_mix_steps(left_ref, weight_ref, gathered, finish, left_t, to_features, scratch):
    far_keep, own_keep, out_box, in_box, sems, *more = scratch
    own = far_keep.shape[0]
    sub = own // MIX_SUBS
    me = lax.axis_index("row")
    near, far, diag = row_peers()
    started = []

    def send(source, target, kind, piece, peer):
        copy = pltpu.make_async_remote_copy(
            src_ref=source,
            dst_ref=target,
            send_sem=sems.at[0, kind, piece],
            recv_sem=sems.at[1, kind, piece],
            device_id={"row": peer},
            device_id_type=MESH,
        )
        copy.start()
        started.append(copy)
        return copy

    def product(owner, piece):
        at = pl.ds(pl.multiple_of(owner * own + piece * sub, sub), sub)
        if left_t:
            left = left_ref[:, at].astype(F32).T.astype(BF16)
        else:
            left = left_ref[at, :]
        return mm(left, weight_ref[...])

    pieces = [slice(piece * sub, (piece + 1) * sub) for piece in range(MIX_SUBS)]
    passed, direct, summed = [], [], []
    for piece, rows in enumerate(pieces):
        out_box[0, rows] = product(diag, piece).astype(BF16)
        passed.append(send(out_box.at[0, rows], in_box.at[0, rows], PASS_ON, piece, near))
        far_keep[rows] = product(far, piece)
    yield
    for piece, rows in enumerate(pieces):
        out_box[1, rows] = product(near, piece).astype(BF16)
        direct.append(send(out_box.at[1, rows], in_box.at[1, rows], TO_NEAR, piece, near))
        passed[piece].wait_recv()
        out_box[2, rows] = (far_keep[rows] + in_box[0, rows].astype(F32)).astype(BF16)
        summed.append(send(out_box.at[2, rows], in_box.at[2, rows], TO_FAR, piece, far))
    yield
    for piece, rows in enumerate(pieces):
        own_keep[rows] = product(me, piece)
    yield
    near_out, far_out, on_out = [], [], []
    for piece, rows in enumerate(pieces):
        direct[piece].wait_recv()
        summed[piece].wait_recv()
        total = own_keep[rows] + in_box[1, rows].astype(F32) + in_box[2, rows].astype(F32)
        result = finish(total, piece, rows)
        if to_features:
            boxes, arrived = more
            part = gathered.shape[0]
            for place in range(4):
                boxes[place, rows] = result[:, place * part : (place + 1) * part].astype(BF16)
            arrived[me, rows] = boxes[me, rows]
            for kind, peer, copies in (
                (OUT_NEAR, near, near_out), (OUT_FAR, far, far_out), (OUT_ON, diag, on_out)
            ):
                copies.append(send(boxes.at[peer, rows], arrived.at[me, rows], kind, piece, peer))
        else:
            gathered[me, rows] = result
            near_out.append(send(gathered.at[me, rows], gathered.at[me, rows], OUT_NEAR, piece, near))
            far_out.append(send(gathered.at[me, rows], gathered.at[me, rows], OUT_FAR, piece, far))
    yield
    for piece, rows in enumerate(pieces):
        far_out[piece].wait_recv()
        if not to_features:
            on_out.append(send(gathered.at[far, rows], gathered.at[far, rows], OUT_ON, piece, near))
    for copy in near_out + on_out:
        copy.wait_recv()
    if to_features:
        boxes, arrived = more
        for source in range(4):
            gathered[:, source * own : (source + 1) * own] = arrived[source].astype(F32).T.astype(gathered.dtype)
    for copy in started:
        copy.wait_send()


def mix_scratch(own, model, to_features):
    boxes = [pltpu.VMEM((4, own, model // 4), BF16)] * 2 if to_features else []
    return [
        pltpu.VMEM((own, model), F32),
        pltpu.VMEM((own, model), F32),
        pltpu.VMEM((3, own, model), BF16),
        pltpu.VMEM((3, own, model), BF16),
        pltpu.SemaphoreType.DMA((2, 6, MIX_SUBS)),
        *boxes,
    ]


def row_mix_kernel(finish, extra, outs, left_t, share, images, left_ref, weight_ref, *refs):
    extra_refs, refs = refs[:extra], refs[extra:]
    if images:
        refs = refs[1:]
    if share:
        share_ref, refs = refs[0], refs[1:]
    (gathered, *out_refs), scratch = refs[:outs], refs[outs:]
    if len(weight_ref.shape) == 3:
        *scratch, held, held_sem = scratch
        copy = fetch(weight_ref, 0, (held, held_sem))
        copy.start()
    near, far, _ = row_peers()
    meet(
        ("row", (near, far)),
        ("col", [col_peer(step) for step in range(1, 4)] if images else ()),
        ("batch", image_peers(2) if share or images == 2 else ()),
    )
    if images:
        *out_refs, weight_all = out_refs
        *scratch, chain_sems, pass_sems = scratch
        chains, swapped = weight_chains(weight_all, images, chain_sems, pass_sems)
        for chain in chains:
            chain.begin(3)
            if swapped:
                chain.each(2, chain.on_block)
    if share:
        *out_refs, share_out = out_refs
        *scratch, got, swap_sems = scratch
        image, half = lax.axis_index("batch"), got.shape[1]
        given = pl.ds(pl.multiple_of((1 - image) * half, 16), half)
        kept = pl.ds(pl.multiple_of(image * half, 16), half)
        swap = image_copy(share_ref.at[:, given], got, swap_sems, 0)
        swap.start()

    def last(total, piece, rows):
        return finish(total, piece, rows, *extra_refs, out_refs)

    if len(weight_ref.shape) == 3:
        copy.wait()
        weight_ref = held
    for stage, _ in enumerate(row_mix_steps(left_ref, weight_ref, gathered, last, left_t, False, scratch)):
        if images and stage == 3:
            for chain in chains:
                chain.hop(3)
    if images:
        for chain in chains:
            chain.end((3,))
            if swapped:
                chain.each(2, swapped)
                chain.each(3, swapped)
    if share:
        swap.wait()
        for place in range(4):
            both = share_ref[place, kept].astype(F32) + got[place].astype(F32)
            share_out[place] = both.astype(BF16)


def fetch(stack_ref, which, scratch):
    return pltpu.make_async_copy(stack_ref.at[which], scratch[0], scratch[1])


def fetch_scratch(stack):
    return [pltpu.VMEM(stack.shape[1:], stack.dtype), pltpu.SemaphoreType.DMA(())]


def row_mix(finish, name, number, left, weight, extra, out_shapes, left_t, share=None, passing=None):
    tokens = left.shape[1] if left_t else left.shape[0]
    model = weight.shape[-1]
    own = tokens // 4
    vmem = pl.BlockSpec(memory_space=pltpu.VMEM)
    shared = share is not None and lax.axis_size("batch") == 2
    specs, outs, scratch = [vmem] * (2 + len(extra)), [*out_shapes], mix_scratch(own, model, False)
    operands = (left, weight, *extra)
    if shared:
        cols, n, _ = share.shape
        specs.append(vmem)
        operands = (*operands, share)
        outs.append(jax.ShapeDtypeStruct((cols, n // 2, model), BF16))
        scratch += [pltpu.VMEM((cols, n // 2, model), BF16), pltpu.SemaphoreType.DMA((2, 1))]
    out_specs = [vmem] * (1 + len(outs))
    alias, images = {}, 0
    if passing is not None:
        images = lax.axis_size("batch")
        alias = {len(operands): len(out_specs)}
        operands = (*operands, passing)
        specs.append(pl.BlockSpec(memory_space=pl.ANY))
        out_specs.append(pl.BlockSpec(memory_space=pl.ANY))
        outs.append(jax.ShapeDtypeStruct(passing.shape, passing.dtype))
        scratch += [pltpu.SemaphoreType.DMA((2, 2, 2, 3)), pltpu.SemaphoreType.DMA((2, 2, 3))]
    if weight.ndim == 3:
        specs[1] = pl.BlockSpec(memory_space=pl.ANY)
        scratch += fetch_scratch(weight)
    results = pl.pallas_call(
        partial(row_mix_kernel, finish, len(extra), 1 + len(outs), left_t, shared, images),
        out_shape=[jax.ShapeDtypeStruct((4, own, model), BF16), *outs],
        in_specs=specs,
        out_specs=out_specs,
        input_output_aliases=alias,
        scratch_shapes=scratch,
        compiler_params=pltpu.CompilerParams(
            collective_id=number, has_side_effects=True, vmem_limit_bytes=48 << 20
        ),
        cost_estimate=pl.CostEstimate(
            flops=2 * tokens * model * model, bytes_accessed=16 * own * model, transcendentals=0
        ),
        name=name,
    )(*operands)
    return results if share is None or shared else (*results, share)


def weight_steps(values_ref, images, scratch, write, joined=False):
    boxes, arrived, other, sems = scratch
    me, part = lax.axis_index("row"), boxes.shape[2]
    for place in range(4):
        boxes[place] = values_ref[:, place * part : (place + 1) * part]
    arrived[me] = boxes[me]
    copies = []
    for order, peer in enumerate(row_peers()):
        copy = pltpu.make_async_remote_copy(
            src_ref=boxes.at[peer],
            dst_ref=arrived.at[me],
            send_sem=sems.at[0, order],
            recv_sem=sems.at[1, order],
            device_id={"row": peer},
            device_id_type=MESH,
        )
        copy.start()
        copies.append(copy)
    yield
    for copy in copies:
        copy.wait()
    if images == 2:
        swap = pltpu.make_async_remote_copy(
            src_ref=arrived,
            dst_ref=other,
            send_sem=sems.at[0, 3],
            recv_sem=sems.at[1, 3],
            device_id={"batch": 1 - lax.axis_index("batch")},
            device_id_type=MESH,
        )
        swap.start()
        yield
        swap.wait()
        for place in range(4):
            if joined:
                write(place, arrived[place].astype(F32), other[place].astype(F32))
            else:
                write(place, arrived[place].astype(F32) + other[place].astype(F32))
    else:
        yield
        for place in range(4):
            write(place, arrived[place].astype(F32))


def weight_scratch(n, part):
    return [*[pltpu.VMEM((4, n, part), BF16)] * 3, pltpu.SemaphoreType.DMA((2, 4))]


def image_peers(images):
    me = lax.axis_index("batch")
    return [lax.rem(me + step, images) for step in range(1, images)]


def sum_steps(total, axes, scratch):
    *slots, sends, recvs = scratch
    for order, (name, size) in enumerate(axes):
        me, slot = lax.axis_index(name), slots[order]
        slot[me] = total[...]
        copies = []
        for step in range(1, size):
            copy = pltpu.make_async_remote_copy(
                src_ref=total,
                dst_ref=slot.at[me],
                send_sem=sends.at[order, step],
                recv_sem=recvs.at[order, step],
                device_id={name: lax.rem(me + step, size)},
                device_id_type=MESH,
            )
            copy.start()
            copies.append(copy)
        yield
        for copy in copies:
            copy.wait()
        whole = slot[0]
        for source in range(1, size):
            whole = whole + slot[source]
        total[...] = whole


def sum_scratch(rows, axes):
    most = max(size for _, size in axes)
    return [
        *[pltpu.VMEM((size, rows, 128), F32) for _, size in axes],
        *[pltpu.SemaphoreType.DMA((len(axes), most))] * 2,
    ]


def column_steps(images, grad_ref, normed_ref, out, scratch):
    keep, give, got, box, arrived, sems, swap_sems = scratch
    image, rows = lax.axis_index("batch"), out.shape[0]
    shared = images == 2
    swaps = {}
    for step in (1, 2, 3, 0):
        keep[step] = mm(grad_ref[col_peer(step)], normed_ref[...])
        if shared:
            give[step] = keep[step, pl.ds(half_start(1 - image), rows)].astype(BF16)
            swaps[step] = image_copy(give.at[step], got.at[step], swap_sems, step)
            swaps[step].start()
    yield

    def total(step):
        if not shared:
            return keep[step]
        swaps[step].wait()
        return keep[step, pl.ds(half_start(image), rows)] + got[step].astype(F32)

    copies = []
    for step in range(1, 4):
        box[step - 1] = total(step).astype(BF16)
        copy = col_copy(box.at[step - 1], arrived.at[step - 1], sems, 0, step)
        copy.start()
        copies.append(copy)
    yield
    whole = total(0)
    for step, copy in enumerate(copies):
        copy.wait()
        whole = whole + arrived[step].astype(F32)
    out[...] = whole.astype(BF16)


def column_scratch(n, rows, model):
    return [
        pltpu.VMEM((4, n, model), F32),
        *[pltpu.VMEM((4, rows, model), BF16)] * 2,
        *[pltpu.VMEM((3, rows, model), BF16)] * 2,
        pltpu.SemaphoreType.DMA((2, 1, 4)),
        pltpu.SemaphoreType.DMA((2, 4)),
    ]


EARLY_ROWS, TABLE_ROWS, BIAS_ROWS, LAST_ROWS = 80, 160, 32, 24


def tail_kernel(
    axes,
    qkv_grad_ref, grads_ref, weight_qkv_ref, normed1_ref, first_ref, middle_grad_ref, gain_ref,
    fc1_ref, proj_ref, early_ref, table_ref, bias_ref, patches_out, qkv_out, fc1_out, proj_out, tables_out, small, *rest,
):
    vector_outs, (sums1, qkv_rows, *scratch) = rest[:6], rest[6:]
    col_scratch, scratch = scratch[:7], scratch[7:]
    mix, qkv_scratch, fc1_scratch, sum_parts = scratch[:7], scratch[7:11], scratch[11:15], scratch[15:20]
    proj_rows, proj_box, proj_sems, fc1_rows, *proj_scratch = scratch[20:]
    row, col = lax.axis_index("row"), lax.axis_index("col")
    images = dict(axes)["batch"]
    meet(
        ("row", row_peers()),
        ("col", [col_peer(step) for step in range(1, 4)]),
        ("batch", image_peers(images)),
    )

    def finish1(total, piece, rows):
        return last_finish(total, piece, rows, gain_ref, first_ref, middle_grad_ref, (None, sums1))

    image = lax.axis_index("batch")
    shared = images == 2

    def write_fc1(place, values, others=None):
        n = values.shape[0]
        if others is None:
            fc1_rows[place * n : (place + 1) * n] = values
        else:
            fc1_rows[pl.ds(pl.multiple_of((2 * place + image) * n, 8), n)] = values
            fc1_rows[pl.ds(pl.multiple_of((2 * place + 1 - image) * n, 8), n)] = others

    def write_proj(place, values):
        proj_out[place] = values

    def proj_steps():
        copies = []
        for step in range(1, 4):
            copies.append(col_copy(proj_ref.at[col_peer(step)], proj_box.at[col], proj_sems, 0, step))
            copies[-1].start()
        proj_box[col] = proj_ref[col]
        yield
        for copy in copies:
            copy.wait()
        total = proj_box[0].astype(F32)
        for source in range(1, 4):
            total = total + proj_box[source].astype(F32)
        proj_rows[...] = total.astype(BF16)
        yield from weight_steps(proj_rows, images, proj_scratch, write_proj)

    head_grads = []

    def write_qkv(place, values, others=None):
        if others is not None:
            first, second = jnp.where(image == 0, values, others), jnp.where(image == 0, others, values)
            values = jnp.concatenate([first[: 3 * HEAD_DIM - HALF_GRAD], second], 0)
        head_grads.append(values)

    qkv_sum = column_steps(images, grads_ref, normed1_ref, qkv_rows, col_scratch)
    patches = row_mix_steps(qkv_grad_ref, weight_qkv_ref, patches_out, finish1, True, True, mix)
    fc1 = weight_steps(fc1_ref, images, fc1_scratch, write_fc1, shared)
    qkv = weight_steps(qkv_rows, images, qkv_scratch, write_qkv, shared)
    sums = sum_steps(small, axes, sum_parts)

    def go(*steps):
        for step in steps:
            next(step, None)

    proj = proj_steps()
    go(proj, qkv_sum, patches, patches, patches, proj, qkv_sum, patches)

    small[0:EARLY_ROWS] = early_ref[...]
    at = EARLY_ROWS
    for half in range(2):
        small[at : at + TABLE_ROWS // 2] = table_ref[:, half * 128 : (half + 1) * 128]
        at += TABLE_ROWS // 2
    place = lax.broadcasted_iota(jnp.int32, (BIAS_ROWS, 128), 0) - 2 * (col * 4 + row)
    small[at : at + BIAS_ROWS] = jnp.where(
        place == 0, bias_ref[0:1], jnp.where(place == 1, bias_ref[1:2], 0.0)
    )
    at += BIAS_ROWS
    lines = sums1.shape[1] // 128
    last = [sums1[i : i + 1, j * 128 : (j + 1) * 128] for i in range(2) for j in range(lines)]
    spare = jnp.zeros((LAST_ROWS - len(last), 128), F32)
    small[at : at + LAST_ROWS] = jnp.concatenate([*last, spare], 0)

    go(sums, fc1, proj, sums, fc1, proj, qkv_sum, qkv, sums, patches, qkv, fc1, proj, sums)
    firsts = [lines * i for i in (5, 6, 7, 4)] + [EARLY_ROWS + TABLE_ROWS + BIAS_ROWS + lines * i for i in range(2)]
    part = vector_outs[0].shape[0]
    for first, out in zip(firsts, vector_outs):
        whole = jnp.concatenate([small[first + i : first + i + 1] for i in range(lines)], 1)
        mine = whole[:, :part]
        for place in range(1, 4):
            mine = jnp.where(row == place, whole[:, place * part : (place + 1) * part], mine)
        out[...] = mine.reshape(part)
    fc1_out[...] = fc1_rows[...].T
    flip = backwards(2 * GRID, 2 * GRID - 1)
    for half in range(2):
        table = small[EARLY_ROWS + half * HEAD_DIM : EARLY_ROWS + (half + 1) * HEAD_DIM]
        tables_out[half] = sum(mm(term, flip) for term in split(table, 3))
    go(qkv)
    for kind in range(3):
        rows = slice(kind * HEAD_DIM, (kind + 1) * HEAD_DIM)
        qkv_out[kind] = jnp.concatenate([values[rows] for values in head_grads], 0).T


def tail(
    qkv_grad, weight_qkv, normed1, first, middle_grad, gain, fc1, proj, early, table, bias
):
    cols, n, tokens = qkv_grad.shape
    model = weight_qkv.shape[1]
    own, part = tokens // 4, model // 4
    shared = lax.axis_size("batch") == 2
    rows = HALF_GRAD if shared else n
    units = fc1.shape[0] * (2 if shared else 1)
    axes = tuple((name, lax.axis_size(name)) for name in ("row", "batch", "col"))
    small_rows = EARLY_ROWS + TABLE_ROWS + BIAS_ROWS + LAST_ROWS
    vmem = pl.BlockSpec(memory_space=pltpu.VMEM)
    return pl.pallas_call(
        partial(tail_kernel, axes),
        in_specs=[vmem] * 12,
        out_specs=[vmem] * 12,
        out_shape=[
            jax.ShapeDtypeStruct((part, tokens), F32),
            jax.ShapeDtypeStruct((3, part, 4 * HEAD_DIM), F32),
            jax.ShapeDtypeStruct((part, 4 * units), F32),
            jax.ShapeDtypeStruct((4, proj.shape[1], part), F32),
            jax.ShapeDtypeStruct((2, HEAD_DIM, 2 * GRID - 1), F32),
            jax.ShapeDtypeStruct((small_rows, 128), F32),
            *[jax.ShapeDtypeStruct((part,), F32)] * 6,
        ],
        scratch_shapes=[
            pltpu.VMEM((3, model), F32),
            pltpu.VMEM((rows, model), BF16),
            *column_scratch(n, rows, model),
            *mix_scratch(own, model, True),
            *weight_scratch(rows, part),
            *weight_scratch(fc1.shape[0], part),
            *sum_scratch(small_rows, axes),
            pltpu.VMEM(proj.shape[1:], BF16),
            pltpu.VMEM(proj.shape, BF16),
            pltpu.SemaphoreType.DMA((2, 1, 4)),
            pltpu.VMEM((4 * units, part), F32),
            *weight_scratch(proj.shape[1], part),
        ],
        compiler_params=pltpu.CompilerParams(
            collective_id=3, has_side_effects=True, vmem_limit_bytes=60 << 20
        ),
        name="tail",
    )(
        qkv_grad.reshape(cols * n, tokens), qkv_grad, weight_qkv, normed1, first, middle_grad, gain,
        fc1, proj, early, table, bias,
    )


HIDDEN = 256
ROWS = 256


def hidden_kernel(x_ref, w1_ref, bias_ref, cot_ref, w2_ref, act_ref, grad_ref, bias_grad_ref):
    total = None
    for start in range(0, x_ref.shape[0], ROWS):
        rows = slice(start, start + ROWS)
        preact = mm_nt(x_ref[rows], w1_ref[...]) + bias_ref[...]
        act_grad = mm_nt(cot_ref[rows], w2_ref[...])
        below = 0.5 + 0.5 * lax.erf(preact * (0.5**0.5))
        density = jnp.exp(preact * preact * -0.5) * ((2 * math.pi) ** -0.5)
        act_ref[rows] = (preact * below).astype(BF16)
        grad = (act_grad * (below + preact * density)).astype(BF16)
        grad_ref[rows] = grad
        part = jnp.sum(grad.astype(F32), 0, keepdims=True)
        total = part if total is None else total + part
    bias_grad_ref[...] = total


def feed_forward(x, weights, bias, cotangent):
    tokens, model = x.shape
    hidden = weights.shape[1]
    step = HIDDEN if hidden % HIDDEN == 0 else hidden
    whole = pl.BlockSpec((tokens, model), lambda i: (0, 0), pipeline_mode=pl.Buffered(1))
    first, second = [pl.BlockSpec((None, step, model), lambda i, j=j: (j, i, 0)) for j in range(2)]
    vector = pl.BlockSpec((1, step), lambda i: (0, i))
    columns = pl.BlockSpec((tokens, step), lambda i: (0, i))
    return pl.pallas_call(
        hidden_kernel,
        grid=(hidden // step,),
        in_specs=[whole, first, vector, whole, second],
        out_specs=[columns, columns, vector],
        out_shape=[
            jax.ShapeDtypeStruct((tokens, hidden), BF16),
            jax.ShapeDtypeStruct((tokens, hidden), BF16),
            jax.ShapeDtypeStruct((1, hidden), F32),
        ],
        compiler_params=pltpu.CompilerParams(vmem_limit_bytes=40 << 20),
        cost_estimate=pl.CostEstimate(
            flops=4 * tokens * hidden * model,
            bytes_accessed=4 * (tokens + hidden) * model + 4 * tokens * hidden,
            transcendentals=2 * tokens * hidden,
        ),
        name="feed_forward",
    )(x, weights, bias, cotangent, weights)


def table_scratch():
    return [pltpu.VMEM((HEAD_DIM, 4 * GRID), BF16), pltpu.VMEM((4 * GRID, HEAD_DIM), BF16)]


def attention(qkv, height, span, cotangent, weights):
    count, _, width = qkv.shape
    tokens = count * width
    images = lax.axis_size("batch")
    vmem = pl.BlockSpec(memory_space=pltpu.VMEM)
    return pl.pallas_call(
        partial(attend_kernel, images),
        in_specs=[*[vmem] * 4, pl.BlockSpec(memory_space=pl.ANY)],
        out_specs=[*[vmem] * 6, pl.BlockSpec(memory_space=pl.ANY)],
        out_shape=[
            jax.ShapeDtypeStruct((count, HEAD_DIM, width), BF16),
            jax.ShapeDtypeStruct(qkv.shape, BF16),
            jax.ShapeDtypeStruct((count, HEAD_DIM, width), F32),
            jax.ShapeDtypeStruct((count, 8, width), F32),
            jax.ShapeDtypeStruct((width, 4 * cotangent.shape[0]), BF16),
            jax.ShapeDtypeStruct((width // 4, 4 * cotangent.shape[0]), BF16),
            jax.ShapeDtypeStruct((2, count, *weights.shape[1:]), BF16),
        ],
        scratch_shapes=[
            pltpu.VMEM((count, width, 256), BF16),
            pltpu.VMEM((count, 256, width), BF16),
            pltpu.VMEM((count, HEAD_DIM, width), F32),
            pltpu.VMEM((count, 8, width), F32),
            pltpu.VMEM((count, 8, width), F32),
            pltpu.VMEM((count, HEAD_DIM, width), BF16),
            pltpu.SemaphoreType.DMA((2, 3, 4)),
            pltpu.VMEM((4, *cotangent.shape), BF16),
            pltpu.SemaphoreType.DMA((2, 1, 3)),
            pltpu.SemaphoreType.DMA((2,)),
            pltpu.SemaphoreType.DMA((2, 2, 2, 3)),
            pltpu.SemaphoreType.DMA((2, 2, 3)),
            *table_scratch(),
        ],
        compiler_params=pltpu.CompilerParams(
            collective_id=5, has_side_effects=True, vmem_limit_bytes=48 << 20
        ),
        cost_estimate=pl.CostEstimate(
            flops=2 * tokens * tokens * 512,
            bytes_accessed=6 * tokens * HEAD_DIM * 2,
            transcendentals=tokens * tokens,
        ),
        name="attend",
    )(qkv, height, span, cotangent, weights)


def attention_back(qkv, height, span, grad, exact, stat, fc2, activated, weights, middle, bias_fc2):
    count, _, width = qkv.shape
    tokens = count * width
    images, part = lax.axis_size("batch"), fc2.shape[1] // 4
    vmem = pl.BlockSpec(memory_space=pltpu.VMEM)
    return pl.pallas_call(
        partial(attend_back_kernel, images),
        in_specs=[*[vmem] * 8, pl.BlockSpec(memory_space=pl.ANY), vmem, vmem],
        out_specs=[vmem] * 5,
        out_shape=[
            jax.ShapeDtypeStruct((count, 3 * HEAD_DIM, width), BF16),
            jax.ShapeDtypeStruct((HEAD_DIM, 4 * GRID), F32),
            jax.ShapeDtypeStruct((2, 128), F32),
            jax.ShapeDtypeStruct((part, 4 * fc2.shape[0]), F32),
            jax.ShapeDtypeStruct((part, width), BF16),
        ],
        scratch_shapes=[
            *table_scratch(),
            *fetch_scratch(weights),
            pltpu.VMEM((384, 128), F32),
            pltpu.VMEM((count, HEAD_DIM, width), BF16),
            pltpu.VMEM((count, width, 256), BF16),
            pltpu.VMEM((count, 256, width), BF16),
            pltpu.VMEM((count, width, 128), BF16),
            pltpu.VMEM((count, width, 128), F32),
            pltpu.VMEM((count, width, 128), F32),
            pltpu.VMEM((count, 256, width), F32),
            pltpu.VMEM((count, 256, width), BF16),
            pltpu.VMEM((count, 128, width), BF16),
            pltpu.VMEM((count, width, 128), BF16),
            pltpu.VMEM((count, width, 128), BF16),
            pltpu.VMEM((count, 3 * HEAD_DIM, width), BF16),
            pltpu.SemaphoreType.DMA((2, 3, 4)),
            *weight_scratch(fc2.shape[0], part),
            *mix_scratch(*middle.shape, True),
        ],
        compiler_params=pltpu.CompilerParams(
            collective_id=4, has_side_effects=True, vmem_limit_bytes=62 << 20
        ),
        cost_estimate=pl.CostEstimate(
            flops=2 * tokens * tokens * 1280,
            bytes_accessed=12 * tokens * HEAD_DIM * 2,
            transcendentals=tokens * tokens,
        ),
        name="attend_back",
    )(qkv, height, span, grad, exact, stat, fc2, activated, weights, middle, bias_fc2)


def moments(values):
    center = jnp.mean(values, -1, keepdims=True)
    spread = jnp.mean(values * values, -1, keepdims=True)
    return center, lax.rsqrt(spread - center * center + EPSILON)


def shards(
    patches,
    qkv_weight,
    qv_bias,
    proj_weight,
    proj_bias,
    norm1_gain,
    norm1_shift,
    norm2_gain,
    norm2_shift,
    fc1_weight,
    fc1_bias,
    fc2_weight,
    fc2_bias,
    height_table,
    width_table,
    out_grad,
):
    rows, cols = lax.axis_size("row"), lax.axis_size("col")
    row, col = lax.axis_index("row"), lax.axis_index("col")
    width = patches.shape[1]
    part = patches.shape[2]
    model = part * rows
    own = width // rows
    hidden = fc1_bias.shape[0] // rows
    head = HEAD_DIM

    images = lax.axis_size("batch")

    local_qkv = qkv_weight.reshape(part, 3, rows, head).transpose(2, 1, 3, 0).reshape(rows, 3 * head, part)
    qkv, normed1, first_own, weight_qkv, weight_proj, local_rest, vectors, columns = start(
        patches[0].T,
        local_qkv,
        proj_weight.reshape(rows, head, part),
        fc1_weight,
        fc2_weight.T,
        qv_bias,
        fc1_bias,
        norm1_gain,
        norm1_shift,
        norm2_gain,
        norm2_shift,
        proj_bias,
        fc2_bias,
    )
    gain1, shift1, gain2, shift2, bias_proj, bias_fc2 = [vectors[i] for i in range(6)]
    weight_qkv = weight_qkv.reshape(cols * 3 * head, model)
    bias_fc1 = columns[:, 0, 256:].reshape(cols * hidden)

    height, span = height_table.T, width_table.T

    merged, qkv, exact, stat, cotangent, cotangent_own, weights = attention(
        qkv, height, span, out_grad[0].T, local_rest.reshape(2, hidden, model)
    )
    weight_proj = weight_proj.reshape(cols * head, model)
    merged = merged.reshape(cols * head, width)

    def contract_rows(left, right):
        return lax.dot_general(left, right, (((0,), (0,)), ((), ())), preferred_element_type=F32)

    def sum_columns(values):
        return lax.psum_scatter(values, "col", scatter_dimension=0, tiled=False)

    def tokens_of_row(values):
        return lax.dynamic_slice_in_dim(values, row * own, own, 0)

    own_shape = (own, model)
    vec2 = jnp.stack([gain2, shift2, bias_proj])
    normed2, middle, weights = row_mix(
        forward_finish, "middle_and_norm2", 1, merged, weight_proj,
        (vec2, first_own), [jax.ShapeDtypeStruct(own_shape, F32)], True, None, weights,
    )
    normed2 = normed2.reshape(width, model)
    weights = weights.reshape(2, cols * hidden, model)
    activated, preact_grad, fc1_bias_part = feed_forward(normed2, weights, bias_fc1[None], cotangent)
    fc2_grad = contract_rows(activated, cotangent).astype(BF16)
    fc2_grad, preact_grad = lax.optimization_barrier((fc2_grad, preact_grad))
    fc1_grad = contract_rows(preact_grad, normed2).astype(BF16).reshape(cols, hidden, model)

    own_and_sums = [jax.ShapeDtypeStruct(own_shape, F32), jax.ShapeDtypeStruct((3, model), F32)]
    branch_grad, middle_grad, sums2, fc1_grad = row_mix(
        backward_finish, "middle_grad", 2, preact_grad, weights,
        (vec2, middle, cotangent_own), own_and_sums, False, fc1_grad,
    )
    branch_grad = branch_grad.reshape(width, model)

    merged_grad = mm_nt(weight_proj, branch_grad).astype(BF16).reshape(cols, head, width)
    proj_grad = mm(merged, branch_grad).astype(BF16)
    fc2_grad = sum_columns(fc2_grad.reshape(cols, hidden, model))
    early = jnp.concatenate(
        [
            lax.dynamic_update_slice(jnp.zeros((rows, cols * hidden), F32), fc1_bias_part, (row, 0)).reshape(-1),
            lax.dynamic_update_slice(
                jnp.zeros((model,), F32), jnp.sum(out_grad[0], 0, dtype=F32), (row * part,)
            ),
            sums2.reshape(-1),
        ]
    ).reshape(-1, 128)
    merged_grad, fc1_grad, proj_grad, fc2_grad, early = lax.optimization_barrier(
        (merged_grad, fc1_grad, proj_grad, fc2_grad, early)
    )
    fc1_grad = sum_columns(fc1_grad)
    qkv_grad, table_grad, bias_grad, fc2_grad, final = attention_back(
        qkv, height, span, merged_grad, exact, stat, fc2_grad, activated, weights, middle, bias_fc2[None]
    )
    input_grad, qkv_weight_grad, fc1_grad, proj_grad, tables, small, *vector_grads = tail(
        qkv_grad, weight_qkv, normed1, first_own, middle_grad, gain1[None],
        fc1_grad, proj_grad.reshape(cols, head, model), early, table_grad, bias_grad,
    )

    def sum_images(values):
        return values if images == 2 else lax.psum(values.astype(BF16), "batch").astype(F32)

    fc2_grad = sum_images(fc2_grad).T
    proj_grad = sum_images(proj_grad).reshape(rows * head, part)
    fc1_grad = sum_images(fc1_grad)
    qkv_weight_grad = sum_images(qkv_weight_grad).transpose(1, 0, 2)

    lines = model // 128
    fc1_bias_grad = small[: 4 * lines].reshape(rows, cols, hidden)
    fc1_bias_grad = lax.dynamic_index_in_dim(fc1_bias_grad, col, 1, keepdims=False).reshape(rows * hidden)
    gain2_grad, shift2_grad, proj_bias_grad, fc2_bias_grad, gain1_grad, shift1_grad = vector_grads
    at = EARLY_ROWS
    at += TABLE_ROWS
    bias_total = small[at : at + BIAS_ROWS].reshape(cols, rows, 2, 128)
    bias_total = lax.dynamic_index_in_dim(bias_total, col, 0, keepdims=False)[:, :, :head]
    bias_total = bias_total.transpose(1, 0, 2).reshape(2, rows * head)

    return (
        final.T[None],
        input_grad.T[None],
        qkv_weight_grad,
        bias_total,
        proj_grad,
        proj_bias_grad,
        gain1_grad,
        shift1_grad,
        gain2_grad,
        shift2_grad,
        fc1_grad,
        fc1_bias_grad,
        fc2_grad,
        fc2_bias_grad,
        tables[0].T,
        tables[1].T,
    )


def solution(mesh):
    in_specs = (
        P("batch", "col", "row"),
        P("row", None, "col"),
        P(None, "col"),
        P("col", "row"),
        P("row"),
        P("row"),
        P("row"),
        P("row"),
        P("row"),
        P("row", "col"),
        P("col"),
        P("col", "row"),
        P("row"),
        P(),
        P(),
        P("batch", "col", "row"),
    )
    out_specs = (
        P("batch", "col", "row"),
        P("batch", "col", "row"),
        P("row", None, "col"),
        P(None, "col"),
        P("col", "row"),
        P("row"),
        P("row"),
        P("row"),
        P("row"),
        P("row"),
        P("row", "col"),
        P("col"),
        P("col", "row"),
        P("row"),
        P(),
        P(),
    )
    return jax.shard_map(shards, mesh=mesh, in_specs=in_specs, out_specs=out_specs, check_vma=False)
```
